32 devices in a mesh: lat: 4 (over y, core), blk: 4 (over z), probe: 2 (over x).
Axes of the slice: x: 2, y: 2, z: 4, core: 2. Of those that a mesh axis runs over, the one named last changes fastest.
Arguments:
- probes_in: bfloat16 [64, 2, 640, 640], P('probe', None, ('lat', 'blk')), may hold values from -1.5 to 1.5
- root_spectrum: float32 [640], replicated, may hold values from 0.2 to 3, as said below
- order_slots: int32 [640], replicated, may hold values from 0 to 639, as said below
- legendre: bfloat16 [640, 640, 1280], P(None, ('lat', 'blk')), as said below
- weight: float32 [1280, 2560], P(('lat', 'blk')), may hold values from 0.2 to 5
- beta: float32 [64], P('probe'), may hold values from 0.5 to 2
Outputs:
- matvec: float32 [64, 2, 640, 640], P('probe', None, ('lat', 'blk'))
- gradient: float32 [1280, 2560], P(('lat', 'blk'), 'probe')
The draws below stay inside these ranges and needn't reach their ends.
Inputs may be any that keep to these rules, and one draw needn't show every extreme that they name: order_slots is a permutation of 0 to 639, and slots 2k and 2k + 1 hold orders that sum to 639. legendre[l, s, j] is the orthonormal associated Legendre function (no Condon-Shortley sign) of degree l and order order_slots[s] at cos(theta_j), zero for l below the order, rounded to bfloat16. root_spectrum is drawn afresh for each degree.
All inputs are finite; a program needn't handle non-finite values.
Results may differ from the reference program's by a relative error of at most 0.0031.
Values may be sent and summed in bfloat16 or wider, within the bound.
No kernel may reach another device: no remote copies, remote signals or barrier semaphores. Data moves between devices by JAX's collectives and lax.ppermute only.
A program may use at most 320 MiB of HBM per device.

```python
import math
import jax
import jax.numpy as jnp
from jax import lax

DEGREES = 640
NLAT = 1280
NLON = 2560
PROBES = 64
ORDERS = 640


def slot_orders(key):
    pair_order = jax.random.permutation(jax.random.fold_in(key, 17), ORDERS // 2).astype(jnp.int32)
    partner = (ORDERS - 1 - pair_order).astype(jnp.int32)
    return jnp.stack([pair_order, partner], axis=1).reshape(ORDERS).astype(jnp.int32)


def draw_order_slots(key, part):
    return slot_orders(key)


def draw_root_spectrum(key, part):
    band_width = max(DEGREES // 20, 4)
    degree = jnp.arange(DEGREES, dtype=jnp.int32)
    upper_band = degree >= DEGREES - band_width
    fraction = jax.random.uniform(jax.random.fold_in(key, 29), (DEGREES,), jnp.float32)
    high_values = 2.4 * jnp.exp(math.log(1.25) * fraction)
    low_values = 0.2 * jnp.exp(math.log(2.0) * fraction)
    return jnp.where(upper_band, high_values, low_values).astype(jnp.float32)


def draw_legendre(key, part):
    orders = slot_orders(key)
    cycle_index = jnp.arange(NLAT, dtype=jnp.int32).astype(jnp.float32)
    colat = math.pi * (cycle_index + 0.5) / NLAT
    cosines = jnp.cos(colat)
    sines = jnp.sin(colat)
    order_f = orders.astype(jnp.float32)[:, None]
    log_start = order_f * jnp.log(sines)[None, :] + 0.5 * (jnp.log((2.0 * order_f + 1.0) / (4.0 * math.pi)) + jax.scipy.special.gammaln(order_f + 0.5) - jax.scipy.special.gammaln(jnp.float32(0.5)) - jax.scipy.special.gammaln(order_f + 1.0))

    def advance(state, degree):
        prev_one, prev_two, exponent = state
        degree_f = degree.astype(jnp.float32)
        denom_a = jnp.maximum(degree_f * degree_f - order_f * order_f, 1.0)
        coef_a = jnp.sqrt(jnp.maximum(4.0 * degree_f * degree_f - 1.0, 1.0) / denom_a)
        before = degree_f - 1.0
        coef_b = jnp.sqrt(jnp.maximum(before * before - order_f * order_f, 0.0) / jnp.maximum(4.0 * before * before - 1.0, 1.0))
        recurred = coef_a * (cosines[None, :] * prev_one - coef_b * prev_two)
        at_start = orders[:, None] == degree
        past_start = degree > orders[:, None]
        current = jnp.where(at_start, 1.0, jnp.where(past_start, recurred, 0.0))
        exponent = jnp.where(at_start, log_start, exponent)
        rescale = jnp.maximum(jnp.maximum(jnp.abs(current), jnp.abs(prev_one)), 1e-30)
        rescale = jnp.where(degree >= orders[:, None], rescale, 1.0)
        current = current / rescale
        shifted = prev_one / rescale
        exponent = exponent + jnp.log(rescale)
        emitted = (current * jnp.exp(exponent)).astype(jnp.bfloat16)
        return ((current, shifted, exponent), emitted)
    zeros_f = jnp.zeros((ORDERS, NLAT), jnp.float32)
    _, table = lax.scan(advance, (zeros_f, zeros_f, zeros_f), jnp.arange(DEGREES, dtype=jnp.int32))
    return table


def shard_levels(rng, extent, cuts, low, high):
    def one(dim, blocks):
        draws = jax.random.uniform(jax.random.fold_in(jax.random.fold_in(rng, 6), dim), (blocks,), jnp.float32, low / len(cuts), high / len(cuts))
        return jnp.repeat(jnp.exp(draws), extent[dim] // blocks).reshape((-1,) + (1,) * (len(extent) - dim - 1))

    gain = one(*cuts[0])
    for cut in cuts[1:]:
        gain = gain * one(*cut)
    return gain


def centred(rng, shape, scale, reach, shards=(), held_as=jnp.bfloat16):
    gain = shard_levels(rng, shape, shards, -0.22, 0.18) if shards else 1.0
    values = jax.random.normal(rng, shape, jnp.float32) * scale * gain
    return jnp.minimum(jnp.maximum(values, -reach), reach).astype(held_as)


def setup_inputs(seed: int = 0) -> dict:
    seeds = jax.random.split(jax.random.key(seed), 7)
    probes_in = centred(seeds[0], (PROBES, 2, ORDERS, DEGREES), 0.25, 1.5, ((0, 2), (2, 16)))
    root_spectrum = draw_root_spectrum(jax.random.fold_in(seeds[6], 71), 0)
    order_slots = draw_order_slots(jax.random.fold_in(seeds[6], 71), 0)
    legendre = draw_legendre(jax.random.fold_in(seeds[6], 71), 0)
    weight = jnp.clip(jnp.exp(math.log(5.0) - 3.218876 * jax.random.uniform(seeds[4], (NLAT, NLON), jnp.float32) ** shard_levels(seeds[4], (NLAT, NLON), ((0, 16),), -0.2, 0.2)), 0.2, 5.0)
    beta = jnp.clip(0.5 + 1.5 * jax.random.uniform(seeds[5], (PROBES,), jnp.float32) ** shard_levels(seeds[5], (PROBES,), ((0, 2),), -0.2, 0.2), 0.5, 2.0)
    return {"probes_in": probes_in, "root_spectrum": root_spectrum, "order_slots": order_slots, "legendre": legendre, "weight": weight, "beta": beta}


def reference(probes_in, root_spectrum, order_slots, legendre, weight, beta):
    block_size = math.gcd(ORDERS, 64)
    block_count = ORDERS // block_size
    cycle_index = jnp.arange(NLAT, dtype=jnp.int32).astype(jnp.float32)
    sines = jnp.sin(math.pi * (cycle_index + 0.5) / NLAT)
    area = (2.0 * math.pi / NLON) * (math.pi / NLAT) * sines
    scaled = (probes_in.astype(jnp.float32) * root_spectrum).astype(jnp.bfloat16)

    def synth(block_index):
        start = (block_index * block_size).astype(jnp.int32)
        table = lax.dynamic_slice_in_dim(legendre, start, block_size, 1)
        sliced = lax.dynamic_slice_in_dim(scaled, start, block_size, 2)
        return jnp.einsum("pcml,lmj->pcmj", sliced.astype(jnp.float32),
                          table.astype(jnp.float32)).astype(jnp.bfloat16)

    pieces = lax.map(synth, jnp.arange(block_count, dtype=jnp.int32))
    spectra = jnp.moveaxis(pieces, 0, 2).reshape(PROBES, 2, ORDERS, NLAT)
    freq_scale = jnp.where(order_slots == 0, 2.0, 1.0).astype(jnp.float32) * (NLON / 2.0)

    def per_probe(grad_sum, inputs):
        coeffs, probe_beta = inputs
        real_part = jnp.zeros((NLAT, NLON // 2 + 1), jnp.float32).at[:, order_slots].set(
            coeffs[0].astype(jnp.float32).T * freq_scale)
        imag_part = jnp.zeros((NLAT, NLON // 2 + 1), jnp.float32).at[:, order_slots].set(
            -coeffs[1].astype(jnp.float32).T * freq_scale)
        grid_field = jnp.fft.irfft(lax.complex(real_part, imag_part), n=NLON, axis=1)
        grad_sum = grad_sum + probe_beta * area[:, None] * grid_field * grid_field
        weighted = (area[:, None] * weight * grid_field).astype(jnp.bfloat16)
        freq = jnp.fft.rfft(weighted.astype(jnp.float32), axis=1)
        chosen = freq[:, order_slots]
        analysed = jnp.stack([jnp.real(chosen), -jnp.imag(chosen)]).transpose(0, 2, 1)
        return grad_sum, analysed.astype(jnp.bfloat16)

    gradient, analysed = lax.scan(per_probe, jnp.zeros((NLAT, NLON), jnp.float32), (spectra, beta))

    def analyse(block_index):
        start = (block_index * block_size).astype(jnp.int32)
        table = lax.dynamic_slice_in_dim(legendre, start, block_size, 1)
        sliced = lax.dynamic_slice_in_dim(analysed, start, block_size, 2)
        result = jnp.einsum("pcmj,lmj->pcml", sliced.astype(jnp.float32),
                            table.astype(jnp.float32))
        return result * root_spectrum

    outputs = lax.map(analyse, jnp.arange(block_count, dtype=jnp.int32))
    matvec = jnp.moveaxis(outputs, 0, 2).reshape(PROBES, 2, ORDERS, DEGREES)
    return matvec, gradient
```

```python
import functools
import math

import jax
import jax.numpy as jnp
from jax import lax
from jax.experimental import pallas as pl
from jax.experimental.pallas import tpu as pltpu
from jax.sharding import PartitionSpec as P

GROUP = 8
DEPTH = 128
WIDTH = 32 * GROUP
CHUNK = 8
TILE = 256
VMEM_LIMIT = 60 * 2**20


def fourier_tables(orders, lon_count):
    longitude = jnp.arange(lon_count, dtype=jnp.int32)
    phase_idx = orders[:, None] * longitude[None, :] % lon_count
    angle = phase_idx.astype(jnp.float32) * (2.0 * math.pi / lon_count)
    twiddle = jnp.stack([jnp.cos(angle), jnp.sin(angle)])
    upper = twiddle.astype(jnp.bfloat16)
    lower = (twiddle - upper.astype(jnp.float32)).astype(jnp.bfloat16)
    return (upper, lower)


def cycle_work(spectra, inverse_tables, forward_tables, area, weight):
    grid_field = jnp.einsum(
        "pcmj,cmx->pjx", spectra, inverse_tables[0], preferred_element_type=jnp.float32
    )
    grid_field = grid_field + jnp.einsum(
        "pcmj,cmx->pjx", spectra, inverse_tables[1], preferred_element_type=jnp.float32
    )
    squares = grid_field * grid_field
    weighted = (area[None, :, None] * weight[None] * grid_field).astype(jnp.bfloat16)
    analysed = jnp.einsum(
        "pjx,cmx->pcmj", weighted, forward_tables[0], preferred_element_type=jnp.float32
    )
    analysed = analysed + jnp.einsum(
        "pjx,cmx->pcmj", weighted, forward_tables[1], preferred_element_type=jnp.float32
    )
    return (squares, analysed.astype(jnp.bfloat16))


def plain_body(probes_in, root_spectrum, order_slots, legendre, weight, beta):
    groups = lax.axis_size(("lat", "blk"))
    my_index = lax.axis_index(("lat", "blk"))
    cycle_count = weight.shape[0]
    lon_count = weight.shape[1]
    all_cycles = cycle_count * groups
    scaled = (probes_in.astype(jnp.float32) * root_spectrum).astype(jnp.bfloat16)
    spectra = jnp.einsum(
        "pcml,lmj->pcmj", scaled, legendre, preferred_element_type=jnp.float32
    ).astype(jnp.bfloat16)
    cycle_index = (my_index * cycle_count + jnp.arange(cycle_count, dtype=jnp.int32)).astype(
        jnp.float32
    )
    local_sines = jnp.sin(math.pi * (cycle_index + 0.5) / all_cycles)
    area = 2.0 * math.pi / lon_count * (math.pi / all_cycles) * local_sines
    forward_tables = fourier_tables(order_slots, lon_count)
    squares, analysed = cycle_work(
        lax.all_to_all(spectra, ("lat", "blk"), split_axis=3, concat_axis=2, tiled=True),
        forward_tables,
        forward_tables,
        area,
        weight,
    )
    returned = lax.all_to_all(analysed, ("lat", "blk"), split_axis=2, concat_axis=3, tiled=True)
    matvec = (
        jnp.einsum("pcmj,lmj->pcml", returned, legendre, preferred_element_type=jnp.float32)
        * root_spectrum
    )
    grad_terms = jnp.einsum("pjx,p->jx", squares, beta) * area[:, None]
    gradient = lax.psum_scatter(grad_terms, "probe", scatter_dimension=1, tiled=True)
    return (matvec, gradient)


def dot(a, b, dims=((1,), (0,))):
    return lax.dot_general(a, b, (dims, ((), ())), preferred_element_type=jnp.float32)


def split(x):
    upper = x.astype(jnp.bfloat16)
    return upper, (x - upper.astype(jnp.float32)).astype(jnp.bfloat16)


def same_slot(rows):
    row = lax.broadcasted_iota(jnp.int32, (rows, WIDTH), 0)
    lane = lax.broadcasted_iota(jnp.int32, (rows, WIDTH), 1)
    return (row % GROUP) == (lane % GROUP)


def table_rows(tbl_ref, parity, part):
    piece = tbl_ref[pl.ds(32 * part, 32), parity]
    return piece.reshape(WIDTH, piece.shape[-1])


def synth_kernel(x_ref, root_ref, tbl_ref, spread_ref, sign_ref, out_ref, acc):
    step = pl.program_id(1)
    cycles = out_ref.shape[3] // CHUNK
    half = out_ref.shape[0] // 2
    rows = CHUNK * 2 * GROUP

    @pl.when(step == 0)
    def _():
        acc[...] = jnp.zeros_like(acc)

    x = (x_ref[...].astype(jnp.float32) * root_ref[...]).reshape(rows, DEPTH).astype(jnp.bfloat16)
    keep = same_slot(rows)
    for parity in range(2):
        total = acc[parity]
        for part in range(DEPTH // 64):
            wide = dot(x, spread_ref[parity, part])
            wide = jnp.where(keep, wide, 0.0).astype(jnp.bfloat16)
            total = total + dot(wide, table_rows(tbl_ref, parity, part))
        acc[parity] = total

    @pl.when(step == pl.num_programs(1) - 1)
    def _():
        even, odd = acc[0], acc[1]
        shape = (CHUNK, 2, GROUP, even.shape[-1])
        north = (even + odd).reshape(shape)
        south = (even - odd).reshape(shape) * sign_ref[...]
        for d in range(half):
            for c in range(2):
                for source, place in ((north, d), (south, 2 * half - 1 - d)):
                    pieces = [
                        source[p, c, :, d * cycles : (d + 1) * cycles] for p in range(CHUNK)
                    ]
                    out_ref[place, c] = jnp.concatenate(pieces, axis=-1).astype(jnp.bfloat16)


def analysis_kernel(*refs, first):
    q_ref, root_ref, tbl_ref, gather_ref, sign_ref = refs[:5]
    out_ref, held = refs[-2:]
    step = pl.program_id(1)
    cycles = q_ref.shape[3] // CHUNK
    half = q_ref.shape[0] // 2
    rows = CHUNK * 2 * GROUP

    @pl.when(step == 0)
    def _():
        north, south = [], []
        blocks = [[q_ref[d, c].astype(jnp.float32) for c in range(2)] for d in range(2 * half)]
        for p in range(CHUNK):
            for c in range(2):
                cut = slice(p * cycles, (p + 1) * cycles)
                north.append(
                    jnp.concatenate([blocks[d][c][:, cut] for d in range(half)], axis=-1)
                )
                other = jnp.concatenate(
                    [blocks[2 * half - 1 - d][c][:, cut] for d in range(half)], axis=-1
                )
                south.append(other * sign_ref[...])
        north = jnp.concatenate(north, axis=0)
        south = jnp.concatenate(south, axis=0)
        for parity, folded in enumerate((north + south, north - south)):
            upper, lower = split(folded)
            held[parity, pl.ds(0, rows)] = upper
            held[parity, pl.ds(rows, rows)] = lower

    keep = same_slot(rows)
    total = jnp.zeros((rows, DEPTH), jnp.float32)
    for parity in range(2):
        for part in range(DEPTH // 64):
            both = dot(held[parity], table_rows(tbl_ref, parity, part), ((1,), (1,)))
            wide = jnp.where(keep, both[:rows] + both[rows:], 0.0)
            upper, lower = split(wide)
            total = total + dot(upper, gather_ref[parity, part])
            total = total + dot(lower, gather_ref[parity, part])
    out_ref[...] = total.reshape(out_ref.shape) * root_ref[...]


def fourier_kernel(*refs, first):
    (r_ref, cos_hi, cos_lo, sin_hi, sin_lo, back_cos_hi, back_cos_lo, back_sin_hi, back_sin_lo) = (
        refs[:9]
    )
    w_low, w_high, turn_ref, beta_ref = refs[9:13]
    out_ref, g_low, g_high, rc, rs, acc_c, acc_s, middle = refs[-8:]
    old_low, old_high = (None, None) if first else refs[13:15]
    step = pl.program_id(0)
    sources, _, slots, _ = r_ref.shape

    @pl.when(step == 0)
    def _():
        for pair in range(sources // 2):
            for c, place in ((0, rc), (1, rs)):
                both = [r_ref[2 * pair + i, c].astype(jnp.float32) for i in range(2)]
                place[pl.ds(2 * slots * pair, 2 * slots)] = jnp.concatenate(both, axis=0).astype(
                    jnp.bfloat16
                )
        turned = turn_ref[...] * rc[...].astype(jnp.float32)
        mid = jnp.sum(turned, axis=0, keepdims=True)
        middle[...] = mid
        w_mid = (w_high[pl.ds(0, 1), :] * mid).astype(jnp.bfloat16).astype(jnp.float32)
        acc_c[...] = turn_ref[...] * w_mid
        acc_s[...] = jnp.zeros_like(acc_s)

    c_part = dot(cos_hi[...], rc[...]) + dot(cos_lo[...], rc[...])
    s_part = dot(sin_hi[...], rs[...]) + dot(sin_lo[...], rs[...])
    low = c_part + s_part
    row = lax.broadcasted_iota(jnp.int32, low.shape, 0) + step * low.shape[0]
    high = jnp.where(row == 0, middle[...], c_part - s_part)
    beta = beta_ref[...]
    low_sq = beta * (low * low)
    high_sq = beta * (high * high)
    g_low[...] = low_sq if first else old_low[...] + low_sq
    g_high[...] = high_sq if first else old_high[...] + high_sq
    low = (w_low[...] * low).astype(jnp.bfloat16).astype(jnp.float32)
    high = jnp.where(row == 0, 0.0, w_high[...] * high).astype(jnp.bfloat16).astype(jnp.float32)
    for folded, hi, lo, acc in (
        (low + high, back_cos_hi, back_cos_lo, acc_c),
        (low - high, back_sin_hi, back_sin_lo, acc_s),
    ):
        upper, lower = split(folded)
        acc[...] += dot(hi[...], upper) + dot(lo[...], upper) + dot(hi[...], lower)

    @pl.when(step == pl.num_programs(0) - 1)
    def _():
        for d in range(sources):
            for c, acc in ((0, acc_c), (1, acc_s)):
                out_ref[d, c] = acc[pl.ds(slots * d, slots)].astype(jnp.bfloat16)


def half_tables(orders, lon_count):
    half = lon_count // 2

    def trig(points):
        idx = orders[:, None] * points[None, :] % lon_count
        angle = idx.astype(jnp.float32) * (2.0 * math.pi / lon_count)
        return lax.optimization_barrier((jnp.cos(angle), jnp.sin(angle)))

    def joined(parts, fine, shape, axes):
        (ca, sa), (cb, sb) = parts
        ca, sa = (t[axes[0]] for t in (ca, sa))
        cb, sb = (t[axes[1]] for t in (cb, sb))
        cosine = (ca * cb - sa * sb).reshape(shape)
        sine = (sa * cb + ca * sb).reshape(shape)
        return split(cosine) + split(sine)

    count = orders.shape[0]
    fine = 128
    coarse_points = jnp.arange(half // fine, dtype=jnp.int32) * fine
    fine_points = jnp.arange(fine, dtype=jnp.int32)
    coarse, small = trig(coarse_points), trig(fine_points)
    every = slice(None)
    back = joined(
        (coarse, small), fine, (count, half), ((every, every, None), (every, None, every))
    )
    coarse_t = tuple(t.T for t in coarse)
    small_t = tuple(t.T for t in small)
    ahead = joined(
        (coarse_t, small_t), fine, (half, count), ((every, None, every), (None, every, every))
    )
    return ahead, back


def fast_body(probes_in, root_spectrum, order_slots, legendre, weight, beta):
    axes = ("lat", "blk")
    groups = lax.axis_size(axes)
    my_index = lax.axis_index(axes)
    cycles, lon_count = weight.shape
    half_lon = lon_count // 2
    all_cycles = cycles * groups
    half_cycles = all_cycles // 2
    degrees, slots = legendre.shape[:2]
    orders_count = order_slots.shape[0]
    probes = probes_in.shape[0]
    chunks = probes // CHUNK
    lanes = CHUNK * cycles
    south = my_index >= groups // 2
    params = functools.partial(pltpu.CompilerParams, vmem_limit_bytes=VMEM_LIMIT)
    f32, bf16 = jnp.float32, jnp.bfloat16

    my_orders = lax.dynamic_slice_in_dim(order_slots, my_index * slots, slots)
    sign = (1 - 2 * (my_orders % 2)).astype(f32)
    sign = jnp.broadcast_to(sign[:, None], (slots, half_cycles))
    root = root_spectrum[None, :]
    table = legendre.reshape(degrees // 2, 2, slots, all_cycles)

    degree = jnp.arange(DEPTH)[:, None]
    place = jnp.arange(WIDTH)[None, :] // GROUP
    spread = jnp.stack(
        [
            jnp.stack([degree == 2 * (32 * part + place) + parity for part in range(DEPTH // 64)])
            for parity in range(2)
        ]
    ).astype(bf16)
    gather = jnp.swapaxes(spread, 2, 3)
    grid = (slots // GROUP, degrees // DEPTH)
    rows = CHUNK * 2 * GROUP
    table_spec = pl.BlockSpec(
        (DEPTH // 2, 2, GROUP, half_cycles), lambda g, i: (i, 0, g, 0)
    )
    root_spec = pl.BlockSpec((1, DEPTH), lambda g, i: (0, i))
    sign_spec = pl.BlockSpec((GROUP, half_cycles), lambda g, i: (g, 0))
    whole = lambda shape: pl.BlockSpec(shape, lambda *_: (0,) * len(shape))
    payload_spec = pl.BlockSpec((groups, 2, GROUP, lanes), lambda g, i: (0, 0, g, 0))
    payload = jax.ShapeDtypeStruct((groups, 2, slots, lanes), bf16)
    table_bytes = degrees * slots * half_cycles * 2

    def synth(q):
        return pl.pallas_call(
            synth_kernel,
            name="synth",
            grid=grid,
            in_specs=[
                pl.BlockSpec((CHUNK, 2, GROUP, DEPTH), lambda g, i: (q, 0, g, i)),
                root_spec,
                table_spec,
                whole(spread.shape),
                sign_spec,
            ],
            out_specs=payload_spec,
            out_shape=payload,
            scratch_shapes=[pltpu.VMEM((2, rows, half_cycles), f32)],
            compiler_params=params(),
            cost_estimate=pl.CostEstimate(
                flops=4 * rows * table_bytes, bytes_accessed=table_bytes, transcendentals=0
            ),
        )(probes_in, root, table, spread, sign)

    def analyse(q, returned, held):
        first = held is None
        return pl.pallas_call(
            functools.partial(analysis_kernel, first=first),
            name="analyse",
            grid=grid,
            in_specs=[payload_spec, root_spec, table_spec, whole(gather.shape), sign_spec]
            + ([] if first else [pl.BlockSpec(memory_space=pl.ANY)]),
            out_specs=pl.BlockSpec((CHUNK, 2, GROUP, DEPTH), lambda g, i: (q, 0, g, i)),
            out_shape=jax.ShapeDtypeStruct((probes, 2, slots, degrees), f32),
            scratch_shapes=[pltpu.VMEM((2, 2 * rows, half_cycles), bf16)],
            input_output_aliases={} if first else {5: 0},
            compiler_params=params(),
            cost_estimate=pl.CostEstimate(
                flops=4 * rows * table_bytes, bytes_accessed=table_bytes, transcendentals=0
            ),
        )(returned, root, table, gather, sign, *([] if first else [held]))

    ahead_spec = pl.BlockSpec((TILE, orders_count), lambda i: (i, 0))
    back_spec = pl.BlockSpec((orders_count, TILE), lambda i: (0, i))
    grid_spec = pl.BlockSpec((TILE, lanes), lambda i: (i, 0))

    def fourier(received, tables, w_low, w_high, turn, chunk_beta, old):
        first = old is None
        ahead, back = tables
        square = jax.ShapeDtypeStruct((half_lon, lanes), f32)
        return pl.pallas_call(
            functools.partial(fourier_kernel, first=first),
            name="fourier",
            grid=(half_lon // TILE,),
            in_specs=[whole(payload.shape)]
            + [ahead_spec] * 4
            + [back_spec] * 4
            + [grid_spec] * 2
            + [whole((orders_count, 1)), whole((1, lanes))]
            + ([] if first else [grid_spec] * 2),
            out_specs=[whole(payload.shape), grid_spec, grid_spec],
            out_shape=[payload, square, square],
            scratch_shapes=[pltpu.VMEM((orders_count, lanes), bf16)] * 2
            + [pltpu.VMEM((orders_count, lanes), f32)] * 2
            + [pltpu.VMEM((1, lanes), f32)],
            input_output_aliases={} if first else {13: 1, 14: 2},
            compiler_params=params(),
            cost_estimate=pl.CostEstimate(
                flops=20 * half_lon * lanes * orders_count,
                bytes_accessed=16 * half_lon * orders_count + 16 * half_lon * lanes,
                transcendentals=0,
            ),
        )(received, *ahead, *back, w_low, w_high, turn, chunk_beta, *([] if first else old))

    def exchange(x):
        return lax.all_to_all(x, axes, split_axis=0, concat_axis=0, tiled=True)

    local = jnp.arange(cycles, dtype=jnp.int32)
    flipped = jnp.where(south, cycles - 1 - local, local)
    cycle_index = (my_index * cycles + flipped).astype(f32)
    area = 2.0 * math.pi / lon_count * (math.pi / all_cycles) * jnp.sin(
        math.pi * (cycle_index + 0.5) / all_cycles
    )
    turned = jnp.where(south, jnp.flip(weight, 0), weight)
    turned = (area[:, None] * turned).T
    w_low = jnp.tile(turned[:half_lon], (1, CHUNK))
    w_high = jnp.concatenate(
        [turned[half_lon : half_lon + 1], jnp.flip(turned[half_lon + 1 :], 0)], axis=0
    )
    w_high = jnp.tile(w_high, (1, CHUNK))
    turn = (1 - 2 * (order_slots % 2)).astype(f32)[:, None]
    tables = half_tables(order_slots, lon_count)

    received = [exchange(synth(q)) for q in range(chunks)]
    old, held = None, None
    returned = []
    for q in range(chunks):
        chunk_beta = jnp.repeat(beta[q * CHUNK : (q + 1) * CHUNK], cycles)[None, :]
        analysed, low, high = fourier(received[q], tables, w_low, w_high, turn, chunk_beta, old)
        old = (low, high)
        returned.append(exchange(analysed))
    for q in range(chunks):
        held = analyse(q, returned[q], held)

    lane_cycle = jnp.arange(lanes, dtype=jnp.int32) % cycles
    pick = (lane_cycle[None, :] == flipped[:, None]).astype(f32)
    sums = [
        lax.dot_general(
            pick, s, (((1,), (1,)), ((), ())), precision=lax.Precision.HIGHEST,
            preferred_element_type=f32,
        )
        for s in old
    ]
    natural = 2.0 * math.pi / lon_count * (math.pi / all_cycles) * jnp.sin(
        math.pi * ((my_index * cycles + local).astype(f32) + 0.5) / all_cycles
    )
    terms = jnp.concatenate([sums[0], sums[1][:, :1], jnp.flip(sums[1][:, 1:], 1)], axis=1)
    gradient = lax.psum_scatter(
        terms * natural[:, None], "probe", scatter_dimension=1, tiled=True
    )
    return (held, gradient)


def body(probes_in, root_spectrum, order_slots, legendre, weight, beta):
    degrees, slots, all_cycles = legendre.shape
    lanes = CHUNK * weight.shape[0]
    fits = (
        slots % GROUP == 0
        and degrees % DEPTH == 0
        and all_cycles % 256 == 0
        and lanes % 128 == 0
        and probes_in.shape[0] % CHUNK == 0
        and weight.shape[1] % (2 * TILE) == 0
        and lax.axis_size(("lat", "blk")) % 2 == 0
        and order_slots.shape[0] % 128 == 0
    )
    chosen = fast_body if fits else plain_body
    return chosen(probes_in, root_spectrum, order_slots, legendre, weight, beta)


def solution(mesh):
    return jax.shard_map(
        body,
        mesh=mesh,
        in_specs=(
            P("probe", None, ("lat", "blk"), None),
            P(),
            P(),
            P(None, ("lat", "blk"), None),
            P(("lat", "blk"), None),
            P("probe"),
        ),
        out_specs=(P("probe", None, ("lat", "blk"), None), P(("lat", "blk"), "probe")),
        check_vma=False,
    )
```

```python
import functools
import math

import jax
import jax.numpy as jnp
from jax import lax
from jax.experimental import pallas as pl
from jax.experimental.pallas import tpu as pltpu
from jax.sharding import PartitionSpec as P

GROUP = 8
DEPTH = 128
CHUNK = 16
PART = 8
TILE = 256
VMEM_LIMIT = 60 * 2**20


def fourier_tables(orders, lon_count):
    longitude = jnp.arange(lon_count, dtype=jnp.int32)
    phase_idx = orders[:, None] * longitude[None, :] % lon_count
    angle = phase_idx.astype(jnp.float32) * (2.0 * math.pi / lon_count)
    twiddle = jnp.stack([jnp.cos(angle), jnp.sin(angle)])
    upper = twiddle.astype(jnp.bfloat16)
    lower = (twiddle - upper.astype(jnp.float32)).astype(jnp.bfloat16)
    return (upper, lower)


def cycle_work(spectra, inverse_tables, forward_tables, area, weight):
    grid_field = jnp.einsum(
        "pcmj,cmx->pjx", spectra, inverse_tables[0], preferred_element_type=jnp.float32
    )
    grid_field = grid_field + jnp.einsum(
        "pcmj,cmx->pjx", spectra, inverse_tables[1], preferred_element_type=jnp.float32
    )
    squares = grid_field * grid_field
    weighted = (area[None, :, None] * weight[None] * grid_field).astype(jnp.bfloat16)
    analysed = jnp.einsum(
        "pjx,cmx->pcmj", weighted, forward_tables[0], preferred_element_type=jnp.float32
    )
    analysed = analysed + jnp.einsum(
        "pjx,cmx->pcmj", weighted, forward_tables[1], preferred_element_type=jnp.float32
    )
    return (squares, analysed.astype(jnp.bfloat16))


def plain_body(probes_in, root_spectrum, order_slots, legendre, weight, beta):
    groups = lax.axis_size(("lat", "blk"))
    my_index = lax.axis_index(("lat", "blk"))
    cycle_count = weight.shape[0]
    lon_count = weight.shape[1]
    all_cycles = cycle_count * groups
    scaled = (probes_in.astype(jnp.float32) * root_spectrum).astype(jnp.bfloat16)
    spectra = jnp.einsum(
        "pcml,lmj->pcmj", scaled, legendre, preferred_element_type=jnp.float32
    ).astype(jnp.bfloat16)
    cycle_index = (my_index * cycle_count + jnp.arange(cycle_count, dtype=jnp.int32)).astype(
        jnp.float32
    )
    local_sines = jnp.sin(math.pi * (cycle_index + 0.5) / all_cycles)
    area = 2.0 * math.pi / lon_count * (math.pi / all_cycles) * local_sines
    forward_tables = fourier_tables(order_slots, lon_count)
    squares, analysed = cycle_work(
        lax.all_to_all(spectra, ("lat", "blk"), split_axis=3, concat_axis=2, tiled=True),
        forward_tables,
        forward_tables,
        area,
        weight,
    )
    returned = lax.all_to_all(analysed, ("lat", "blk"), split_axis=2, concat_axis=3, tiled=True)
    matvec = (
        jnp.einsum("pcmj,lmj->pcml", returned, legendre, preferred_element_type=jnp.float32)
        * root_spectrum
    )
    grad_terms = jnp.einsum("pjx,p->jx", squares, beta) * area[:, None]
    gradient = lax.psum_scatter(grad_terms, "probe", scatter_dimension=1, tiled=True)
    return (matvec, gradient)


def dot(a, b, dims=((1,), (0,))):
    return lax.dot_general(a, b, (dims, ((), ())), preferred_element_type=jnp.float32)


def split(x):
    upper = x.astype(jnp.bfloat16)
    return upper, (x - upper.astype(jnp.float32)).astype(jnp.bfloat16)


LANES = 128


def every(slot, count):
    return pl.ds(slot, count, stride=GROUP)


def tiles(ref):
    return range(ref.shape[0])


def put(ref, rows, value):
    for t in tiles(ref):
        ref[t, rows, :] = value[:, t * LANES : (t + 1) * LANES]


def take(ref, rows):
    return jnp.concatenate([ref[t, rows, :] for t in tiles(ref)], axis=-1)


def spread_rows(tbl_ref, wide):
    @pl.loop(0, tbl_ref.shape[0] * 2 // DEPTH)
    def _(step):
        some = pl.ds(step * (DEPTH // 2), DEPTH // 2)
        for t in tiles(wide):
            piece = tbl_ref[some, :, :, t * LANES : (t + 1) * LANES].astype(jnp.float32)
            wide[t, pl.ds(step * (DEPTH * GROUP), DEPTH * GROUP)] = piece.reshape(
                DEPTH * GROUP, LANES
            )


def visit(orders_ref, group, turn, pair, steps):
    first = orders_ref[group * GROUP + 2 * pair] // DEPTH
    mine = turn < steps - first
    slot = 2 * pair + jnp.where(mine, 0, 1)
    return slot, jnp.where(mine, first + turn, turn - 1)


def even_degree(shape):
    return lax.broadcasted_iota(jnp.int32, shape, 1) % 2 == 0


def synth_kernel(orders_ref, x_ref, root_ref, tbl_ref, sign_ref, out_ref, xs, wide, acc, ns, ss):
    group = pl.program_id(0)
    chunk = x_ref.shape[0]
    cycles = out_ref.shape[3] // chunk
    half = out_ref.shape[0] // 2
    rows = chunk * 2
    scaled = (x_ref[...].astype(jnp.float32) * root_ref[...]).astype(jnp.bfloat16)
    put(xs, slice(None), scaled.astype(jnp.float32).reshape(rows * GROUP, scaled.shape[-1]))
    acc[...] = jnp.zeros_like(acc)

    spread_rows(tbl_ref, wide)
    steps = tbl_ref.shape[0] * 2 // DEPTH

    @pl.loop(0, steps + 1)
    def _(turn):
        for pair in range(GROUP // 2):
            slot, step = visit(orders_ref, group, turn, pair, steps)
            x = xs[step, every(slot, rows), :]
            even = even_degree(x.shape)
            x = jnp.concatenate([jnp.where(even, x, 0.0), jnp.where(even, 0.0, x)], axis=0)
            table = take(wide, every(step * (DEPTH * GROUP) + slot, DEPTH)).astype(jnp.bfloat16)
            acc[slot] += dot(x.astype(jnp.bfloat16), table)

    for slot in range(GROUP):
        even, odd = acc[slot, :rows], acc[slot, rows:]
        put(ns, every(slot, rows), even + odd)
        put(ss, every(slot, rows), even - odd)
    for c in range(2):
        north, south = [], []
        for p in range(chunk):
            place = pl.ds((2 * p + c) * GROUP, GROUP)
            north.append(take(ns, place))
            south.append(take(ss, place) * sign_ref[...])
        for d in range(half):
            for source, place in ((north, d), (south, 2 * half - 1 - d)):
                pieces = [piece[:, d * cycles : (d + 1) * cycles] for piece in source]
                out_ref[place, c] = jnp.concatenate(pieces, axis=-1).astype(jnp.bfloat16)


def analysis_kernel(*refs):
    orders_ref, q_ref, root_ref, tbl_ref, sign_ref = refs[:5]
    out_ref, plus, minus, wide, held, outs = refs[-6:]
    group = pl.program_id(0)
    chunk = out_ref.shape[0]
    cycles = q_ref.shape[3] // chunk
    half = q_ref.shape[0] // 2
    rows = chunk * 2

    for c in range(2):
        blocks = [q_ref[d, c].astype(jnp.float32) for d in range(2 * half)]
        for p in range(chunk):
            cut = slice(p * cycles, (p + 1) * cycles)
            north = jnp.concatenate([blocks[d][:, cut] for d in range(half)], axis=-1)
            other = [blocks[2 * half - 1 - d][:, cut] for d in range(half)]
            south = jnp.concatenate(other, axis=-1) * sign_ref[...]
            place = pl.ds((2 * p + c) * GROUP, GROUP)
            put(plus, place, north + south)
            put(minus, place, north - south)
    for slot in range(GROUP):
        both = [take(ref, every(slot, rows)) for ref in (plus, minus)]
        upper, lower = split(jnp.concatenate(both, axis=0))
        held[slot, : 2 * rows] = upper
        held[slot, 2 * rows :] = lower
    outs[...] = jnp.zeros_like(outs)

    spread_rows(tbl_ref, wide)
    steps = tbl_ref.shape[0] * 2 // DEPTH

    @pl.loop(0, steps + 1)
    def _(turn):
        for pair in range(GROUP // 2):
            slot, step = visit(orders_ref, group, turn, pair, steps)
            now = pl.ds(pl.multiple_of(step * DEPTH, DEPTH), DEPTH)
            table = take(wide, every(step * (DEPTH * GROUP) + slot, DEPTH)).astype(jnp.bfloat16)
            both = dot(held[slot], table, ((1,), (1,)))
            both = both[: 2 * rows] + both[2 * rows :]
            even = even_degree((rows, DEPTH))
            chosen = jnp.where(even, both[:rows], both[rows:])
            outs[step, every(slot, rows), :] = chosen * root_ref[:, now]

    for t in tiles(outs):
        cut = slice(t * LANES, (t + 1) * LANES)
        out_ref[:, :, :, cut] = outs[t].reshape(chunk, 2, GROUP, LANES)


def fourier_kernel(*refs, first):
    r_ref, ahead_cos, ahead_sin, back_cos, back_sin, w_low, w_high, turn_ref, beta_ref = refs[:9]
    out_ref, g_low, g_high, rc, rs, acc_c, acc_s, middle = refs[-8:]
    old_low, old_high = (None, None) if first else refs[9:11]
    step, part = pl.program_id(0), pl.program_id(1)
    sources, _, slots, _ = r_ref.shape
    tile, lanes = g_low.shape
    count = acc_c.shape[1]
    mine = pl.ds(pl.multiple_of(part * lanes, LANES), lanes)

    @pl.when(step == 0)
    def _():
        for pair in range(sources // 2):
            for c, place in ((0, rc), (1, rs)):
                both = [r_ref[2 * pair + i, c, :, mine].astype(jnp.float32) for i in range(2)]
                place[part, pl.ds(2 * slots * pair, 2 * slots)] = jnp.concatenate(
                    both, axis=0
                ).astype(jnp.bfloat16)
        turned = turn_ref[...] * rc[part].astype(jnp.float32)
        mid = jnp.sum(turned, axis=0, keepdims=True)
        middle[part] = mid
        w_mid = (w_high[pl.ds(0, 1), :] * mid).astype(jnp.bfloat16).astype(jnp.float32)
        acc_c[part] = turn_ref[...] * w_mid
        acc_s[part] = jnp.zeros_like(acc_s[part])

    c_part = dot(ahead_cos[0], rc[part])
    c_part = c_part[:tile] + c_part[tile:]
    s_part = dot(ahead_sin[0], rs[part])
    s_part = s_part[:tile] + s_part[tile:]
    low = c_part + s_part
    row = lax.broadcasted_iota(jnp.int32, low.shape, 0) + step * tile
    high = jnp.where(row == 0, middle[part], c_part - s_part)
    beta = beta_ref[:, mine]
    low_sq = beta * (low * low)
    high_sq = beta * (high * high)

    @pl.when(part == 0)
    def _():
        g_low[...] = low_sq if first else old_low[...] + low_sq
        g_high[...] = high_sq if first else old_high[...] + high_sq

    @pl.when(part > 0)
    def _():
        g_low[...] += low_sq
        g_high[...] += high_sq

    low = (w_low[...] * low).astype(jnp.bfloat16).astype(jnp.float32)
    high = jnp.where(row == 0, 0.0, w_high[...] * high).astype(jnp.bfloat16).astype(jnp.float32)
    for folded, back, acc in ((low + high, back_cos, acc_c), (low - high, back_sin, acc_s)):
        upper, lower = split(folded)
        both = dot(back[...], upper)
        acc[part] += both[:count] + both[count:] + dot(back[pl.ds(0, count), :], lower)

    @pl.when(step == pl.num_programs(0) - 1)
    def _():
        for d in range(sources):
            for c, acc in ((0, acc_c), (1, acc_s)):
                out_ref[d, c, :, mine] = acc[part, pl.ds(slots * d, slots)].astype(jnp.bfloat16)


def half_tables(orders, lon_count):
    half = lon_count // 2

    def trig(points):
        idx = orders[:, None] * points[None, :] % lon_count
        angle = idx.astype(jnp.float32) * (2.0 * math.pi / lon_count)
        return lax.optimization_barrier((jnp.cos(angle), jnp.sin(angle)))

    def joined(parts, fine, shape, axes):
        (ca, sa), (cb, sb) = parts
        ca, sa = (t[axes[0]] for t in (ca, sa))
        cb, sb = (t[axes[1]] for t in (cb, sb))
        cosine = (ca * cb - sa * sb).reshape(shape)
        sine = (sa * cb + ca * sb).reshape(shape)
        return split(cosine) + split(sine)

    count = orders.shape[0]
    fine = 128
    coarse_points = jnp.arange(half // fine, dtype=jnp.int32) * fine
    fine_points = jnp.arange(fine, dtype=jnp.int32)
    coarse, small = trig(coarse_points), trig(fine_points)
    every = slice(None)
    back = joined(
        (coarse, small), fine, (count, half), ((every, every, None), (every, None, every))
    )
    coarse_t = tuple(t.T for t in coarse)
    small_t = tuple(t.T for t in small)
    ahead = joined(
        (coarse_t, small_t), fine, (half, count), ((every, None, every), (None, every, every))
    )
    tiled = [t.reshape(half // TILE, TILE, count) for t in ahead]
    ahead = [jnp.concatenate(tiled[i : i + 2], axis=1) for i in (0, 2)]
    back = [jnp.concatenate(back[i : i + 2], axis=0) for i in (0, 2)]
    return ahead, back


def fast_body(probes_in, root_spectrum, order_slots, legendre, weight, beta):
    axes = ("lat", "blk")
    groups = lax.axis_size(axes)
    my_index = lax.axis_index(axes)
    cycles, lon_count = weight.shape
    half_lon = lon_count // 2
    all_cycles = cycles * groups
    half_cycles = all_cycles // 2
    degrees, slots = legendre.shape[:2]
    orders_count = order_slots.shape[0]
    probes = probes_in.shape[0]
    chunks = probes // CHUNK
    lanes = CHUNK * cycles
    part_lanes = PART * cycles
    parts = CHUNK // PART
    south = my_index >= groups // 2
    params = functools.partial(pltpu.CompilerParams, vmem_limit_bytes=VMEM_LIMIT)
    f32, bf16 = jnp.float32, jnp.bfloat16

    my_orders = lax.dynamic_slice_in_dim(order_slots, my_index * slots, slots)
    sign = (1 - 2 * (my_orders % 2)).astype(f32)
    sign = jnp.broadcast_to(sign[:, None], (slots, half_cycles))
    root = root_spectrum[None, :]
    table = legendre.reshape(degrees // 2, 2, slots, all_cycles)
    rows = CHUNK * 2
    whole = lambda shape: pl.BlockSpec(shape, lambda *_: (0,) * len(shape))
    table_spec = pl.BlockSpec((degrees // 2, 2, GROUP, half_cycles), lambda g, o: (0, 0, g, 0))
    sign_spec = pl.BlockSpec((GROUP, half_cycles), lambda g, o: (g, 0))
    payload_spec = pl.BlockSpec((groups, 2, GROUP, lanes), lambda g, o: (0, 0, g, 0))
    payload = jax.ShapeDtypeStruct((groups, 2, slots, lanes), bf16)
    table_bytes = degrees * slots * half_cycles * 2
    legendre_cost = pl.CostEstimate(
        flops=1000 * table_bytes, bytes_accessed=table_bytes, transcendentals=0
    )
    tiled = lambda width, height: pltpu.VMEM((width // LANES, height, LANES), f32)
    degree_tiles = tiled(degrees, rows * GROUP)
    cycle_tiles = tiled(half_cycles, rows * GROUP)
    wide = tiled(half_cycles, degrees * GROUP)

    def chunk_spec(q):
        return pl.BlockSpec((CHUNK, 2, GROUP, degrees), lambda g, o: (q, 0, g, 0))

    def synth(q):
        return pl.pallas_call(
            synth_kernel,
            name="synth",
            grid_spec=pltpu.PrefetchScalarGridSpec(
                num_scalar_prefetch=1,
                grid=(slots // GROUP,),
                in_specs=[chunk_spec(q), whole(root.shape), table_spec, sign_spec],
                out_specs=payload_spec,
                scratch_shapes=[
                    degree_tiles,
                    wide,
                    pltpu.VMEM((GROUP, 2 * rows, half_cycles), f32),
                    cycle_tiles,
                    cycle_tiles,
                ],
            ),
            out_shape=payload,
            compiler_params=params(),
            cost_estimate=legendre_cost,
        )(my_orders, probes_in, root, table, sign)

    def analyse(q, returned, held):
        first = held is None
        return pl.pallas_call(
            analysis_kernel,
            name="analyse",
            grid_spec=pltpu.PrefetchScalarGridSpec(
                num_scalar_prefetch=1,
                grid=(slots // GROUP,),
                in_specs=[payload_spec, whole(root.shape), table_spec, sign_spec]
                + ([] if first else [pl.BlockSpec(memory_space=pl.ANY)]),
                out_specs=chunk_spec(q),
                scratch_shapes=[
                    cycle_tiles,
                    cycle_tiles,
                    wide,
                    pltpu.VMEM((GROUP, 4 * rows, half_cycles), bf16),
                    degree_tiles,
                ],
            ),
            out_shape=jax.ShapeDtypeStruct((probes, 2, slots, degrees), f32),
            input_output_aliases={} if first else {5: 0},
            compiler_params=params(),
            cost_estimate=legendre_cost,
        )(my_orders, returned, root, table, sign, *([] if first else [held]))

    ahead_spec = pl.BlockSpec((1, 2 * TILE, orders_count), lambda i, h: (i, 0, 0))
    back_spec = pl.BlockSpec((2 * orders_count, TILE), lambda i, h: (0, i))
    grid_spec = pl.BlockSpec((TILE, part_lanes), lambda i, h: (i, 0))

    def fourier(received, tables, w_low, w_high, turn, chunk_beta, old):
        first = old is None
        ahead, back = tables
        square = jax.ShapeDtypeStruct((half_lon, part_lanes), f32)
        return pl.pallas_call(
            functools.partial(fourier_kernel, first=first),
            name="fourier",
            grid=(half_lon // TILE, parts),
            in_specs=[whole(payload.shape)]
            + [ahead_spec] * 2
            + [back_spec] * 2
            + [grid_spec] * 2
            + [whole((orders_count, 1)), whole((1, lanes))]
            + ([] if first else [grid_spec] * 2),
            out_specs=[whole(payload.shape), grid_spec, grid_spec],
            out_shape=[payload, square, square],
            scratch_shapes=[pltpu.VMEM((parts, orders_count, part_lanes), bf16)] * 2
            + [pltpu.VMEM((parts, orders_count, part_lanes), f32)] * 2
            + [pltpu.VMEM((parts, 1, part_lanes), f32)],
            input_output_aliases={} if first else {9: 1, 10: 2},
            compiler_params=params(),
            cost_estimate=pl.CostEstimate(
                flops=40 * half_lon * lanes * orders_count,
                bytes_accessed=16 * half_lon * orders_count + 16 * half_lon * part_lanes,
                transcendentals=0,
            ),
        )(received, *ahead, *back, w_low, w_high, turn, chunk_beta, *([] if first else old))

    def exchange(x):
        return lax.all_to_all(x, axes, split_axis=0, concat_axis=0, tiled=True)

    local = jnp.arange(cycles, dtype=jnp.int32)
    flipped = jnp.where(south, cycles - 1 - local, local)
    cycle_index = (my_index * cycles + flipped).astype(f32)
    area = 2.0 * math.pi / lon_count * (math.pi / all_cycles) * jnp.sin(
        math.pi * (cycle_index + 0.5) / all_cycles
    )
    turned = jnp.where(south, jnp.flip(weight, 0), weight)
    turned = (area[:, None] * turned).T
    w_low = jnp.tile(turned[:half_lon], (1, PART))
    w_high = jnp.concatenate(
        [turned[half_lon : half_lon + 1], jnp.flip(turned[half_lon + 1 :], 0)], axis=0
    )
    w_high = jnp.tile(w_high, (1, PART))
    turn = (1 - 2 * (order_slots % 2)).astype(f32)[:, None]
    tables = half_tables(order_slots, lon_count)

    received = [exchange(synth(q)) for q in range(chunks)]
    old, held = None, None
    returned = []
    for q in range(chunks):
        chunk_beta = jnp.repeat(beta[q * CHUNK : (q + 1) * CHUNK], cycles)[None, :]
        analysed, low, high = fourier(received[q], tables, w_low, w_high, turn, chunk_beta, old)
        old = (low, high)
        returned.append(exchange(analysed))
    for q in range(chunks):
        held = analyse(q, returned[q], held)

    lane_cycle = jnp.arange(part_lanes, dtype=jnp.int32) % cycles
    pick = (lane_cycle[None, :] == flipped[:, None]).astype(f32)
    sums = [
        lax.dot_general(
            pick, s, (((1,), (1,)), ((), ())), precision=lax.Precision.HIGHEST,
            preferred_element_type=f32,
        )
        for s in old
    ]
    natural = 2.0 * math.pi / lon_count * (math.pi / all_cycles) * jnp.sin(
        math.pi * ((my_index * cycles + local).astype(f32) + 0.5) / all_cycles
    )
    terms = jnp.concatenate([sums[0], sums[1][:, :1], jnp.flip(sums[1][:, 1:], 1)], axis=1)
    gradient = lax.psum_scatter(
        terms * natural[:, None], "probe", scatter_dimension=1, tiled=True
    )
    return (held, gradient)


def body(probes_in, root_spectrum, order_slots, legendre, weight, beta):
    degrees, slots, all_cycles = legendre.shape
    fits = (
        slots % GROUP == 0
        and degrees % DEPTH == 0
        and degrees == order_slots.shape[0]
        and all_cycles % (2 * LANES) == 0
        and (PART * weight.shape[0]) % LANES == 0
        and probes_in.shape[0] % CHUNK == 0
        and weight.shape[1] % (2 * TILE) == 0
        and lax.axis_size(("lat", "blk")) % 2 == 0
    )
    chosen = fast_body if fits else plain_body
    return chosen(probes_in, root_spectrum, order_slots, legendre, weight, beta)


def solution(mesh):
    return jax.shard_map(
        body,
        mesh=mesh,
        in_specs=(
            P("probe", None, ("lat", "blk"), None),
            P(),
            P(),
            P(None, ("lat", "blk"), None),
            P(("lat", "blk"), None),
            P("probe"),
        ),
        out_specs=(P("probe", None, ("lat", "blk"), None), P(("lat", "blk"), "probe")),
        check_vma=False,
    )
```

```python
import functools
import math

import jax
import jax.numpy as jnp
from jax import lax
from jax.experimental import pallas as pl
from jax.experimental.pallas import tpu as pltpu
from jax.sharding import PartitionSpec as P

GROUP = 8
DEPTH = 128
CHUNK = 16
PART = 8
TILE = 256
VMEM_LIMIT = 60 * 2**20


def fourier_tables(orders, lon_count):
    longitude = jnp.arange(lon_count, dtype=jnp.int32)
    phase_idx = orders[:, None] * longitude[None, :] % lon_count
    angle = phase_idx.astype(jnp.float32) * (2.0 * math.pi / lon_count)
    twiddle = jnp.stack([jnp.cos(angle), jnp.sin(angle)])
    upper = twiddle.astype(jnp.bfloat16)
    lower = (twiddle - upper.astype(jnp.float32)).astype(jnp.bfloat16)
    return (upper, lower)


def cycle_work(spectra, inverse_tables, forward_tables, area, weight):
    grid_field = jnp.einsum(
        "pcmj,cmx->pjx", spectra, inverse_tables[0], preferred_element_type=jnp.float32
    )
    grid_field = grid_field + jnp.einsum(
        "pcmj,cmx->pjx", spectra, inverse_tables[1], preferred_element_type=jnp.float32
    )
    squares = grid_field * grid_field
    weighted = (area[None, :, None] * weight[None] * grid_field).astype(jnp.bfloat16)
    analysed = jnp.einsum(
        "pjx,cmx->pcmj", weighted, forward_tables[0], preferred_element_type=jnp.float32
    )
    analysed = analysed + jnp.einsum(
        "pjx,cmx->pcmj", weighted, forward_tables[1], preferred_element_type=jnp.float32
    )
    return (squares, analysed.astype(jnp.bfloat16))


def plain_body(probes_in, root_spectrum, order_slots, legendre, weight, beta):
    groups = lax.axis_size(("lat", "blk"))
    my_index = lax.axis_index(("lat", "blk"))
    cycle_count = weight.shape[0]
    lon_count = weight.shape[1]
    all_cycles = cycle_count * groups
    scaled = (probes_in.astype(jnp.float32) * root_spectrum).astype(jnp.bfloat16)
    spectra = jnp.einsum(
        "pcml,lmj->pcmj", scaled, legendre, preferred_element_type=jnp.float32
    ).astype(jnp.bfloat16)
    cycle_index = (my_index * cycle_count + jnp.arange(cycle_count, dtype=jnp.int32)).astype(
        jnp.float32
    )
    local_sines = jnp.sin(math.pi * (cycle_index + 0.5) / all_cycles)
    area = 2.0 * math.pi / lon_count * (math.pi / all_cycles) * local_sines
    forward_tables = fourier_tables(order_slots, lon_count)
    squares, analysed = cycle_work(
        lax.all_to_all(spectra, ("lat", "blk"), split_axis=3, concat_axis=2, tiled=True),
        forward_tables,
        forward_tables,
        area,
        weight,
    )
    returned = lax.all_to_all(analysed, ("lat", "blk"), split_axis=2, concat_axis=3, tiled=True)
    matvec = (
        jnp.einsum("pcmj,lmj->pcml", returned, legendre, preferred_element_type=jnp.float32)
        * root_spectrum
    )
    grad_terms = jnp.einsum("pjx,p->jx", squares, beta) * area[:, None]
    gradient = lax.psum_scatter(grad_terms, "probe", scatter_dimension=1, tiled=True)
    return (matvec, gradient)


def dot(a, b, dims=((1,), (0,))):
    return lax.dot_general(a, b, (dims, ((), ())), preferred_element_type=jnp.float32)


def split(x):
    upper = x.astype(jnp.bfloat16)
    return upper, (x - upper.astype(jnp.float32)).astype(jnp.bfloat16)


LANES = 128


def every(slot, count):
    return pl.ds(slot, count, stride=GROUP)


def tiles(ref):
    return range(ref.shape[0])


def put(ref, rows, value):
    for t in tiles(ref):
        ref[t, rows, :] = value[:, t * LANES : (t + 1) * LANES]


def take(ref, rows):
    return jnp.concatenate([ref[t, rows, :] for t in tiles(ref)], axis=-1)


def spread_rows(tbl_ref, wide):
    @pl.loop(0, tbl_ref.shape[0] * 2 // DEPTH)
    def _(step):
        some = pl.ds(step * (DEPTH // 2), DEPTH // 2)
        for t in tiles(wide):
            piece = tbl_ref[some, :, :, t * LANES : (t + 1) * LANES].astype(jnp.float32)
            wide[t, pl.ds(step * (DEPTH * GROUP), DEPTH * GROUP)] = piece.reshape(
                DEPTH * GROUP, LANES
            )


def visit(orders_ref, group, turn, pair, steps):
    first = orders_ref[group * GROUP + 2 * pair] // DEPTH
    mine = turn < steps - first
    slot = 2 * pair + jnp.where(mine, 0, 1)
    return slot, jnp.where(mine, first + turn, turn - 1)


def even_degree(shape):
    return lax.broadcasted_iota(jnp.int32, shape, 1) % 2 == 0


def synth_kernel(orders_ref, x_ref, root_ref, tbl_ref, sign_ref, out_ref, xs, wide, acc, ns, ss):
    group = pl.program_id(0)
    chunk = x_ref.shape[0]
    cycles = out_ref.shape[3] // chunk
    half = out_ref.shape[0] // 2
    rows = chunk * 2
    scaled = (x_ref[...].astype(jnp.float32) * root_ref[...]).astype(jnp.bfloat16)
    put(xs, slice(None), scaled.astype(jnp.float32).reshape(rows * GROUP, scaled.shape[-1]))
    acc[...] = jnp.zeros_like(acc)

    spread_rows(tbl_ref, wide)
    steps = tbl_ref.shape[0] * 2 // DEPTH

    @pl.loop(0, steps + 1)
    def _(turn):
        for pair in range(GROUP // 2):
            slot, step = visit(orders_ref, group, turn, pair, steps)
            x = xs[step, every(slot, rows), :]
            even = even_degree(x.shape)
            x = jnp.concatenate([jnp.where(even, x, 0.0), jnp.where(even, 0.0, x)], axis=0)
            table = take(wide, every(step * (DEPTH * GROUP) + slot, DEPTH)).astype(jnp.bfloat16)
            acc[slot] += dot(x.astype(jnp.bfloat16), table)

    for slot in range(GROUP):
        even, odd = acc[slot, :rows], acc[slot, rows:]
        put(ns, every(slot, rows), even + odd)
        put(ss, every(slot, rows), even - odd)
    for c in range(2):
        north, south = [], []
        for p in range(chunk):
            place = pl.ds((2 * p + c) * GROUP, GROUP)
            north.append(take(ns, place))
            south.append(take(ss, place) * sign_ref[...])
        for d in range(half):
            for source, place in ((north, d), (south, 2 * half - 1 - d)):
                pieces = [piece[:, d * cycles : (d + 1) * cycles] for piece in source]
                out_ref[place, c] = jnp.concatenate(pieces, axis=-1).astype(jnp.bfloat16)


def analysis_kernel(*refs):
    orders_ref, q_ref, root_ref, tbl_ref, sign_ref = refs[:5]
    out_ref, plus, minus, wide, held, outs = refs[-6:]
    group = pl.program_id(0)
    chunk = out_ref.shape[0]
    cycles = q_ref.shape[3] // chunk
    half = q_ref.shape[0] // 2
    rows = chunk * 2

    for c in range(2):
        blocks = [q_ref[d, c].astype(jnp.float32) for d in range(2 * half)]
        for p in range(chunk):
            cut = slice(p * cycles, (p + 1) * cycles)
            north = jnp.concatenate([blocks[d][:, cut] for d in range(half)], axis=-1)
            other = [blocks[2 * half - 1 - d][:, cut] for d in range(half)]
            south = jnp.concatenate(other, axis=-1) * sign_ref[...]
            place = pl.ds((2 * p + c) * GROUP, GROUP)
            put(plus, place, north + south)
            put(minus, place, north - south)
    for slot in range(GROUP):
        both = [take(ref, every(slot, rows)) for ref in (plus, minus)]
        upper, lower = split(jnp.concatenate(both, axis=0))
        held[slot, : 2 * rows] = upper
        held[slot, 2 * rows :] = lower
    outs[...] = jnp.zeros_like(outs)

    spread_rows(tbl_ref, wide)
    steps = tbl_ref.shape[0] * 2 // DEPTH

    @pl.loop(0, steps + 1)
    def _(turn):
        for pair in range(GROUP // 2):
            slot, step = visit(orders_ref, group, turn, pair, steps)
            now = pl.ds(pl.multiple_of(step * DEPTH, DEPTH), DEPTH)
            table = take(wide, every(step * (DEPTH * GROUP) + slot, DEPTH)).astype(jnp.bfloat16)
            both = dot(held[slot], table, ((1,), (1,)))
            both = both[: 2 * rows] + both[2 * rows :]
            even = even_degree((rows, DEPTH))
            chosen = jnp.where(even, both[:rows], both[rows:])
            outs[step, every(slot, rows), :] = chosen * root_ref[:, now]

    for t in tiles(outs):
        cut = slice(t * LANES, (t + 1) * LANES)
        out_ref[:, :, :, cut] = outs[t].reshape(chunk, 2, GROUP, LANES)


def fourier_kernel(*refs, first):
    r_ref, ahead_cos, ahead_sin, back_cos, back_sin, w_low, w_high, turn_ref, beta_ref = refs[:9]
    out_ref, g_low, g_high, rc, rs, acc_c, acc_s, middle = refs[-8:]
    old_low, old_high = (None, None) if first else refs[9:11]
    step, part = pl.program_id(0), pl.program_id(1)
    sources, _, slots, _ = r_ref.shape
    tile, lanes = g_low.shape
    count = acc_c.shape[1]
    mine = pl.ds(pl.multiple_of(part * lanes, LANES), lanes)

    @pl.when(step == 0)
    def _():
        for pair in range(sources // 2):
            for c, place in ((0, rc), (1, rs)):
                both = [r_ref[2 * pair + i, c, :, mine].astype(jnp.float32) for i in range(2)]
                place[part, pl.ds(2 * slots * pair, 2 * slots)] = jnp.concatenate(
                    both, axis=0
                ).astype(jnp.bfloat16)
        turned = turn_ref[...] * rc[part].astype(jnp.float32)
        mid = jnp.sum(turned, axis=0, keepdims=True)
        middle[part] = mid
        w_mid = (w_high[pl.ds(0, 1), :] * mid).astype(jnp.bfloat16).astype(jnp.float32)
        acc_c[part] = turn_ref[...] * w_mid
        acc_s[part] = jnp.zeros_like(acc_s[part])

    c_part = dot(ahead_cos[0], rc[part])
    c_part = c_part[:tile] + c_part[tile:]
    s_part = dot(ahead_sin[0], rs[part])
    s_part = s_part[:tile] + s_part[tile:]
    low = c_part + s_part
    row = lax.broadcasted_iota(jnp.int32, low.shape, 0) + step * tile
    high = jnp.where(row == 0, middle[part], c_part - s_part)
    beta = beta_ref[:, mine]
    low_sq = beta * (low * low)
    high_sq = beta * (high * high)

    @pl.when(part == 0)
    def _():
        g_low[...] = low_sq if first else old_low[...] + low_sq
        g_high[...] = high_sq if first else old_high[...] + high_sq

    @pl.when(part > 0)
    def _():
        g_low[...] += low_sq
        g_high[...] += high_sq

    low = (w_low[...] * low).astype(jnp.bfloat16).astype(jnp.float32)
    high = jnp.where(row == 0, 0.0, w_high[...] * high).astype(jnp.bfloat16).astype(jnp.float32)
    for folded, back, acc in ((low + high, back_cos, acc_c), (low - high, back_sin, acc_s)):
        upper, lower = split(folded)
        both = dot(back[...], upper)
        acc[part] += both[:count] + both[count:] + dot(back[pl.ds(0, count), :], lower)

    @pl.when(step == pl.num_programs(0) - 1)
    def _():
        for d in range(sources):
            for c, acc in ((0, acc_c), (1, acc_s)):
                out_ref[d, c, :, mine] = acc[part, pl.ds(slots * d, slots)].astype(jnp.bfloat16)


def half_tables(orders, lon_count):
    half = lon_count // 2

    def trig(points):
        idx = orders[:, None] * points[None, :] % lon_count
        angle = idx.astype(jnp.float32) * (2.0 * math.pi / lon_count)
        return lax.optimization_barrier((jnp.cos(angle), jnp.sin(angle)))

    def joined(parts, fine, shape, axes):
        (ca, sa), (cb, sb) = parts
        ca, sa = (t[axes[0]] for t in (ca, sa))
        cb, sb = (t[axes[1]] for t in (cb, sb))
        cosine = (ca * cb - sa * sb).reshape(shape)
        sine = (sa * cb + ca * sb).reshape(shape)
        return split(cosine) + split(sine)

    count = orders.shape[0]
    fine = 128
    coarse_points = jnp.arange(half // fine, dtype=jnp.int32) * fine
    fine_points = jnp.arange(fine, dtype=jnp.int32)
    coarse, small = trig(coarse_points), trig(fine_points)
    every = slice(None)
    back = joined(
        (coarse, small), fine, (count, half), ((every, every, None), (every, None, every))
    )
    coarse_t = tuple(t.T for t in coarse)
    small_t = tuple(t.T for t in small)
    ahead = joined(
        (coarse_t, small_t), fine, (half, count), ((every, None, every), (None, every, every))
    )
    tiled = [t.reshape(half // TILE, TILE, count) for t in ahead]
    ahead = [jnp.concatenate(tiled[i : i + 2], axis=1) for i in (0, 2)]
    back = [jnp.concatenate(back[i : i + 2], axis=0) for i in (0, 2)]
    return ahead, back


def fast_body(probes_in, root_spectrum, order_slots, legendre, weight, beta):
    axes = ("lat", "blk")
    groups = lax.axis_size(axes)
    my_index = lax.axis_index(axes)
    cycles, lon_count = weight.shape
    half_lon = lon_count // 2
    all_cycles = cycles * groups
    half_cycles = all_cycles // 2
    degrees, slots = legendre.shape[:2]
    orders_count = order_slots.shape[0]
    probes = probes_in.shape[0]
    chunks = probes // CHUNK
    lanes = CHUNK * cycles
    part_lanes = PART * cycles
    parts = CHUNK // PART
    south = my_index >= groups // 2
    params = functools.partial(pltpu.CompilerParams, vmem_limit_bytes=VMEM_LIMIT)
    f32, bf16 = jnp.float32, jnp.bfloat16

    my_orders = lax.dynamic_slice_in_dim(order_slots, my_index * slots, slots)
    sign = (1 - 2 * (my_orders % 2)).astype(f32)
    sign = jnp.broadcast_to(sign[:, None], (slots, half_cycles))
    root = root_spectrum[None, :]
    table = legendre.reshape(degrees // 2, 2, slots, all_cycles)
    rows = CHUNK * 2
    whole = lambda shape: pl.BlockSpec(shape, lambda *_: (0,) * len(shape))
    table_spec = pl.BlockSpec((degrees // 2, 2, GROUP, half_cycles), lambda g, o: (0, 0, g, 0))
    sign_spec = pl.BlockSpec((GROUP, half_cycles), lambda g, o: (g, 0))
    payload_spec = pl.BlockSpec((groups, 2, GROUP, lanes), lambda g, o: (0, 0, g, 0))
    payload = jax.ShapeDtypeStruct((groups, 2, slots, lanes), bf16)
    table_bytes = degrees * slots * half_cycles * 2
    legendre_cost = pl.CostEstimate(
        flops=1000 * table_bytes, bytes_accessed=table_bytes, transcendentals=0
    )
    tiled = lambda width, height: pltpu.VMEM((width // LANES, height, LANES), f32)
    degree_tiles = tiled(degrees, rows * GROUP)
    cycle_tiles = tiled(half_cycles, rows * GROUP)
    wide = tiled(half_cycles, degrees * GROUP)

    def chunk_spec(q):
        return pl.BlockSpec((CHUNK, 2, GROUP, degrees), lambda g, o: (q, 0, g, 0))

    def synth(q):
        return pl.pallas_call(
            synth_kernel,
            name="synth",
            grid_spec=pltpu.PrefetchScalarGridSpec(
                num_scalar_prefetch=1,
                grid=(slots // GROUP,),
                in_specs=[chunk_spec(q), whole(root.shape), table_spec, sign_spec],
                out_specs=payload_spec,
                scratch_shapes=[
                    degree_tiles,
                    wide,
                    pltpu.VMEM((GROUP, 2 * rows, half_cycles), f32),
                    cycle_tiles,
                    cycle_tiles,
                ],
            ),
            out_shape=payload,
            compiler_params=params(),
            cost_estimate=legendre_cost,
        )(my_orders, probes_in, root, table, sign)

    def analyse(q, returned, held):
        first = held is None
        return pl.pallas_call(
            analysis_kernel,
            name="analyse",
            grid_spec=pltpu.PrefetchScalarGridSpec(
                num_scalar_prefetch=1,
                grid=(slots // GROUP,),
                in_specs=[payload_spec, whole(root.shape), table_spec, sign_spec]
                + ([] if first else [pl.BlockSpec(memory_space=pl.ANY)]),
                out_specs=chunk_spec(q),
                scratch_shapes=[
                    cycle_tiles,
                    cycle_tiles,
                    wide,
                    pltpu.VMEM((GROUP, 4 * rows, half_cycles), bf16),
                    degree_tiles,
                ],
            ),
            out_shape=jax.ShapeDtypeStruct((probes, 2, slots, degrees), f32),
            input_output_aliases={} if first else {5: 0},
            compiler_params=params(),
            cost_estimate=legendre_cost,
        )(my_orders, returned, root, table, sign, *([] if first else [held]))

    ahead_spec = pl.BlockSpec((1, 2 * TILE, orders_count), lambda i, h: (i, 0, 0))
    back_spec = pl.BlockSpec((2 * orders_count, TILE), lambda i, h: (0, i))
    grid_spec = pl.BlockSpec((TILE, part_lanes), lambda i, h: (i, 0))

    def fourier(received, tables, w_low, w_high, turn, chunk_beta, old):
        first = old is None
        ahead, back = tables
        square = jax.ShapeDtypeStruct((half_lon, part_lanes), f32)
        return pl.pallas_call(
            functools.partial(fourier_kernel, first=first),
            name="fourier",
            grid=(half_lon // TILE, parts),
            in_specs=[whole(payload.shape)]
            + [ahead_spec] * 2
            + [back_spec] * 2
            + [grid_spec] * 2
            + [whole((orders_count, 1)), whole((1, lanes))]
            + ([] if first else [grid_spec] * 2),
            out_specs=[whole(payload.shape), grid_spec, grid_spec],
            out_shape=[payload, square, square],
            scratch_shapes=[pltpu.VMEM((parts, orders_count, part_lanes), bf16)] * 2
            + [pltpu.VMEM((parts, orders_count, part_lanes), f32)] * 2
            + [pltpu.VMEM((parts, 1, part_lanes), f32)],
            input_output_aliases={} if first else {9: 1, 10: 2},
            compiler_params=params(),
            cost_estimate=pl.CostEstimate(
                flops=40 * half_lon * lanes * orders_count,
                bytes_accessed=16 * half_lon * orders_count + 16 * half_lon * part_lanes,
                transcendentals=0,
            ),
        )(received, *ahead, *back, w_low, w_high, turn, chunk_beta, *([] if first else old))

    def exchange(x):
        return lax.all_to_all(x, axes, split_axis=0, concat_axis=0, tiled=True)

    local = jnp.arange(cycles, dtype=jnp.int32)
    flipped = jnp.where(south, cycles - 1 - local, local)
    cycle_index = (my_index * cycles + flipped).astype(f32)
    area = 2.0 * math.pi / lon_count * (math.pi / all_cycles) * jnp.sin(
        math.pi * (cycle_index + 0.5) / all_cycles
    )
    turned = jnp.where(south, jnp.flip(weight, 0), weight)
    turned = (area[:, None] * turned).T
    w_low = jnp.tile(turned[:half_lon], (1, PART))
    w_high = jnp.concatenate(
        [turned[half_lon : half_lon + 1], jnp.flip(turned[half_lon + 1 :], 0)], axis=0
    )
    w_high = jnp.tile(w_high, (1, PART))
    turn = (1 - 2 * (order_slots % 2)).astype(f32)[:, None]
    tables = half_tables(order_slots, lon_count)

    received = [exchange(synth(q)) for q in range(chunks)]
    old, held = None, None
    returned = []
    for q in range(chunks):
        chunk_beta = jnp.repeat(beta[q * CHUNK : (q + 1) * CHUNK], cycles)[None, :]
        analysed, low, high = fourier(received[q], tables, w_low, w_high, turn, chunk_beta, old)
        old = (low, high)
        returned.append(exchange(analysed))
    for q in range(chunks):
        held = analyse(q, returned[q], held)

    lane_cycle = jnp.arange(part_lanes, dtype=jnp.int32) % cycles
    pick = (lane_cycle[None, :] == flipped[:, None]).astype(f32)
    sums = [
        lax.dot_general(
            pick, s, (((1,), (1,)), ((), ())), precision=lax.Precision.HIGHEST,
            preferred_element_type=f32,
        )
        for s in old
    ]
    natural = 2.0 * math.pi / lon_count * (math.pi / all_cycles) * jnp.sin(
        math.pi * ((my_index * cycles + local).astype(f32) + 0.5) / all_cycles
    )
    if lax.axis_size("probe") == 2:
        ahead_half = lax.axis_index("probe") == 0
        keep = jnp.where(ahead_half, sums[0], sums[1])
        give = jnp.where(ahead_half, sums[1], sums[0])
        half = (keep + lax.ppermute(give, "probe", [(0, 1), (1, 0)])) * natural[:, None]
        mirrored = jnp.concatenate([half[:, :1], jnp.flip(half[:, 1:], 1)], axis=1)
        gradient = jnp.where(ahead_half, half, mirrored)
    else:
        terms = jnp.concatenate([sums[0], sums[1][:, :1], jnp.flip(sums[1][:, 1:], 1)], axis=1)
        gradient = lax.psum_scatter(
            terms * natural[:, None], "probe", scatter_dimension=1, tiled=True
        )
    return (held, gradient)


def body(probes_in, root_spectrum, order_slots, legendre, weight, beta):
    degrees, slots, all_cycles = legendre.shape
    fits = (
        slots % GROUP == 0
        and degrees % DEPTH == 0
        and degrees == order_slots.shape[0]
        and all_cycles % (2 * LANES) == 0
        and (PART * weight.shape[0]) % LANES == 0
        and probes_in.shape[0] % CHUNK == 0
        and weight.shape[1] % (2 * TILE) == 0
        and lax.axis_size(("lat", "blk")) % 2 == 0
    )
    chosen = fast_body if fits else plain_body
    return chosen(probes_in, root_spectrum, order_slots, legendre, weight, beta)


def solution(mesh):
    return jax.shard_map(
        body,
        mesh=mesh,
        in_specs=(
            P("probe", None, ("lat", "blk"), None),
            P(),
            P(),
            P(None, ("lat", "blk"), None),
            P(("lat", "blk"), None),
            P("probe"),
        ),
        out_specs=(P("probe", None, ("lat", "blk"), None), P(("lat", "blk"), "probe")),
        check_vma=False,
    )
```

```python
import functools
import math

import jax
import jax.numpy as jnp
from jax import lax
from jax.experimental import pallas as pl
from jax.experimental.pallas import tpu as pltpu
from jax.sharding import PartitionSpec as P

GROUP = 8
DEPTH = 128
CHUNK = 16
PART = 8
TILE = 256
VMEM_LIMIT = 60 * 2**20


def fourier_tables(orders, lon_count):
    longitude = jnp.arange(lon_count, dtype=jnp.int32)
    phase_idx = orders[:, None] * longitude[None, :] % lon_count
    angle = phase_idx.astype(jnp.float32) * (2.0 * math.pi / lon_count)
    twiddle = jnp.stack([jnp.cos(angle), jnp.sin(angle)])
    upper = twiddle.astype(jnp.bfloat16)
    lower = (twiddle - upper.astype(jnp.float32)).astype(jnp.bfloat16)
    return (upper, lower)


def cycle_work(spectra, inverse_tables, forward_tables, area, weight):
    grid_field = jnp.einsum(
        "pcmj,cmx->pjx", spectra, inverse_tables[0], preferred_element_type=jnp.float32
    )
    grid_field = grid_field + jnp.einsum(
        "pcmj,cmx->pjx", spectra, inverse_tables[1], preferred_element_type=jnp.float32
    )
    squares = grid_field * grid_field
    weighted = (area[None, :, None] * weight[None] * grid_field).astype(jnp.bfloat16)
    analysed = jnp.einsum(
        "pjx,cmx->pcmj", weighted, forward_tables[0], preferred_element_type=jnp.float32
    )
    analysed = analysed + jnp.einsum(
        "pjx,cmx->pcmj", weighted, forward_tables[1], preferred_element_type=jnp.float32
    )
    return (squares, analysed.astype(jnp.bfloat16))


def plain_body(probes_in, root_spectrum, order_slots, legendre, weight, beta):
    groups = lax.axis_size(("lat", "blk"))
    my_index = lax.axis_index(("lat", "blk"))
    cycle_count = weight.shape[0]
    lon_count = weight.shape[1]
    all_cycles = cycle_count * groups
    scaled = (probes_in.astype(jnp.float32) * root_spectrum).astype(jnp.bfloat16)
    spectra = jnp.einsum(
        "pcml,lmj->pcmj", scaled, legendre, preferred_element_type=jnp.float32
    ).astype(jnp.bfloat16)
    cycle_index = (my_index * cycle_count + jnp.arange(cycle_count, dtype=jnp.int32)).astype(
        jnp.float32
    )
    local_sines = jnp.sin(math.pi * (cycle_index + 0.5) / all_cycles)
    area = 2.0 * math.pi / lon_count * (math.pi / all_cycles) * local_sines
    forward_tables = fourier_tables(order_slots, lon_count)
    squares, analysed = cycle_work(
        lax.all_to_all(spectra, ("lat", "blk"), split_axis=3, concat_axis=2, tiled=True),
        forward_tables,
        forward_tables,
        area,
        weight,
    )
    returned = lax.all_to_all(analysed, ("lat", "blk"), split_axis=2, concat_axis=3, tiled=True)
    matvec = (
        jnp.einsum("pcmj,lmj->pcml", returned, legendre, preferred_element_type=jnp.float32)
        * root_spectrum
    )
    grad_terms = jnp.einsum("pjx,p->jx", squares, beta) * area[:, None]
    gradient = lax.psum_scatter(grad_terms, "probe", scatter_dimension=1, tiled=True)
    return (matvec, gradient)


def dot(a, b, dims=((1,), (0,))):
    return lax.dot_general(a, b, (dims, ((), ())), preferred_element_type=jnp.float32)


def split(x):
    upper = x.astype(jnp.bfloat16)
    return upper, (x - upper.astype(jnp.float32)).astype(jnp.bfloat16)


LANES = 128
PITCH = GROUP + 1


def every(slot, count):
    return pl.ds(slot, count, stride=PITCH)


def tiles(ref):
    return range(ref.shape[0])


def put(ref, rows, value):
    for t in tiles(ref):
        ref[t, rows, :] = value[:, t * LANES : (t + 1) * LANES]


def take(ref, rows):
    return jnp.concatenate([ref[t, rows, :] for t in tiles(ref)], axis=-1)


def spread_rows(tbl_ref, wide):
    @pl.loop(0, tbl_ref.shape[0] * 2 // DEPTH)
    def _(step):
        some = pl.ds(step * (DEPTH // 2), DEPTH // 2)
        for t in tiles(wide):
            piece = tbl_ref[some, :, :, t * LANES : (t + 1) * LANES].astype(jnp.float32)
            piece = piece.reshape(DEPTH, GROUP, LANES)
            for i in range(DEPTH):
                wide[t, pl.ds(step * (DEPTH * PITCH) + i * PITCH, GROUP), :] = piece[i]


def table_block(wide, step, slot):
    rows = pl.ds(step * (DEPTH * PITCH) + slot, DEPTH, stride=PITCH)
    return take(wide, rows).astype(jnp.bfloat16)


def visit(orders_ref, group, turn, pair, steps):
    first = orders_ref[group * GROUP + 2 * pair] // DEPTH
    mine = turn < steps - first
    slot = 2 * pair + jnp.where(mine, 0, 1)
    return slot, jnp.where(mine, first + turn, turn - 1)


def even_degree(shape):
    return lax.broadcasted_iota(jnp.int32, shape, 1) % 2 == 0


def synth_kernel(orders_ref, x_ref, root_ref, tbl_ref, sign_ref, out_ref, xs, wide, acc, ns, ss):
    group = pl.program_id(0)
    chunk = x_ref.shape[0]
    cycles = out_ref.shape[3] // chunk
    half = out_ref.shape[0] // 2
    rows = chunk * 2
    scaled = (x_ref[...].astype(jnp.float32) * root_ref[...]).astype(jnp.bfloat16)
    scaled = scaled.astype(jnp.float32).reshape(rows, GROUP, scaled.shape[-1])
    for i in range(rows):
        put(xs, pl.ds(i * PITCH, GROUP), scaled[i])
    acc[...] = jnp.zeros_like(acc)

    spread_rows(tbl_ref, wide)
    steps = tbl_ref.shape[0] * 2 // DEPTH

    @pl.loop(0, steps + 1)
    def _(turn):
        for pair in range(GROUP // 2):
            slot, step = visit(orders_ref, group, turn, pair, steps)
            x = xs[step, every(slot, rows), :]
            even = even_degree(x.shape)
            x = jnp.concatenate([jnp.where(even, x, 0.0), jnp.where(even, 0.0, x)], axis=0)
            table = table_block(wide, step, slot)
            acc[slot] += dot(x.astype(jnp.bfloat16), table)

    for slot in range(GROUP):
        even, odd = acc[slot, :rows], acc[slot, rows:]
        put(ns, every(slot, rows), even + odd)
        put(ss, every(slot, rows), even - odd)
    for c in range(2):
        north, south = [], []
        for p in range(chunk):
            place = pl.ds((2 * p + c) * PITCH, GROUP)
            north.append(take(ns, place))
            south.append(take(ss, place) * sign_ref[...])
        for d in range(half):
            for source, place in ((north, d), (south, 2 * half - 1 - d)):
                pieces = [piece[:, d * cycles : (d + 1) * cycles] for piece in source]
                out_ref[place, c] = jnp.concatenate(pieces, axis=-1).astype(jnp.bfloat16)


def analysis_kernel(*refs):
    orders_ref, q_ref, root_ref, tbl_ref, sign_ref = refs[:5]
    out_ref, plus, minus, wide, held, outs = refs[-6:]
    group = pl.program_id(0)
    chunk = out_ref.shape[0]
    cycles = q_ref.shape[3] // chunk
    half = q_ref.shape[0] // 2
    rows = chunk * 2

    for c in range(2):
        blocks = [q_ref[d, c].astype(jnp.float32) for d in range(2 * half)]
        for p in range(chunk):
            cut = slice(p * cycles, (p + 1) * cycles)
            north = jnp.concatenate([blocks[d][:, cut] for d in range(half)], axis=-1)
            other = [blocks[2 * half - 1 - d][:, cut] for d in range(half)]
            south = jnp.concatenate(other, axis=-1) * sign_ref[...]
            place = pl.ds((2 * p + c) * PITCH, GROUP)
            put(plus, place, north + south)
            put(minus, place, north - south)
    for slot in range(GROUP):
        both = [take(ref, every(slot, rows)) for ref in (plus, minus)]
        upper, lower = split(jnp.concatenate(both, axis=0))
        held[slot, : 2 * rows] = upper
        held[slot, 2 * rows :] = lower
    outs[...] = jnp.zeros_like(outs)

    spread_rows(tbl_ref, wide)
    steps = tbl_ref.shape[0] * 2 // DEPTH

    @pl.loop(0, steps + 1)
    def _(turn):
        for pair in range(GROUP // 2):
            slot, step = visit(orders_ref, group, turn, pair, steps)
            now = pl.ds(pl.multiple_of(step * DEPTH, DEPTH), DEPTH)
            table = table_block(wide, step, slot)
            both = dot(held[slot], table, ((1,), (1,)))
            both = both[: 2 * rows] + both[2 * rows :]
            even = even_degree((rows, DEPTH))
            chosen = jnp.where(even, both[:rows], both[rows:])
            outs[step, every(slot, rows), :] = chosen * root_ref[:, now]

    for p in range(chunk):
        for c in range(2):
            out_ref[p, c] = take(outs, pl.ds((2 * p + c) * PITCH, GROUP))


def fourier_kernel(*refs, first):
    r_ref, ahead_cos, ahead_sin, back_cos, back_sin, w_low, w_high, turn_ref, beta_ref = refs[:9]
    out_ref, g_low, g_high, rc, rs, acc_c, acc_s, middle = refs[-8:]
    old_low, old_high = (None, None) if first else refs[9:11]
    step, part = pl.program_id(0), pl.program_id(1)
    sources, _, slots, _ = r_ref.shape
    tile, lanes = g_low.shape
    count = acc_c.shape[1]
    mine = pl.ds(pl.multiple_of(part * lanes, LANES), lanes)

    @pl.when(step == 0)
    def _():
        for pair in range(sources // 2):
            for c, place in ((0, rc), (1, rs)):
                both = [r_ref[2 * pair + i, c, :, mine].astype(jnp.float32) for i in range(2)]
                place[part, pl.ds(2 * slots * pair, 2 * slots)] = jnp.concatenate(
                    both, axis=0
                ).astype(jnp.bfloat16)
        turned = turn_ref[...] * rc[part].astype(jnp.float32)
        mid = jnp.sum(turned, axis=0, keepdims=True)
        middle[part] = mid
        w_mid = (w_high[pl.ds(0, 1), :] * mid).astype(jnp.bfloat16).astype(jnp.float32)
        acc_c[part] = turn_ref[...] * w_mid
        acc_s[part] = jnp.zeros_like(acc_s[part])

    c_part = dot(ahead_cos[0], rc[part])
    c_part = c_part[:tile] + c_part[tile:]
    s_part = dot(ahead_sin[0], rs[part])
    s_part = s_part[:tile] + s_part[tile:]
    low = c_part + s_part
    row = lax.broadcasted_iota(jnp.int32, low.shape, 0) + step * tile
    high = jnp.where(row == 0, middle[part], c_part - s_part)
    beta = beta_ref[:, mine]
    low_sq = beta * (low * low)
    high_sq = beta * (high * high)

    @pl.when(part == 0)
    def _():
        g_low[...] = low_sq if first else old_low[...] + low_sq
        g_high[...] = high_sq if first else old_high[...] + high_sq

    @pl.when(part > 0)
    def _():
        g_low[...] += low_sq
        g_high[...] += high_sq

    low = (w_low[...] * low).astype(jnp.bfloat16).astype(jnp.float32)
    high = jnp.where(row == 0, 0.0, w_high[...] * high).astype(jnp.bfloat16).astype(jnp.float32)
    for folded, back, acc in ((low + high, back_cos, acc_c), (low - high, back_sin, acc_s)):
        upper, lower = split(folded)
        both = dot(back[...], upper)
        acc[part] += both[:count] + both[count:] + dot(back[pl.ds(0, count), :], lower)

    @pl.when(step == pl.num_programs(0) - 1)
    def _():
        for d in range(sources):
            for c, acc in ((0, acc_c), (1, acc_s)):
                out_ref[d, c, :, mine] = acc[part, pl.ds(slots * d, slots)].astype(jnp.bfloat16)


def half_tables(orders, lon_count):
    half = lon_count // 2

    def trig(points):
        idx = orders[:, None] * points[None, :] % lon_count
        angle = idx.astype(jnp.float32) * (2.0 * math.pi / lon_count)
        return lax.optimization_barrier((jnp.cos(angle), jnp.sin(angle)))

    def joined(parts, fine, shape, axes):
        (ca, sa), (cb, sb) = parts
        ca, sa = (t[axes[0]] for t in (ca, sa))
        cb, sb = (t[axes[1]] for t in (cb, sb))
        cosine = (ca * cb - sa * sb).reshape(shape)
        sine = (sa * cb + ca * sb).reshape(shape)
        return split(cosine) + split(sine)

    count = orders.shape[0]
    fine = 128
    coarse_points = jnp.arange(half // fine, dtype=jnp.int32) * fine
    fine_points = jnp.arange(fine, dtype=jnp.int32)
    coarse, small = trig(coarse_points), trig(fine_points)
    every = slice(None)
    back = joined(
        (coarse, small), fine, (count, half), ((every, every, None), (every, None, every))
    )
    coarse_t = tuple(t.T for t in coarse)
    small_t = tuple(t.T for t in small)
    ahead = joined(
        (coarse_t, small_t), fine, (half, count), ((every, None, every), (None, every, every))
    )
    tiled = [t.reshape(half // TILE, TILE, count) for t in ahead]
    ahead = [jnp.concatenate(tiled[i : i + 2], axis=1) for i in (0, 2)]
    back = [jnp.concatenate(back[i : i + 2], axis=0) for i in (0, 2)]
    return ahead, back


def fast_body(probes_in, root_spectrum, order_slots, legendre, weight, beta):
    axes = ("lat", "blk")
    groups = lax.axis_size(axes)
    my_index = lax.axis_index(axes)
    cycles, lon_count = weight.shape
    half_lon = lon_count // 2
    all_cycles = cycles * groups
    half_cycles = all_cycles // 2
    degrees, slots = legendre.shape[:2]
    orders_count = order_slots.shape[0]
    probes = probes_in.shape[0]
    chunks = probes // CHUNK
    lanes = CHUNK * cycles
    part_lanes = PART * cycles
    parts = CHUNK // PART
    south = my_index >= groups // 2
    params = functools.partial(pltpu.CompilerParams, vmem_limit_bytes=VMEM_LIMIT)
    f32, bf16 = jnp.float32, jnp.bfloat16

    my_orders = lax.dynamic_slice_in_dim(order_slots, my_index * slots, slots)
    sign = (1 - 2 * (my_orders % 2)).astype(f32)
    sign = jnp.broadcast_to(sign[:, None], (slots, half_cycles))
    root = root_spectrum[None, :]
    table = legendre.reshape(degrees // 2, 2, slots, all_cycles)
    rows = CHUNK * 2
    whole = lambda shape: pl.BlockSpec(shape, lambda *_: (0,) * len(shape))
    table_spec = pl.BlockSpec((degrees // 2, 2, GROUP, half_cycles), lambda g, o: (0, 0, g, 0))
    sign_spec = pl.BlockSpec((GROUP, half_cycles), lambda g, o: (g, 0))
    payload_spec = pl.BlockSpec((groups, 2, GROUP, lanes), lambda g, o: (0, 0, g, 0))
    payload = jax.ShapeDtypeStruct((groups, 2, slots, lanes), bf16)
    table_bytes = degrees * slots * half_cycles * 2
    legendre_cost = pl.CostEstimate(
        flops=1000 * table_bytes, bytes_accessed=table_bytes, transcendentals=0
    )
    tiled = lambda width, height: pltpu.VMEM((width // LANES, height, LANES), f32)
    degree_tiles = tiled(degrees, rows * PITCH)
    cycle_tiles = tiled(half_cycles, rows * PITCH)
    wide = tiled(half_cycles, degrees * PITCH)

    def chunk_spec(q):
        return pl.BlockSpec((CHUNK, 2, GROUP, degrees), lambda g, o: (q, 0, g, 0))

    def synth(q):
        return pl.pallas_call(
            synth_kernel,
            name="synth",
            grid_spec=pltpu.PrefetchScalarGridSpec(
                num_scalar_prefetch=1,
                grid=(slots // GROUP,),
                in_specs=[chunk_spec(q), whole(root.shape), table_spec, sign_spec],
                out_specs=payload_spec,
                scratch_shapes=[
                    degree_tiles,
                    wide,
                    pltpu.VMEM((GROUP, 2 * rows, half_cycles), f32),
                    cycle_tiles,
                    cycle_tiles,
                ],
            ),
            out_shape=payload,
            compiler_params=params(),
            cost_estimate=legendre_cost,
        )(my_orders, probes_in, root, table, sign)

    def analyse(q, returned, held):
        first = held is None
        return pl.pallas_call(
            analysis_kernel,
            name="analyse",
            grid_spec=pltpu.PrefetchScalarGridSpec(
                num_scalar_prefetch=1,
                grid=(slots // GROUP,),
                in_specs=[payload_spec, whole(root.shape), table_spec, sign_spec]
                + ([] if first else [pl.BlockSpec(memory_space=pl.ANY)]),
                out_specs=chunk_spec(q),
                scratch_shapes=[
                    cycle_tiles,
                    cycle_tiles,
                    wide,
                    pltpu.VMEM((GROUP, 4 * rows, half_cycles), bf16),
                    degree_tiles,
                ],
            ),
            out_shape=jax.ShapeDtypeStruct((probes, 2, slots, degrees), f32),
            input_output_aliases={} if first else {5: 0},
            compiler_params=params(),
            cost_estimate=legendre_cost,
        )(my_orders, returned, root, table, sign, *([] if first else [held]))

    ahead_spec = pl.BlockSpec((1, 2 * TILE, orders_count), lambda i, h: (i, 0, 0))
    back_spec = pl.BlockSpec((2 * orders_count, TILE), lambda i, h: (0, i))
    grid_spec = pl.BlockSpec((TILE, part_lanes), lambda i, h: (i, 0))

    def fourier(received, tables, w_low, w_high, turn, chunk_beta, old):
        first = old is None
        ahead, back = tables
        square = jax.ShapeDtypeStruct((half_lon, part_lanes), f32)
        return pl.pallas_call(
            functools.partial(fourier_kernel, first=first),
            name="fourier",
            grid=(half_lon // TILE, parts),
            in_specs=[whole(payload.shape)]
            + [ahead_spec] * 2
            + [back_spec] * 2
            + [grid_spec] * 2
            + [whole((orders_count, 1)), whole((1, lanes))]
            + ([] if first else [grid_spec] * 2),
            out_specs=[whole(payload.shape), grid_spec, grid_spec],
            out_shape=[payload, square, square],
            scratch_shapes=[pltpu.VMEM((parts, orders_count, part_lanes), bf16)] * 2
            + [pltpu.VMEM((parts, orders_count, part_lanes), f32)] * 2
            + [pltpu.VMEM((parts, 1, part_lanes), f32)],
            input_output_aliases={} if first else {9: 1, 10: 2},
            compiler_params=params(),
            cost_estimate=pl.CostEstimate(
                flops=40 * half_lon * lanes * orders_count,
                bytes_accessed=16 * half_lon * orders_count + 16 * half_lon * part_lanes,
                transcendentals=0,
            ),
        )(received, *ahead, *back, w_low, w_high, turn, chunk_beta, *([] if first else old))

    def exchange(x):
        return lax.all_to_all(x, axes, split_axis=0, concat_axis=0, tiled=True)

    local = jnp.arange(cycles, dtype=jnp.int32)
    flipped = jnp.where(south, cycles - 1 - local, local)
    cycle_index = (my_index * cycles + flipped).astype(f32)
    area = 2.0 * math.pi / lon_count * (math.pi / all_cycles) * jnp.sin(
        math.pi * (cycle_index + 0.5) / all_cycles
    )
    turned = jnp.where(south, jnp.flip(weight, 0), weight)
    turned = (area[:, None] * turned).T
    w_low = jnp.tile(turned[:half_lon], (1, PART))
    w_high = jnp.concatenate(
        [turned[half_lon : half_lon + 1], jnp.flip(turned[half_lon + 1 :], 0)], axis=0
    )
    w_high = jnp.tile(w_high, (1, PART))
    turn = (1 - 2 * (order_slots % 2)).astype(f32)[:, None]
    tables = half_tables(order_slots, lon_count)

    received = [exchange(synth(q)) for q in range(chunks)]
    old, held = None, None
    returned = []
    for q in range(chunks):
        chunk_beta = jnp.repeat(beta[q * CHUNK : (q + 1) * CHUNK], cycles)[None, :]
        analysed, low, high = fourier(received[q], tables, w_low, w_high, turn, chunk_beta, old)
        old = (low, high)
        returned.append(exchange(analysed))
    for q in range(chunks):
        held = analyse(q, returned[q], held)

    lane_cycle = jnp.arange(part_lanes, dtype=jnp.int32) % cycles
    pick = (lane_cycle[None, :] == flipped[:, None]).astype(f32)
    sums = [
        lax.dot_general(
            pick, s, (((1,), (1,)), ((), ())), precision=lax.Precision.HIGHEST,
            preferred_element_type=f32,
        )
        for s in old
    ]
    natural = 2.0 * math.pi / lon_count * (math.pi / all_cycles) * jnp.sin(
        math.pi * ((my_index * cycles + local).astype(f32) + 0.5) / all_cycles
    )
    if lax.axis_size("probe") == 2:
        ahead_half = lax.axis_index("probe") == 0
        keep = jnp.where(ahead_half, sums[0], sums[1])
        give = jnp.where(ahead_half, sums[1], sums[0])
        half = (keep + lax.ppermute(give, "probe", [(0, 1), (1, 0)])) * natural[:, None]
        mirrored = jnp.concatenate([half[:, :1], jnp.flip(half[:, 1:], 1)], axis=1)
        gradient = jnp.where(ahead_half, half, mirrored)
    else:
        terms = jnp.concatenate([sums[0], sums[1][:, :1], jnp.flip(sums[1][:, 1:], 1)], axis=1)
        gradient = lax.psum_scatter(
            terms * natural[:, None], "probe", scatter_dimension=1, tiled=True
        )
    return (held, gradient)


def body(probes_in, root_spectrum, order_slots, legendre, weight, beta):
    degrees, slots, all_cycles = legendre.shape
    fits = (
        slots % GROUP == 0
        and degrees % DEPTH == 0
        and degrees == order_slots.shape[0]
        and all_cycles % (2 * LANES) == 0
        and (PART * weight.shape[0]) % LANES == 0
        and probes_in.shape[0] % CHUNK == 0
        and weight.shape[1] % (2 * TILE) == 0
        and lax.axis_size(("lat", "blk")) % 2 == 0
    )
    chosen = fast_body if fits else plain_body
    return chosen(probes_in, root_spectrum, order_slots, legendre, weight, beta)


def solution(mesh):
    return jax.shard_map(
        body,
        mesh=mesh,
        in_specs=(
            P("probe", None, ("lat", "blk"), None),
            P(),
            P(),
            P(None, ("lat", "blk"), None),
            P(("lat", "blk"), None),
            P("probe"),
        ),
        out_specs=(P("probe", None, ("lat", "blk"), None), P(("lat", "blk"), "probe")),
        check_vma=False,
    )
```

```python
import functools
import math

import jax
import jax.numpy as jnp
from jax import lax
from jax.experimental import pallas as pl
from jax.experimental.pallas import tpu as pltpu
from jax.sharding import PartitionSpec as P

GROUP = 8
DEPTH = 128
CHUNK = 16
PART = 8
TILE = 256
VMEM_LIMIT = 60 * 2**20


def fourier_tables(orders, lon_count):
    longitude = jnp.arange(lon_count, dtype=jnp.int32)
    phase_idx = orders[:, None] * longitude[None, :] % lon_count
    angle = phase_idx.astype(jnp.float32) * (2.0 * math.pi / lon_count)
    twiddle = jnp.stack([jnp.cos(angle), jnp.sin(angle)])
    upper = twiddle.astype(jnp.bfloat16)
    lower = (twiddle - upper.astype(jnp.float32)).astype(jnp.bfloat16)
    return (upper, lower)


def cycle_work(spectra, inverse_tables, forward_tables, area, weight):
    grid_field = jnp.einsum(
        "pcmj,cmx->pjx", spectra, inverse_tables[0], preferred_element_type=jnp.float32
    )
    grid_field = grid_field + jnp.einsum(
        "pcmj,cmx->pjx", spectra, inverse_tables[1], preferred_element_type=jnp.float32
    )
    squares = grid_field * grid_field
    weighted = (area[None, :, None] * weight[None] * grid_field).astype(jnp.bfloat16)
    analysed = jnp.einsum(
        "pjx,cmx->pcmj", weighted, forward_tables[0], preferred_element_type=jnp.float32
    )
    analysed = analysed + jnp.einsum(
        "pjx,cmx->pcmj", weighted, forward_tables[1], preferred_element_type=jnp.float32
    )
    return (squares, analysed.astype(jnp.bfloat16))


def plain_body(probes_in, root_spectrum, order_slots, legendre, weight, beta):
    groups = lax.axis_size(("lat", "blk"))
    my_index = lax.axis_index(("lat", "blk"))
    cycle_count = weight.shape[0]
    lon_count = weight.shape[1]
    all_cycles = cycle_count * groups
    scaled = (probes_in.astype(jnp.float32) * root_spectrum).astype(jnp.bfloat16)
    spectra = jnp.einsum(
        "pcml,lmj->pcmj", scaled, legendre, preferred_element_type=jnp.float32
    ).astype(jnp.bfloat16)
    cycle_index = (my_index * cycle_count + jnp.arange(cycle_count, dtype=jnp.int32)).astype(
        jnp.float32
    )
    local_sines = jnp.sin(math.pi * (cycle_index + 0.5) / all_cycles)
    area = 2.0 * math.pi / lon_count * (math.pi / all_cycles) * local_sines
    forward_tables = fourier_tables(order_slots, lon_count)
    squares, analysed = cycle_work(
        lax.all_to_all(spectra, ("lat", "blk"), split_axis=3, concat_axis=2, tiled=True),
        forward_tables,
        forward_tables,
        area,
        weight,
    )
    returned = lax.all_to_all(analysed, ("lat", "blk"), split_axis=2, concat_axis=3, tiled=True)
    matvec = (
        jnp.einsum("pcmj,lmj->pcml", returned, legendre, preferred_element_type=jnp.float32)
        * root_spectrum
    )
    grad_terms = jnp.einsum("pjx,p->jx", squares, beta) * area[:, None]
    gradient = lax.psum_scatter(grad_terms, "probe", scatter_dimension=1, tiled=True)
    return (matvec, gradient)


def dot(a, b, dims=((1,), (0,))):
    return lax.dot_general(a, b, (dims, ((), ())), preferred_element_type=jnp.float32)


def split(x):
    upper = x.astype(jnp.bfloat16)
    return upper, (x - upper.astype(jnp.float32)).astype(jnp.bfloat16)


LANES = 128
PITCH = GROUP + 1


def every(slot, count):
    return pl.ds(slot, count, stride=PITCH)


def tiles(ref):
    return range(ref.shape[0])


def put(ref, rows, value):
    for t in tiles(ref):
        ref[t, rows, :] = value[:, t * LANES : (t + 1) * LANES]


def take(ref, rows):
    return jnp.concatenate([ref[t, rows, :] for t in tiles(ref)], axis=-1)


def spread_rows(tbl_ref, wide):
    @pl.loop(0, tbl_ref.shape[0] * 2 // DEPTH)
    def _(step):
        some = pl.ds(step * (DEPTH // 2), DEPTH // 2)
        for t in tiles(wide):
            piece = tbl_ref[some, :, :, t * LANES : (t + 1) * LANES].astype(jnp.float32)
            piece = piece.reshape(DEPTH, GROUP, LANES)
            for i in range(DEPTH):
                wide[t, pl.ds(step * (DEPTH * PITCH) + i * PITCH, GROUP), :] = piece[i]


def table_block(wide, step, slot):
    rows = pl.ds(step * (DEPTH * PITCH) + slot, DEPTH, stride=PITCH)
    return take(wide, rows).astype(jnp.bfloat16)


def visit(orders_ref, group, turn, pair, steps):
    first = orders_ref[group * GROUP + 2 * pair] // DEPTH
    mine = turn < steps - first
    slot = 2 * pair + jnp.where(mine, 0, 1)
    return slot, jnp.where(mine, first + turn, turn - 1)


def even_degree(shape):
    return lax.broadcasted_iota(jnp.int32, shape, 1) % 2 == 0


def synth_kernel(orders_ref, x_ref, root_ref, tbl_ref, sign_ref, *refs, split_up):
    xs, wide, acc, ns, ss = refs[-6:-1] if split_up else refs[-5:]
    outs = refs[:-6] if split_up else refs[:1]
    out_ref = refs[-1] if split_up else outs[0]
    mine = orders_ref[orders_ref.shape[0] - 1] if split_up else 0
    group = pl.program_id(0)
    chunk = x_ref.shape[0]
    cycles = out_ref.shape[3] // chunk
    half = out_ref.shape[0] // 2
    rows = chunk * 2
    scaled = (x_ref[...].astype(jnp.float32) * root_ref[...]).astype(jnp.bfloat16)
    scaled = scaled.astype(jnp.float32).reshape(rows, GROUP, scaled.shape[-1])
    for i in range(rows):
        put(xs, pl.ds(i * PITCH, GROUP), scaled[i])
    acc[...] = jnp.zeros_like(acc)

    spread_rows(tbl_ref, wide)
    steps = tbl_ref.shape[0] * 2 // DEPTH

    @pl.loop(0, steps + 1)
    def _(turn):
        for pair in range(GROUP // 2):
            slot, step = visit(orders_ref, group, turn, pair, steps)
            x = xs[step, every(slot, rows), :]
            even = even_degree(x.shape)
            x = jnp.concatenate([jnp.where(even, x, 0.0), jnp.where(even, 0.0, x)], axis=0)
            table = table_block(wide, step, slot)
            acc[slot] += dot(x.astype(jnp.bfloat16), table)

    for slot in range(GROUP):
        even, odd = acc[slot, :rows], acc[slot, rows:]
        put(ns, every(slot, rows), even + odd)
        put(ss, every(slot, rows), even - odd)
    for c in range(2):
        north, south = [], []
        for p in range(chunk):
            place = pl.ds((2 * p + c) * PITCH, GROUP)
            north.append(take(ns, place))
            south.append(take(ss, place) * sign_ref[...])
        for d in range(half):
            for source, place in ((north, d), (south, 2 * half - 1 - d)):
                pieces = [piece[:, d * cycles : (d + 1) * cycles] for piece in source]
                at = place ^ mine if split_up else place
                out_ref[at, c] = jnp.concatenate(pieces, axis=-1).astype(jnp.bfloat16)
    if split_up:
        for r, out in enumerate(outs):
            out[...] = out_ref[r]


def analysis_kernel(orders_ref, root_ref, tbl_ref, sign_ref, *refs, sources, split_up):
    if split_up:
        q_ref = refs[-1]
        refs, parts = refs[:-1], refs[:sources]
        mine = orders_ref[orders_ref.shape[0] - 1]
        for r, part in enumerate(parts):
            q_ref[mine ^ r] = part[...]
    else:
        q_ref = refs[0]
    out_ref, plus, minus, wide, held, outs = refs[-6:]
    group = pl.program_id(0)
    chunk = out_ref.shape[0]
    cycles = q_ref.shape[3] // chunk
    half = q_ref.shape[0] // 2
    rows = chunk * 2

    for c in range(2):
        blocks = [q_ref[d, c].astype(jnp.float32) for d in range(2 * half)]
        for p in range(chunk):
            cut = slice(p * cycles, (p + 1) * cycles)
            north = jnp.concatenate([blocks[d][:, cut] for d in range(half)], axis=-1)
            other = [blocks[2 * half - 1 - d][:, cut] for d in range(half)]
            south = jnp.concatenate(other, axis=-1) * sign_ref[...]
            place = pl.ds((2 * p + c) * PITCH, GROUP)
            put(plus, place, north + south)
            put(minus, place, north - south)
    for slot in range(GROUP):
        both = [take(ref, every(slot, rows)) for ref in (plus, minus)]
        upper, lower = split(jnp.concatenate(both, axis=0))
        held[slot, : 2 * rows] = upper
        held[slot, 2 * rows :] = lower
    outs[...] = jnp.zeros_like(outs)

    spread_rows(tbl_ref, wide)
    steps = tbl_ref.shape[0] * 2 // DEPTH

    @pl.loop(0, steps + 1)
    def _(turn):
        for pair in range(GROUP // 2):
            slot, step = visit(orders_ref, group, turn, pair, steps)
            now = pl.ds(pl.multiple_of(step * DEPTH, DEPTH), DEPTH)
            table = table_block(wide, step, slot)
            both = dot(held[slot], table, ((1,), (1,)))
            both = both[: 2 * rows] + both[2 * rows :]
            even = even_degree((rows, DEPTH))
            chosen = jnp.where(even, both[:rows], both[rows:])
            outs[step, every(slot, rows), :] = chosen * root_ref[:, now]

    for p in range(chunk):
        for c in range(2):
            out_ref[p, c] = take(outs, pl.ds((2 * p + c) * PITCH, GROUP))


def fourier_kernel(me_ref, *refs, first, sources, split_up):
    ahead_cos, ahead_sin, back_cos, back_sin, w_low, w_high, turn_ref, beta_ref = refs[:8]
    old_low, old_high = (None, None) if first else refs[8:10]
    refs = refs[8:] if first else refs[10:]
    mine_at = me_ref[0]
    step, part = pl.program_id(0), pl.program_id(1)
    if split_up:
        arrived, sent = refs[:sources], refs[sources : 2 * sources]
        g_low, g_high, rc, rs, acc_c, acc_s, middle, r_ref = refs[2 * sources :]

        @pl.when((step == 0) & (part == 0))
        def _():
            for r, piece in enumerate(arrived):
                r_ref[mine_at ^ r] = piece[...]

    else:
        r_ref, out_ref, g_low, g_high, rc, rs, acc_c, acc_s, middle = refs
    slots = r_ref.shape[2]
    tile, lanes = g_low.shape
    count = acc_c.shape[1]
    mine = pl.ds(pl.multiple_of(part * lanes, LANES), lanes)

    @pl.when(step == 0)
    def _():
        for pair in range(sources // 2):
            for c, place in ((0, rc), (1, rs)):
                both = [r_ref[2 * pair + i, c, :, mine].astype(jnp.float32) for i in range(2)]
                place[part, pl.ds(2 * slots * pair, 2 * slots)] = jnp.concatenate(
                    both, axis=0
                ).astype(jnp.bfloat16)
        turned = turn_ref[...] * rc[part].astype(jnp.float32)
        mid = jnp.sum(turned, axis=0, keepdims=True)
        middle[part] = mid
        w_mid = (w_high[pl.ds(0, 1), :] * mid).astype(jnp.bfloat16).astype(jnp.float32)
        acc_c[part] = turn_ref[...] * w_mid
        acc_s[part] = jnp.zeros_like(acc_s[part])

    c_part = dot(ahead_cos[0], rc[part])
    c_part = c_part[:tile] + c_part[tile:]
    s_part = dot(ahead_sin[0], rs[part])
    s_part = s_part[:tile] + s_part[tile:]
    low = c_part + s_part
    row = lax.broadcasted_iota(jnp.int32, low.shape, 0) + step * tile
    high = jnp.where(row == 0, middle[part], c_part - s_part)
    beta = beta_ref[:, mine]
    low_sq = beta * (low * low)
    high_sq = beta * (high * high)

    @pl.when(part == 0)
    def _():
        g_low[...] = low_sq if first else old_low[...] + low_sq
        g_high[...] = high_sq if first else old_high[...] + high_sq

    @pl.when(part > 0)
    def _():
        g_low[...] += low_sq
        g_high[...] += high_sq

    low = (w_low[...] * low).astype(jnp.bfloat16).astype(jnp.float32)
    high = jnp.where(row == 0, 0.0, w_high[...] * high).astype(jnp.bfloat16).astype(jnp.float32)
    for folded, back, acc in ((low + high, back_cos, acc_c), (low - high, back_sin, acc_s)):
        upper, lower = split(folded)
        both = dot(back[...], upper)
        acc[part] += both[:count] + both[count:] + dot(back[pl.ds(0, count), :], lower)

    @pl.when(step == pl.num_programs(0) - 1)
    def _():
        for d in range(sources):
            for c, acc in ((0, acc_c), (1, acc_s)):
                if split_up:
                    start = pl.multiple_of((mine_at ^ d) * slots, GROUP)
                    sent[d][c, :, mine] = acc[part, pl.ds(start, slots)].astype(jnp.bfloat16)
                else:
                    found = acc[part, pl.ds(slots * d, slots)]
                    out_ref[d, c, :, mine] = found.astype(jnp.bfloat16)


def half_tables(orders, lon_count):
    half = lon_count // 2

    def trig(points):
        idx = orders[:, None] * points[None, :] % lon_count
        angle = idx.astype(jnp.float32) * (2.0 * math.pi / lon_count)
        return lax.optimization_barrier((jnp.cos(angle), jnp.sin(angle)))

    def joined(parts, fine, shape, axes):
        (ca, sa), (cb, sb) = parts
        ca, sa = (t[axes[0]] for t in (ca, sa))
        cb, sb = (t[axes[1]] for t in (cb, sb))
        cosine = (ca * cb - sa * sb).reshape(shape)
        sine = (sa * cb + ca * sb).reshape(shape)
        return split(cosine) + split(sine)

    count = orders.shape[0]
    fine = 128
    coarse_points = jnp.arange(half // fine, dtype=jnp.int32) * fine
    fine_points = jnp.arange(fine, dtype=jnp.int32)
    coarse, small = trig(coarse_points), trig(fine_points)
    every = slice(None)
    back = joined(
        (coarse, small), fine, (count, half), ((every, every, None), (every, None, every))
    )
    coarse_t = tuple(t.T for t in coarse)
    small_t = tuple(t.T for t in small)
    ahead = joined(
        (coarse_t, small_t), fine, (half, count), ((every, None, every), (None, every, every))
    )
    tiled = [t.reshape(half // TILE, TILE, count) for t in ahead]
    ahead = [jnp.concatenate(tiled[i : i + 2], axis=1) for i in (0, 2)]
    back = [jnp.concatenate(back[i : i + 2], axis=0) for i in (0, 2)]
    return ahead, back


def fast_body(probes_in, root_spectrum, order_slots, legendre, weight, beta):
    axes = ("lat", "blk")
    groups = lax.axis_size(axes)
    my_index = lax.axis_index(axes)
    cycles, lon_count = weight.shape
    half_lon = lon_count // 2
    all_cycles = cycles * groups
    half_cycles = all_cycles // 2
    degrees, slots = legendre.shape[:2]
    orders_count = order_slots.shape[0]
    probes = probes_in.shape[0]
    chunks = probes // CHUNK
    lanes = CHUNK * cycles
    part_lanes = PART * cycles
    parts = CHUNK // PART
    south = my_index >= groups // 2
    params = functools.partial(pltpu.CompilerParams, vmem_limit_bytes=VMEM_LIMIT)
    f32, bf16 = jnp.float32, jnp.bfloat16

    my_orders = lax.dynamic_slice_in_dim(order_slots, my_index * slots, slots)
    sign = (1 - 2 * (my_orders % 2)).astype(f32)
    sign = jnp.broadcast_to(sign[:, None], (slots, half_cycles))
    root = root_spectrum[None, :]
    table = legendre.reshape(degrees // 2, 2, slots, all_cycles)
    rows = CHUNK * 2
    whole = lambda shape: pl.BlockSpec(shape, lambda *_: (0,) * len(shape))
    table_spec = pl.BlockSpec((degrees // 2, 2, GROUP, half_cycles), lambda g, o: (0, 0, g, 0))
    sign_spec = pl.BlockSpec((GROUP, half_cycles), lambda g, o: (g, 0))
    payload_spec = pl.BlockSpec((groups, 2, GROUP, lanes), lambda g, o: (0, 0, g, 0))
    payload = jax.ShapeDtypeStruct((groups, 2, slots, lanes), bf16)
    table_bytes = degrees * slots * half_cycles * 2
    legendre_cost = pl.CostEstimate(
        flops=1000 * table_bytes, bytes_accessed=table_bytes, transcendentals=0
    )
    tiled = lambda width, height: pltpu.VMEM((width // LANES, height, LANES), f32)
    degree_tiles = tiled(degrees, rows * PITCH)
    cycle_tiles = tiled(half_cycles, rows * PITCH)
    wide = tiled(half_cycles, degrees * PITCH)

    def chunk_spec(q):
        return pl.BlockSpec((CHUNK, 2, GROUP, degrees), lambda g, o: (q, 0, g, 0))

    scalars = jnp.concatenate([my_orders, my_index[None].astype(jnp.int32)])
    piece = jax.ShapeDtypeStruct((2, slots, lanes), bf16)
    piece_spec = pl.BlockSpec((2, GROUP, lanes), lambda g, o: (0, g, 0))
    stack = pltpu.VMEM((groups, 2, GROUP, lanes), bf16)

    def synth(q, split_up):
        return pl.pallas_call(
            functools.partial(synth_kernel, split_up=split_up),
            name="synth",
            grid_spec=pltpu.PrefetchScalarGridSpec(
                num_scalar_prefetch=1,
                grid=(slots // GROUP,),
                in_specs=[chunk_spec(q), whole(root.shape), table_spec, sign_spec],
                out_specs=[piece_spec] * groups if split_up else payload_spec,
                scratch_shapes=[
                    degree_tiles,
                    wide,
                    pltpu.VMEM((GROUP, 2 * rows, half_cycles), f32),
                    cycle_tiles,
                    cycle_tiles,
                ]
                + ([stack] if split_up else []),
            ),
            out_shape=[piece] * groups if split_up else payload,
            compiler_params=params(),
            cost_estimate=legendre_cost,
        )(scalars, probes_in, root, table, sign)

    def analyse(q, returned, held, split_up):
        first = held is None
        arrays = list(returned) if split_up else [returned]
        return pl.pallas_call(
            functools.partial(analysis_kernel, sources=groups, split_up=split_up),
            name="analyse",
            grid_spec=pltpu.PrefetchScalarGridSpec(
                num_scalar_prefetch=1,
                grid=(slots // GROUP,),
                in_specs=[whole(root.shape), table_spec, sign_spec]
                + [piece_spec if split_up else payload_spec] * len(arrays)
                + ([] if first else [pl.BlockSpec(memory_space=pl.ANY)]),
                out_specs=chunk_spec(q),
                scratch_shapes=[
                    cycle_tiles,
                    cycle_tiles,
                    wide,
                    pltpu.VMEM((GROUP, 4 * rows, half_cycles), bf16),
                    degree_tiles,
                ]
                + ([stack] if split_up else []),
            ),
            out_shape=jax.ShapeDtypeStruct((probes, 2, slots, degrees), f32),
            input_output_aliases={} if first else {4 + len(arrays): 0},
            compiler_params=params(),
            cost_estimate=legendre_cost,
        )(scalars, root, table, sign, *arrays, *([] if first else [held]))

    ahead_spec = pl.BlockSpec((1, 2 * TILE, orders_count), lambda i, h, o: (i, 0, 0))
    back_spec = pl.BlockSpec((2 * orders_count, TILE), lambda i, h, o: (0, i))
    grid_spec = pl.BlockSpec((TILE, part_lanes), lambda i, h, o: (i, 0))

    def fourier(received, tables, w_low, w_high, turn, chunk_beta, old, split_up):
        first = old is None
        ahead, back = tables
        square = jax.ShapeDtypeStruct((half_lon, part_lanes), f32)
        arrays = list(received) if split_up else [received]
        shapes = [piece] * groups if split_up else [payload]
        specs = [whole(shape.shape) for shape in shapes]
        return pl.pallas_call(
            functools.partial(
                fourier_kernel, first=first, sources=groups, split_up=split_up
            ),
            name="fourier",
            grid_spec=pltpu.PrefetchScalarGridSpec(
                num_scalar_prefetch=1,
                grid=(half_lon // TILE, parts),
                in_specs=[ahead_spec] * 2
                + [back_spec] * 2
                + [grid_spec] * 2
                + [whole((orders_count, 1)), whole((1, lanes))]
                + ([] if first else [grid_spec] * 2)
                + specs,
                out_specs=specs + [grid_spec, grid_spec],
                scratch_shapes=[pltpu.VMEM((parts, orders_count, part_lanes), bf16)] * 2
                + [pltpu.VMEM((parts, orders_count, part_lanes), f32)] * 2
                + [pltpu.VMEM((parts, 1, part_lanes), f32)]
                + ([pltpu.VMEM(payload.shape, bf16)] if split_up else []),
            ),
            out_shape=shapes + [square, square],
            input_output_aliases={} if first else {9: len(shapes), 10: len(shapes) + 1},
            compiler_params=params(),
            cost_estimate=pl.CostEstimate(
                flops=40 * half_lon * lanes * orders_count,
                bytes_accessed=16 * half_lon * orders_count + 16 * half_lon * part_lanes,
                transcendentals=0,
            ),
        )(
            my_index[None].astype(jnp.int32),
            *ahead,
            *back,
            w_low,
            w_high,
            turn,
            chunk_beta,
            *([] if first else old),
            *arrays,
        )

    def exchange(x, split_up):
        if split_up:
            return [x[0]] + [
                lax.ppermute(x[r], axes, [(i, i ^ r) for i in range(groups)])
                for r in range(1, groups)
            ]
        return lax.all_to_all(x, axes, split_axis=0, concat_axis=0, tiled=True)

    local = jnp.arange(cycles, dtype=jnp.int32)
    flipped = jnp.where(south, cycles - 1 - local, local)
    cycle_index = (my_index * cycles + flipped).astype(f32)
    area = 2.0 * math.pi / lon_count * (math.pi / all_cycles) * jnp.sin(
        math.pi * (cycle_index + 0.5) / all_cycles
    )
    turned = jnp.where(south, jnp.flip(weight, 0), weight)
    turned = (area[:, None] * turned).T
    w_low = jnp.tile(turned[:half_lon], (1, PART))
    w_high = jnp.concatenate(
        [turned[half_lon : half_lon + 1], jnp.flip(turned[half_lon + 1 :], 0)], axis=0
    )
    w_high = jnp.tile(w_high, (1, PART))
    turn = (1 - 2 * (order_slots % 2)).astype(f32)[:, None]
    tables = half_tables(order_slots, lon_count)

    split_up = [q % 2 == 1 for q in range(chunks)]
    received = [exchange(synth(q, split_up[q]), split_up[q]) for q in range(chunks)]
    old, held = None, None
    returned = []
    for q in range(chunks):
        chunk_beta = jnp.repeat(beta[q * CHUNK : (q + 1) * CHUNK], cycles)[None, :]
        *analysed, low, high = fourier(
            received[q], tables, w_low, w_high, turn, chunk_beta, old, split_up[q]
        )
        old = (low, high)
        returned.append(exchange(analysed if split_up[q] else analysed[0], split_up[q]))
    for q in range(chunks):
        held = analyse(q, returned[q], held, split_up[q])

    lane_cycle = jnp.arange(part_lanes, dtype=jnp.int32) % cycles
    pick = (lane_cycle[None, :] == flipped[:, None]).astype(f32)
    sums = [
        lax.dot_general(
            pick, s, (((1,), (1,)), ((), ())), precision=lax.Precision.HIGHEST,
            preferred_element_type=f32,
        )
        for s in old
    ]
    natural = 2.0 * math.pi / lon_count * (math.pi / all_cycles) * jnp.sin(
        math.pi * ((my_index * cycles + local).astype(f32) + 0.5) / all_cycles
    )
    if lax.axis_size("probe") == 2:
        ahead_half = lax.axis_index("probe") == 0
        keep = jnp.where(ahead_half, sums[0], sums[1])
        give = jnp.where(ahead_half, sums[1], sums[0])
        half = (keep + lax.ppermute(give, "probe", [(0, 1), (1, 0)])) * natural[:, None]
        mirrored = jnp.concatenate([half[:, :1], jnp.flip(half[:, 1:], 1)], axis=1)
        gradient = jnp.where(ahead_half, half, mirrored)
    else:
        terms = jnp.concatenate([sums[0], sums[1][:, :1], jnp.flip(sums[1][:, 1:], 1)], axis=1)
        gradient = lax.psum_scatter(
            terms * natural[:, None], "probe", scatter_dimension=1, tiled=True
        )
    return (held, gradient)


def body(probes_in, root_spectrum, order_slots, legendre, weight, beta):
    degrees, slots, all_cycles = legendre.shape
    fits = (
        slots % GROUP == 0
        and degrees % DEPTH == 0
        and degrees == order_slots.shape[0]
        and all_cycles % (2 * LANES) == 0
        and (PART * weight.shape[0]) % LANES == 0
        and probes_in.shape[0] % CHUNK == 0
        and weight.shape[1] % (2 * TILE) == 0
        and lax.axis_size(("lat", "blk")) in (2, 4, 8, 16, 32)
    )
    chosen = fast_body if fits else plain_body
    return chosen(probes_in, root_spectrum, order_slots, legendre, weight, beta)


def solution(mesh):
    return jax.shard_map(
        body,
        mesh=mesh,
        in_specs=(
            P("probe", None, ("lat", "blk"), None),
            P(),
            P(),
            P(None, ("lat", "blk"), None),
            P(("lat", "blk"), None),
            P("probe"),
        ),
        out_specs=(P("probe", None, ("lat", "blk"), None), P(("lat", "blk"), "probe")),
        check_vma=False,
    )
```

```python
import functools
import math

import jax
import jax.numpy as jnp
from jax import lax
from jax.experimental import pallas as pl
from jax.experimental.pallas import tpu as pltpu
from jax.sharding import PartitionSpec as P


GROUP = 8
DEPTH = 128
CHUNK = 16
PART = 8
TILE = 256
VMEM_LIMIT = 60 * 2**20


def fourier_tables(orders, lon_count):
    longitude = jnp.arange(lon_count, dtype=jnp.int32)
    phase_idx = orders[:, None] * longitude[None, :] % lon_count
    angle = phase_idx.astype(jnp.float32) * (2.0 * math.pi / lon_count)
    twiddle = jnp.stack([jnp.cos(angle), jnp.sin(angle)])
    upper = twiddle.astype(jnp.bfloat16)
    lower = (twiddle - upper.astype(jnp.float32)).astype(jnp.bfloat16)
    return (upper, lower)


def cycle_work(spectra, inverse_tables, forward_tables, area, weight):
    grid_field = jnp.einsum(
        "pcmj,cmx->pjx", spectra, inverse_tables[0], preferred_element_type=jnp.float32
    )
    grid_field = grid_field + jnp.einsum(
        "pcmj,cmx->pjx", spectra, inverse_tables[1], preferred_element_type=jnp.float32
    )
    squares = grid_field * grid_field
    weighted = (area[None, :, None] * weight[None] * grid_field).astype(jnp.bfloat16)
    analysed = jnp.einsum(
        "pjx,cmx->pcmj", weighted, forward_tables[0], preferred_element_type=jnp.float32
    )
    analysed = analysed + jnp.einsum(
        "pjx,cmx->pcmj", weighted, forward_tables[1], preferred_element_type=jnp.float32
    )
    return (squares, analysed.astype(jnp.bfloat16))


def plain_body(probes_in, root_spectrum, order_slots, legendre, weight, beta):
    groups = lax.axis_size(("lat", "blk"))
    my_index = lax.axis_index(("lat", "blk"))
    cycle_count = weight.shape[0]
    lon_count = weight.shape[1]
    all_cycles = cycle_count * groups
    scaled = (probes_in.astype(jnp.float32) * root_spectrum).astype(jnp.bfloat16)
    spectra = jnp.einsum(
        "pcml,lmj->pcmj", scaled, legendre, preferred_element_type=jnp.float32
    ).astype(jnp.bfloat16)
    cycle_index = (my_index * cycle_count + jnp.arange(cycle_count, dtype=jnp.int32)).astype(
        jnp.float32
    )
    local_sines = jnp.sin(math.pi * (cycle_index + 0.5) / all_cycles)
    area = 2.0 * math.pi / lon_count * (math.pi / all_cycles) * local_sines
    forward_tables = fourier_tables(order_slots, lon_count)
    squares, analysed = cycle_work(
        lax.all_to_all(spectra, ("lat", "blk"), split_axis=3, concat_axis=2, tiled=True),
        forward_tables,
        forward_tables,
        area,
        weight,
    )
    returned = lax.all_to_all(analysed, ("lat", "blk"), split_axis=2, concat_axis=3, tiled=True)
    matvec = (
        jnp.einsum("pcmj,lmj->pcml", returned, legendre, preferred_element_type=jnp.float32)
        * root_spectrum
    )
    grad_terms = jnp.einsum("pjx,p->jx", squares, beta) * area[:, None]
    gradient = lax.psum_scatter(grad_terms, "probe", scatter_dimension=1, tiled=True)
    return (matvec, gradient)


def dot(a, b, dims=((1,), (0,))):
    return lax.dot_general(a, b, (dims, ((), ())), preferred_element_type=jnp.float32)


def split(x):
    upper = x.astype(jnp.bfloat16)
    return upper, (x - upper.astype(jnp.float32)).astype(jnp.bfloat16)


LANES = 128
PITCH = GROUP + 1


def every(slot, count):
    return pl.ds(slot, count, stride=PITCH)


def tiles(ref):
    return range(ref.shape[0])


def put(ref, rows, value):
    for t in tiles(ref):
        ref[t, rows, :] = value[:, t * LANES : (t + 1) * LANES]


def take(ref, rows):
    return jnp.concatenate([ref[t, rows, :] for t in tiles(ref)], axis=-1)


def spread_rows(tbl_ref, wide):
    @pl.loop(0, tbl_ref.shape[0] * 2 // DEPTH)
    def _(step):
        some = pl.ds(step * (DEPTH // 2), DEPTH // 2)
        for t in tiles(wide):
            piece = tbl_ref[some, :, :, t * LANES : (t + 1) * LANES].astype(jnp.float32)
            piece = piece.reshape(DEPTH, GROUP, LANES)
            for i in range(DEPTH):
                wide[t, pl.ds(step * (DEPTH * PITCH) + i * PITCH, GROUP), :] = piece[i]


def table_block(wide, step, slot):
    rows = pl.ds(step * (DEPTH * PITCH) + slot, DEPTH, stride=PITCH)
    return take(wide, rows).astype(jnp.bfloat16)


def slot_signs(orders_ref, base, shape):
    row = lax.broadcasted_iota(jnp.int32, shape, 0)
    odd = jnp.zeros(shape, jnp.int32)
    for slot in range(GROUP):
        odd = jnp.where(row == slot, orders_ref[base + slot] % 2, odd)
    return (1 - 2 * odd).astype(jnp.float32)


def visit(orders_ref, base, turn, pair, steps):
    first = orders_ref[base + 2 * pair] // DEPTH
    mine = turn < steps - first
    slot = 2 * pair + jnp.where(mine, 0, 1)
    return slot, jnp.where(mine, first + turn, turn - 1)


def even_degree(shape):
    return lax.broadcasted_iota(jnp.int32, shape, 1) % 2 == 0


def synth_kernel(orders_ref, me_ref, x_ref, root_ref, tbl_ref, *refs, slots, split_up):
    xs, wide, acc, ns, ss = refs[-6:-1] if split_up else refs[-5:]
    outs = refs[:-6] if split_up else refs[:1]
    out_ref = refs[-1] if split_up else outs[0]
    mine = me_ref[0]
    base = mine * slots + pl.program_id(0) * GROUP
    chunk = x_ref.shape[0]
    cycles = out_ref.shape[3] // chunk
    half = out_ref.shape[0] // 2
    rows = chunk * 2
    scaled = (x_ref[...].astype(jnp.float32) * root_ref[...]).astype(jnp.bfloat16)
    scaled = scaled.astype(jnp.float32).reshape(rows, GROUP, scaled.shape[-1])
    for i in range(rows):
        put(xs, pl.ds(i * PITCH, GROUP), scaled[i])
    acc[...] = jnp.zeros_like(acc)

    spread_rows(tbl_ref, wide)
    steps = tbl_ref.shape[0] * 2 // DEPTH

    @pl.loop(0, steps + 1)
    def _(turn):
        for pair in range(GROUP // 2):
            slot, step = visit(orders_ref, base, turn, pair, steps)
            x = xs[step, every(slot, rows), :]
            even = even_degree(x.shape)
            x = jnp.concatenate([jnp.where(even, x, 0.0), jnp.where(even, 0.0, x)], axis=0)
            table = table_block(wide, step, slot)
            acc[slot] += dot(x.astype(jnp.bfloat16), table)

    for slot in range(GROUP):
        even, odd = acc[slot, :rows], acc[slot, rows:]
        put(ns, every(slot, rows), even + odd)
        put(ss, every(slot, rows), even - odd)
    sign = slot_signs(orders_ref, base, (GROUP, acc.shape[-1]))
    for c in range(2):
        north, south = [], []
        for p in range(chunk):
            place = pl.ds((2 * p + c) * PITCH, GROUP)
            north.append(take(ns, place))
            south.append(take(ss, place) * sign)
        for d in range(half):
            for source, place in ((north, d), (south, 2 * half - 1 - d)):
                pieces = [piece[:, d * cycles : (d + 1) * cycles] for piece in source]
                at = place ^ mine if split_up else place
                out_ref[at, c] = jnp.concatenate(pieces, axis=-1).astype(jnp.bfloat16)
    if split_up:
        for r, out in enumerate(outs):
            out[...] = out_ref[r]


def analysis_kernel(orders_ref, me_ref, root_ref, tbl_ref, *refs, slots, sources, split_up):
    mine = me_ref[0]
    if split_up:
        q_ref = refs[-1]
        refs, parts = refs[:-1], refs[:sources]
        for r, part in enumerate(parts):
            q_ref[mine ^ r] = part[...]
    else:
        q_ref = refs[0]
    out_ref, plus, minus, wide, held, outs = refs[-6:]
    base = mine * slots + pl.program_id(0) * GROUP
    chunk = out_ref.shape[0]
    cycles = q_ref.shape[3] // chunk
    half = q_ref.shape[0] // 2
    rows = chunk * 2

    sign = slot_signs(orders_ref, base, (GROUP, half * cycles))
    for c in range(2):
        blocks = [q_ref[d, c].astype(jnp.float32) for d in range(2 * half)]
        for p in range(chunk):
            cut = slice(p * cycles, (p + 1) * cycles)
            north = jnp.concatenate([blocks[d][:, cut] for d in range(half)], axis=-1)
            other = [blocks[2 * half - 1 - d][:, cut] for d in range(half)]
            south = jnp.concatenate(other, axis=-1) * sign
            place = pl.ds((2 * p + c) * PITCH, GROUP)
            put(plus, place, north + south)
            put(minus, place, north - south)
    for slot in range(GROUP):
        both = [take(ref, every(slot, rows)) for ref in (plus, minus)]
        upper, lower = split(jnp.concatenate(both, axis=0))
        held[slot, : 2 * rows] = upper
        held[slot, 2 * rows :] = lower
    outs[...] = jnp.zeros_like(outs)

    spread_rows(tbl_ref, wide)
    steps = tbl_ref.shape[0] * 2 // DEPTH

    @pl.loop(0, steps + 1)
    def _(turn):
        for pair in range(GROUP // 2):
            slot, step = visit(orders_ref, base, turn, pair, steps)
            now = pl.ds(pl.multiple_of(step * DEPTH, DEPTH), DEPTH)
            table = table_block(wide, step, slot)
            both = dot(held[slot], table, ((1,), (1,)))
            both = both[: 2 * rows] + both[2 * rows :]
            even = even_degree((rows, DEPTH))
            chosen = jnp.where(even, both[:rows], both[rows:])
            outs[step, every(slot, rows), :] = chosen * root_ref[:, now]

    for p in range(chunk):
        for c in range(2):
            out_ref[p, c] = take(outs, pl.ds((2 * p + c) * PITCH, GROUP))


def fourier_kernel(me_ref, *refs, first, sources, split_up):
    ahead_cos, ahead_sin, back_cos, back_sin, w_low, w_high, turn_ref, beta_ref = refs[:8]
    old_low, old_high = (None, None) if first else refs[8:10]
    refs = refs[8:] if first else refs[10:]
    mine_at = me_ref[0]
    step, part = pl.program_id(0), pl.program_id(1)
    if split_up:
        arrived, sent = refs[:sources], refs[sources : 2 * sources]
        g_low, g_high, rc, rs, acc_c, acc_s, middle, r_ref = refs[2 * sources :]

        @pl.when((step == 0) & (part == 0))
        def _():
            for r, piece in enumerate(arrived):
                r_ref[mine_at ^ r] = piece[...]

    else:
        r_ref, out_ref, g_low, g_high, rc, rs, acc_c, acc_s, middle = refs
    slots = r_ref.shape[2]
    tile, lanes = g_low.shape
    count = acc_c.shape[1]
    mine = pl.ds(pl.multiple_of(part * lanes, LANES), lanes)

    @pl.when(step == 0)
    def _():
        for pair in range(sources // 2):
            for c, place in ((0, rc), (1, rs)):
                both = [r_ref[2 * pair + i, c, :, mine].astype(jnp.float32) for i in range(2)]
                place[part, pl.ds(2 * slots * pair, 2 * slots)] = jnp.concatenate(
                    both, axis=0
                ).astype(jnp.bfloat16)
        turned = turn_ref[...] * rc[part].astype(jnp.float32)
        mid = jnp.sum(turned, axis=0, keepdims=True)
        middle[part] = mid
        w_mid = (w_high[pl.ds(0, 1), :] * mid).astype(jnp.bfloat16).astype(jnp.float32)
        acc_c[part] = turn_ref[...] * w_mid
        acc_s[part] = jnp.zeros_like(acc_s[part])

    c_part = dot(ahead_cos[0], rc[part])
    c_part = c_part[:tile] + c_part[tile:]
    s_part = dot(ahead_sin[0], rs[part])
    s_part = s_part[:tile] + s_part[tile:]
    low = c_part + s_part
    row = lax.broadcasted_iota(jnp.int32, low.shape, 0) + step * tile
    high = jnp.where(row == 0, middle[part], c_part - s_part)
    beta = beta_ref[:, mine]
    low_sq = beta * (low * low)
    high_sq = beta * (high * high)

    @pl.when(part == 0)
    def _():
        g_low[...] = low_sq if first else old_low[...] + low_sq
        g_high[...] = high_sq if first else old_high[...] + high_sq

    @pl.when(part > 0)
    def _():
        g_low[...] += low_sq
        g_high[...] += high_sq

    low = (w_low[...] * low).astype(jnp.bfloat16).astype(jnp.float32)
    high = jnp.where(row == 0, 0.0, w_high[...] * high).astype(jnp.bfloat16).astype(jnp.float32)
    for folded, back, acc in ((low + high, back_cos, acc_c), (low - high, back_sin, acc_s)):
        upper, lower = split(folded)
        both = dot(back[...], upper)
        acc[part] += both[:count] + both[count:] + dot(back[pl.ds(0, count), :], lower)

    @pl.when(step == pl.num_programs(0) - 1)
    def _():
        for d in range(sources):
            for c, acc in ((0, acc_c), (1, acc_s)):
                if split_up:
                    start = pl.multiple_of((mine_at ^ d) * slots, GROUP)
                    sent[d][c, :, mine] = acc[part, pl.ds(start, slots)].astype(jnp.bfloat16)
                else:
                    found = acc[part, pl.ds(slots * d, slots)]
                    out_ref[d, c, :, mine] = found.astype(jnp.bfloat16)


def half_tables(orders, lon_count):
    half = lon_count // 2

    def trig(points):
        idx = orders[:, None] * points[None, :] % lon_count
        angle = idx.astype(jnp.float32) * (2.0 * math.pi / lon_count)
        return lax.optimization_barrier((jnp.cos(angle), jnp.sin(angle)))

    def joined(parts, shape, axes):
        (ca, sa), (cb, sb) = parts
        ca, sa = (t[axes[0]] for t in (ca, sa))
        cb, sb = (t[axes[1]] for t in (cb, sb))
        cosine = (ca * cb - sa * sb).reshape(shape)
        sine = (sa * cb + ca * sb).reshape(shape)
        return split(cosine) + split(sine)

    count = orders.shape[0]
    fine = 128
    coarse_points = jnp.arange(half // fine, dtype=jnp.int32) * fine
    fine_points = jnp.arange(fine, dtype=jnp.int32)
    coarse, small = trig(coarse_points), trig(fine_points)
    every = slice(None)
    back = joined((coarse, small), (count, half), ((every, every, None), (every, None, every)))
    coarse_t = tuple(t.T for t in coarse)
    small_t = tuple(t.T for t in small)
    ahead = joined((coarse_t, small_t), (half, count), ((every, None, every), (None, every, every)))
    tiled = [t.reshape(half // TILE, TILE, count) for t in ahead]
    ahead = [jnp.concatenate(tiled[i : i + 2], axis=1) for i in (0, 2)]
    back = [jnp.concatenate(back[i : i + 2], axis=0) for i in (0, 2)]
    return ahead, back


def fast_body(probes_in, root_spectrum, order_slots, legendre, weight, beta):
    axes = ("lat", "blk")
    groups = lax.axis_size(axes)
    my_index = lax.axis_index(axes)
    cycles, lon_count = weight.shape
    half_lon = lon_count // 2
    all_cycles = cycles * groups
    half_cycles = all_cycles // 2
    degrees, slots = legendre.shape[:2]
    orders_count = order_slots.shape[0]
    probes = probes_in.shape[0]
    chunks = probes // CHUNK
    lanes = CHUNK * cycles
    part_lanes = PART * cycles
    parts = CHUNK // PART
    south = my_index >= groups // 2
    params = functools.partial(pltpu.CompilerParams, vmem_limit_bytes=VMEM_LIMIT)
    f32, bf16 = jnp.float32, jnp.bfloat16

    me = my_index[None].astype(jnp.int32)
    root = root_spectrum[None, :]
    table = legendre.reshape(degrees // 2, 2, slots, all_cycles)
    rows = CHUNK * 2
    whole = lambda shape: pl.BlockSpec(shape, lambda *_: (0,) * len(shape))
    table_spec = pl.BlockSpec((degrees // 2, 2, GROUP, half_cycles), lambda g, *_: (0, 0, g, 0))
    payload_spec = pl.BlockSpec((groups, 2, GROUP, lanes), lambda g, *_: (0, 0, g, 0))
    payload = jax.ShapeDtypeStruct((groups, 2, slots, lanes), bf16)
    table_bytes = degrees * slots * half_cycles * 2
    legendre_cost = pl.CostEstimate(
        flops=1000 * table_bytes, bytes_accessed=table_bytes, transcendentals=0
    )
    tiled = lambda width, height: pltpu.VMEM((width // LANES, height, LANES), f32)
    degree_tiles = tiled(degrees, rows * PITCH)
    cycle_tiles = tiled(half_cycles, rows * PITCH)
    wide = tiled(half_cycles, degrees * PITCH)

    def chunk_spec(q):
        return pl.BlockSpec((CHUNK, 2, GROUP, degrees), lambda g, *_: (q, 0, g, 0))

    piece = jax.ShapeDtypeStruct((2, slots, lanes), bf16)
    piece_spec = pl.BlockSpec((2, GROUP, lanes), lambda g, *_: (0, g, 0))
    stack = pltpu.VMEM((groups, 2, GROUP, lanes), bf16)

    def synth(q, split_up):
        return pl.pallas_call(
            functools.partial(synth_kernel, slots=slots, split_up=split_up),
            name="synth",
            grid_spec=pltpu.PrefetchScalarGridSpec(
                num_scalar_prefetch=2,
                grid=(slots // GROUP,),
                in_specs=[chunk_spec(q), whole(root.shape), table_spec],
                out_specs=[piece_spec] * groups if split_up else payload_spec,
                scratch_shapes=[
                    degree_tiles,
                    wide,
                    pltpu.VMEM((GROUP, 2 * rows, half_cycles), f32),
                    cycle_tiles,
                    cycle_tiles,
                ]
                + ([stack] if split_up else []),
            ),
            out_shape=[piece] * groups if split_up else payload,
            compiler_params=params(),
            cost_estimate=legendre_cost,
        )(order_slots, me, probes_in, root, table)

    def analyse(q, returned, held, split_up):
        first = held is None
        arrays = list(returned) if split_up else [returned]
        return pl.pallas_call(
            functools.partial(
                analysis_kernel, slots=slots, sources=groups, split_up=split_up
            ),
            name="analyse",
            grid_spec=pltpu.PrefetchScalarGridSpec(
                num_scalar_prefetch=2,
                grid=(slots // GROUP,),
                in_specs=[whole(root.shape), table_spec]
                + [piece_spec if split_up else payload_spec] * len(arrays)
                + ([] if first else [pl.BlockSpec(memory_space=pl.ANY)]),
                out_specs=chunk_spec(q),
                scratch_shapes=[
                    cycle_tiles,
                    cycle_tiles,
                    wide,
                    pltpu.VMEM((GROUP, 4 * rows, half_cycles), bf16),
                    degree_tiles,
                ]
                + ([stack] if split_up else []),
            ),
            out_shape=jax.ShapeDtypeStruct((probes, 2, slots, degrees), f32),
            input_output_aliases={} if first else {4 + len(arrays): 0},
            compiler_params=params(),
            cost_estimate=legendre_cost,
        )(order_slots, me, root, table, *arrays, *([] if first else [held]))

    ahead_spec = pl.BlockSpec((1, 2 * TILE, orders_count), lambda i, h, o: (i, 0, 0))
    back_spec = pl.BlockSpec((2 * orders_count, TILE), lambda i, h, o: (0, i))
    grid_spec = pl.BlockSpec((TILE, part_lanes), lambda i, h, o: (i, 0))

    def fourier(received, tables, w_low, w_high, turn, chunk_beta, old, split_up):
        first = old is None
        ahead, back = tables
        square = jax.ShapeDtypeStruct((half_lon, part_lanes), f32)
        arrays = list(received) if split_up else [received]
        shapes = [piece] * groups if split_up else [payload]
        specs = [whole(shape.shape) for shape in shapes]
        return pl.pallas_call(
            functools.partial(
                fourier_kernel, first=first, sources=groups, split_up=split_up
            ),
            name="fourier",
            grid_spec=pltpu.PrefetchScalarGridSpec(
                num_scalar_prefetch=1,
                grid=(half_lon // TILE, parts),
                in_specs=[ahead_spec] * 2
                + [back_spec] * 2
                + [grid_spec] * 2
                + [whole((orders_count, 1)), whole((1, lanes))]
                + ([] if first else [grid_spec] * 2)
                + specs,
                out_specs=specs + [grid_spec, grid_spec],
                scratch_shapes=[pltpu.VMEM((parts, orders_count, part_lanes), bf16)] * 2
                + [pltpu.VMEM((parts, orders_count, part_lanes), f32)] * 2
                + [pltpu.VMEM((parts, 1, part_lanes), f32)]
                + ([pltpu.VMEM(payload.shape, bf16)] if split_up else []),
            ),
            out_shape=shapes + [square, square],
            input_output_aliases={} if first else {9: len(shapes), 10: len(shapes) + 1},
            compiler_params=params(),
            cost_estimate=pl.CostEstimate(
                flops=40 * half_lon * lanes * orders_count,
                bytes_accessed=16 * half_lon * orders_count + 16 * half_lon * part_lanes,
                transcendentals=0,
            ),
        )(
            me,
            *ahead,
            *back,
            w_low,
            w_high,
            turn,
            chunk_beta,
            *([] if first else old),
            *arrays,
        )

    def exchange(x, split_up):
        if split_up:
            pieces = [x[0]]
            for r in range(1, groups):
                pairs = [(i, i ^ r) for i in range(groups)]
                pieces.append(lax.ppermute(x[r], axes, pairs))
            return pieces
        return lax.all_to_all(x, axes, split_axis=0, concat_axis=0, tiled=True)

    local = jnp.arange(cycles, dtype=jnp.int32)
    flipped = jnp.where(south, cycles - 1 - local, local)
    cycle_index = (my_index * cycles + flipped).astype(f32)
    area = 2.0 * math.pi / lon_count * (math.pi / all_cycles) * jnp.sin(
        math.pi * (cycle_index + 0.5) / all_cycles
    )
    turned = jnp.where(south, jnp.flip(weight, 0), weight)
    turned = (area[:, None] * turned).T
    w_low = jnp.tile(turned[:half_lon], (1, PART))
    w_high = jnp.concatenate(
        [turned[half_lon : half_lon + 1], jnp.flip(turned[half_lon + 1 :], 0)], axis=0
    )
    w_high = jnp.tile(w_high, (1, PART))
    turn = (1 - 2 * (order_slots % 2)).astype(f32)[:, None]
    tables = half_tables(order_slots, lon_count)

    split_up = [q % 2 == 1 for q in range(chunks)]
    received = [exchange(synth(q, split_up[q]), split_up[q]) for q in range(chunks)]
    old, held = None, None
    returned = []
    for q in range(chunks):
        chunk_beta = jnp.repeat(beta[q * CHUNK : (q + 1) * CHUNK], cycles)[None, :]
        *analysed, low, high = fourier(
            received[q], tables, w_low, w_high, turn, chunk_beta, old, split_up[q]
        )
        old = (low, high)
        ready = analysed if split_up[q] else analysed[0]
        returned.append(exchange(ready, split_up[q]))
    for q in range(chunks):
        held = analyse(q, returned[q], held, split_up[q])

    lane_cycle = jnp.arange(part_lanes, dtype=jnp.int32) % cycles
    pick = (lane_cycle[None, :] == flipped[:, None]).astype(f32)
    sums = [
        lax.dot_general(
            pick, s, (((1,), (1,)), ((), ())), precision=lax.Precision.HIGHEST,
            preferred_element_type=f32,
        )
        for s in old
    ]
    natural = 2.0 * math.pi / lon_count * (math.pi / all_cycles) * jnp.sin(
        math.pi * ((my_index * cycles + local).astype(f32) + 0.5) / all_cycles
    )
    if lax.axis_size("probe") == 2:
        ahead_half = lax.axis_index("probe") == 0
        keep = jnp.where(ahead_half, sums[0], sums[1])
        give = jnp.where(ahead_half, sums[1], sums[0])
        half = (keep + lax.ppermute(give, "probe", [(0, 1), (1, 0)])) * natural[:, None]
        mirrored = jnp.concatenate([half[:, :1], jnp.flip(half[:, 1:], 1)], axis=1)
        gradient = jnp.where(ahead_half, half, mirrored)
    else:
        terms = jnp.concatenate([sums[0], sums[1][:, :1], jnp.flip(sums[1][:, 1:], 1)], axis=1)
        gradient = lax.psum_scatter(
            terms * natural[:, None], "probe", scatter_dimension=1, tiled=True
        )
    return (held, gradient)


def body(probes_in, root_spectrum, order_slots, legendre, weight, beta):
    degrees, slots, all_cycles = legendre.shape
    fits = (
        slots % GROUP == 0
        and degrees % DEPTH == 0
        and degrees == order_slots.shape[0]
        and all_cycles % (2 * LANES) == 0
        and (PART * weight.shape[0]) % LANES == 0
        and probes_in.shape[0] % CHUNK == 0
        and weight.shape[1] % (2 * TILE) == 0
        and lax.axis_size(("lat", "blk")) in (2, 4, 8, 16, 32)
    )
    chosen = fast_body if fits else plain_body
    return chosen(probes_in, root_spectrum, order_slots, legendre, weight, beta)


def solution(mesh):
    return jax.shard_map(
        body,
        mesh=mesh,
        in_specs=(
            P("probe", None, ("lat", "blk"), None),
            P(),
            P(),
            P(None, ("lat", "blk"), None),
            P(("lat", "blk"), None),
            P("probe"),
        ),
        out_specs=(P("probe", None, ("lat", "blk"), None), P(("lat", "blk"), "probe")),
        check_vma=False,
    )
```

```python
import functools
import math

import jax
import jax.numpy as jnp
from jax import lax
from jax.experimental import pallas as pl
from jax.experimental.pallas import tpu as pltpu
from jax.sharding import PartitionSpec as P


GROUP = 8
DEPTH = 128
CHUNK = 16
PART = 8
TILE = 256
VMEM_LIMIT = 60 * 2**20


def fourier_tables(orders, lon_count):
    longitude = jnp.arange(lon_count, dtype=jnp.int32)
    phase_idx = orders[:, None] * longitude[None, :] % lon_count
    angle = phase_idx.astype(jnp.float32) * (2.0 * math.pi / lon_count)
    twiddle = jnp.stack([jnp.cos(angle), jnp.sin(angle)])
    upper = twiddle.astype(jnp.bfloat16)
    lower = (twiddle - upper.astype(jnp.float32)).astype(jnp.bfloat16)
    return (upper, lower)


def cycle_work(spectra, inverse_tables, forward_tables, area, weight):
    grid_field = jnp.einsum(
        "pcmj,cmx->pjx", spectra, inverse_tables[0], preferred_element_type=jnp.float32
    )
    grid_field = grid_field + jnp.einsum(
        "pcmj,cmx->pjx", spectra, inverse_tables[1], preferred_element_type=jnp.float32
    )
    squares = grid_field * grid_field
    weighted = (area[None, :, None] * weight[None] * grid_field).astype(jnp.bfloat16)
    analysed = jnp.einsum(
        "pjx,cmx->pcmj", weighted, forward_tables[0], preferred_element_type=jnp.float32
    )
    analysed = analysed + jnp.einsum(
        "pjx,cmx->pcmj", weighted, forward_tables[1], preferred_element_type=jnp.float32
    )
    return (squares, analysed.astype(jnp.bfloat16))


def plain_body(probes_in, root_spectrum, order_slots, legendre, weight, beta):
    groups = lax.axis_size(("lat", "blk"))
    my_index = lax.axis_index(("lat", "blk"))
    cycle_count = weight.shape[0]
    lon_count = weight.shape[1]
    all_cycles = cycle_count * groups
    scaled = (probes_in.astype(jnp.float32) * root_spectrum).astype(jnp.bfloat16)
    spectra = jnp.einsum(
        "pcml,lmj->pcmj", scaled, legendre, preferred_element_type=jnp.float32
    ).astype(jnp.bfloat16)
    cycle_index = (my_index * cycle_count + jnp.arange(cycle_count, dtype=jnp.int32)).astype(
        jnp.float32
    )
    local_sines = jnp.sin(math.pi * (cycle_index + 0.5) / all_cycles)
    area = 2.0 * math.pi / lon_count * (math.pi / all_cycles) * local_sines
    forward_tables = fourier_tables(order_slots, lon_count)
    squares, analysed = cycle_work(
        lax.all_to_all(spectra, ("lat", "blk"), split_axis=3, concat_axis=2, tiled=True),
        forward_tables,
        forward_tables,
        area,
        weight,
    )
    returned = lax.all_to_all(analysed, ("lat", "blk"), split_axis=2, concat_axis=3, tiled=True)
    matvec = (
        jnp.einsum("pcmj,lmj->pcml", returned, legendre, preferred_element_type=jnp.float32)
        * root_spectrum
    )
    grad_terms = jnp.einsum("pjx,p->jx", squares, beta) * area[:, None]
    gradient = lax.psum_scatter(grad_terms, "probe", scatter_dimension=1, tiled=True)
    return (matvec, gradient)


def dot(a, b, dims=((1,), (0,))):
    return lax.dot_general(a, b, (dims, ((), ())), preferred_element_type=jnp.float32)


def split(x):
    upper = x.astype(jnp.bfloat16)
    return upper, (x - upper.astype(jnp.float32)).astype(jnp.bfloat16)


LANES = 128
PITCH = GROUP + 1


def every(slot, count):
    return pl.ds(slot, count, stride=PITCH)


def tiles(ref):
    return range(ref.shape[0])


def put(ref, rows, value):
    for t in tiles(ref):
        ref[t, rows, :] = value[:, t * LANES : (t + 1) * LANES]


def take(ref, rows):
    return jnp.concatenate([ref[t, rows, :] for t in tiles(ref)], axis=-1)


def spread_rows(tbl_ref, wide):
    @pl.loop(0, tbl_ref.shape[0] * 2 // DEPTH)
    def _(step):
        some = pl.ds(step * (DEPTH // 2), DEPTH // 2)
        for t in tiles(wide):
            piece = tbl_ref[some, :, :, t * LANES : (t + 1) * LANES].astype(jnp.float32)
            piece = piece.reshape(DEPTH, GROUP, LANES)
            for i in range(DEPTH):
                wide[t, pl.ds(step * (DEPTH * PITCH) + i * PITCH, GROUP), :] = piece[i]


def table_block(wide, step, slot):
    rows = pl.ds(step * (DEPTH * PITCH) + slot, DEPTH, stride=PITCH)
    return take(wide, rows).astype(jnp.bfloat16)


def slot_signs(orders_ref, base, shape):
    row = lax.broadcasted_iota(jnp.int32, shape, 0)
    odd = jnp.zeros(shape, jnp.int32)
    for slot in range(GROUP):
        odd = jnp.where(row == slot, orders_ref[base + slot] % 2, odd)
    return (1 - 2 * odd).astype(jnp.float32)


def visit(orders_ref, base, turn, pair, steps):
    first = orders_ref[base + 2 * pair] // DEPTH
    mine = turn < steps - first
    slot = 2 * pair + jnp.where(mine, 0, 1)
    return slot, jnp.where(mine, first + turn, turn - 1)


def even_degree(shape):
    return lax.broadcasted_iota(jnp.int32, shape, 1) % 2 == 0


def synth_kernel(orders_ref, me_ref, x_ref, root_ref, tbl_ref, *refs, slots, split_up):
    xs, wide, acc, ns, ss = refs[-6:-1] if split_up else refs[-5:]
    outs = refs[:-6] if split_up else refs[:1]
    out_ref = refs[-1] if split_up else outs[0]
    mine = me_ref[0]
    base = mine * slots + pl.program_id(0) * GROUP
    chunk = x_ref.shape[0]
    cycles = out_ref.shape[3] // chunk
    half = out_ref.shape[0] // 2
    rows = chunk * 2
    scaled = (x_ref[...].astype(jnp.float32) * root_ref[...]).astype(jnp.bfloat16)
    scaled = scaled.astype(jnp.float32).reshape(rows, GROUP, scaled.shape[-1])
    for i in range(rows):
        put(xs, pl.ds(i * PITCH, GROUP), scaled[i])
    acc[...] = jnp.zeros_like(acc)

    spread_rows(tbl_ref, wide)
    steps = tbl_ref.shape[0] * 2 // DEPTH

    @pl.loop(0, steps + 1)
    def _(turn):
        for pair in range(GROUP // 2):
            slot, step = visit(orders_ref, base, turn, pair, steps)
            x = xs[step, every(slot, rows), :]
            even = even_degree(x.shape)
            x = jnp.concatenate([jnp.where(even, x, 0.0), jnp.where(even, 0.0, x)], axis=0)
            table = table_block(wide, step, slot)
            acc[slot] += dot(x.astype(jnp.bfloat16), table)

    for slot in range(GROUP):
        even, odd = acc[slot, :rows], acc[slot, rows:]
        put(ns, every(slot, rows), even + odd)
        put(ss, every(slot, rows), even - odd)
    sign = slot_signs(orders_ref, base, (GROUP, acc.shape[-1]))
    for c in range(2):
        north, south = [], []
        for p in range(chunk):
            place = pl.ds((2 * p + c) * PITCH, GROUP)
            north.append(take(ns, place))
            south.append(take(ss, place) * sign)
        for d in range(half):
            for source, place in ((north, d), (south, 2 * half - 1 - d)):
                pieces = [piece[:, d * cycles : (d + 1) * cycles] for piece in source]
                at = place ^ mine if split_up else place
                out_ref[at, c] = jnp.concatenate(pieces, axis=-1).astype(jnp.bfloat16)
    if split_up:
        for r, out in enumerate(outs):
            out[...] = out_ref[r]


def analysis_kernel(orders_ref, me_ref, root_ref, tbl_ref, *refs, slots, sources, split_up):
    mine = me_ref[0]
    if split_up:
        q_ref = refs[-1]
        refs, parts = refs[:-1], refs[:sources]
        for r, part in enumerate(parts):
            q_ref[mine ^ r] = part[...]
    else:
        q_ref = refs[0]
    out_ref, plus, minus, wide, held, outs = refs[-6:]
    base = mine * slots + pl.program_id(0) * GROUP
    chunk = out_ref.shape[0]
    cycles = q_ref.shape[3] // chunk
    half = q_ref.shape[0] // 2
    rows = chunk * 2

    sign = slot_signs(orders_ref, base, (GROUP, half * cycles))
    for c in range(2):
        blocks = [q_ref[d, c].astype(jnp.float32) for d in range(2 * half)]
        for p in range(chunk):
            cut = slice(p * cycles, (p + 1) * cycles)
            north = jnp.concatenate([blocks[d][:, cut] for d in range(half)], axis=-1)
            other = [blocks[2 * half - 1 - d][:, cut] for d in range(half)]
            south = jnp.concatenate(other, axis=-1) * sign
            place = pl.ds((2 * p + c) * PITCH, GROUP)
            put(plus, place, north + south)
            put(minus, place, north - south)
    for slot in range(GROUP):
        both = [take(ref, every(slot, rows)) for ref in (plus, minus)]
        upper, lower = split(jnp.concatenate(both, axis=0))
        held[slot, : 2 * rows] = upper
        held[slot, 2 * rows :] = lower
    outs[...] = jnp.zeros_like(outs)

    spread_rows(tbl_ref, wide)
    steps = tbl_ref.shape[0] * 2 // DEPTH

    @pl.loop(0, steps + 1)
    def _(turn):
        for pair in range(GROUP // 2):
            slot, step = visit(orders_ref, base, turn, pair, steps)
            now = pl.ds(pl.multiple_of(step * DEPTH, DEPTH), DEPTH)
            table = table_block(wide, step, slot)
            both = dot(held[slot], table, ((1,), (1,)))
            both = both[: 2 * rows] + both[2 * rows :]
            even = even_degree((rows, DEPTH))
            chosen = jnp.where(even, both[:rows], both[rows:])
            outs[step, every(slot, rows), :] = chosen * root_ref[:, now]

    for p in range(chunk):
        for c in range(2):
            out_ref[p, c] = take(outs, pl.ds((2 * p + c) * PITCH, GROUP))


def fourier_kernel(me_ref, *refs, first, sources, split_up):
    ahead_cos, ahead_sin, back_cos, back_sin, w_low, w_high, turn_ref, beta_ref = refs[:8]
    old_low, old_high = (None, None) if first else refs[8:10]
    refs = refs[8:] if first else refs[10:]
    mine_at = me_ref[0]
    step, part = pl.program_id(0), pl.program_id(1)
    if split_up:
        arrived, sent = refs[:sources], refs[sources : 2 * sources]
        g_low, g_high, rc, rs, acc_c, acc_s, middle, r_ref = refs[2 * sources :]

        @pl.when((step == 0) & (part == 0))
        def _():
            for r, piece in enumerate(arrived):
                r_ref[mine_at ^ r] = piece[...]

    else:
        r_ref, out_ref, g_low, g_high, rc, rs, acc_c, acc_s, middle = refs
    slots = r_ref.shape[2]
    tile, lanes = g_low.shape
    count = acc_c.shape[1]
    mine = pl.ds(pl.multiple_of(part * lanes, LANES), lanes)

    @pl.when(step == 0)
    def _():
        for pair in range(sources // 2):
            for c, place in ((0, rc), (1, rs)):
                both = [r_ref[2 * pair + i, c, :, mine].astype(jnp.float32) for i in range(2)]
                place[part, pl.ds(2 * slots * pair, 2 * slots)] = jnp.concatenate(
                    both, axis=0
                ).astype(jnp.bfloat16)
        turned = turn_ref[...] * rc[part].astype(jnp.float32)
        mid = jnp.sum(turned, axis=0, keepdims=True)
        middle[part] = mid
        w_mid = (w_high[pl.ds(0, 1), :] * mid).astype(jnp.bfloat16).astype(jnp.float32)
        acc_c[part] = turn_ref[...] * w_mid
        acc_s[part] = jnp.zeros_like(acc_s[part])

    c_part = dot(ahead_cos[0], rc[part])
    c_part = c_part[:tile] + c_part[tile:]
    s_part = dot(ahead_sin[0], rs[part])
    s_part = s_part[:tile] + s_part[tile:]
    low = c_part + s_part
    row = lax.broadcasted_iota(jnp.int32, low.shape, 0) + step * tile
    high = jnp.where(row == 0, middle[part], c_part - s_part)
    beta = beta_ref[:, mine]
    low_sq = beta * (low * low)
    high_sq = beta * (high * high)

    @pl.when(part == 0)
    def _():
        g_low[...] = low_sq if first else old_low[...] + low_sq
        g_high[...] = high_sq if first else old_high[...] + high_sq

    @pl.when(part > 0)
    def _():
        g_low[...] += low_sq
        g_high[...] += high_sq

    low = (w_low[...] * low).astype(jnp.bfloat16).astype(jnp.float32)
    high = jnp.where(row == 0, 0.0, w_high[...] * high).astype(jnp.bfloat16).astype(jnp.float32)
    for folded, back, acc in ((low + high, back_cos, acc_c), (low - high, back_sin, acc_s)):
        upper, lower = split(folded)
        both = dot(back[...], upper)
        acc[part] += both[:count] + both[count:] + dot(back[pl.ds(0, count), :], lower)

    @pl.when(step == pl.num_programs(0) - 1)
    def _():
        for d in range(sources):
            for c, acc in ((0, acc_c), (1, acc_s)):
                if split_up:
                    start = pl.multiple_of((mine_at ^ d) * slots, GROUP)
                    sent[d][c, :, mine] = acc[part, pl.ds(start, slots)].astype(jnp.bfloat16)
                else:
                    found = acc[part, pl.ds(slots * d, slots)]
                    out_ref[d, c, :, mine] = found.astype(jnp.bfloat16)


def half_tables(orders, lon_count):
    half = lon_count // 2

    def trig(points):
        idx = orders[:, None] * points[None, :] % lon_count
        angle = idx.astype(jnp.float32) * (2.0 * math.pi / lon_count)
        return lax.optimization_barrier((jnp.cos(angle), jnp.sin(angle)))

    def joined(parts, shape, axes):
        (ca, sa), (cb, sb) = parts
        ca, sa = (t[axes[0]] for t in (ca, sa))
        cb, sb = (t[axes[1]] for t in (cb, sb))
        cosine = (ca * cb - sa * sb).reshape(shape)
        sine = (sa * cb + ca * sb).reshape(shape)
        return split(cosine) + split(sine)

    count = orders.shape[0]
    fine = 128
    coarse_points = jnp.arange(half // fine, dtype=jnp.int32) * fine
    fine_points = jnp.arange(fine, dtype=jnp.int32)
    coarse, small = trig(coarse_points), trig(fine_points)
    every = slice(None)
    back = joined((coarse, small), (count, half), ((every, every, None), (every, None, every)))
    coarse_t = tuple(t.T for t in coarse)
    small_t = tuple(t.T for t in small)
    ahead = joined((coarse_t, small_t), (half, count), ((every, None, every), (None, every, every)))
    tiled = [t.reshape(half // TILE, TILE, count) for t in ahead]
    ahead = [jnp.concatenate(tiled[i : i + 2], axis=1) for i in (0, 2)]
    back = [jnp.concatenate(back[i : i + 2], axis=0) for i in (0, 2)]
    return ahead, back


def fast_body(probes_in, root_spectrum, order_slots, legendre, weight, beta):
    axes = ("lat", "blk")
    groups = lax.axis_size(axes)
    my_index = lax.axis_index(axes)
    cycles, lon_count = weight.shape
    half_lon = lon_count // 2
    all_cycles = cycles * groups
    half_cycles = all_cycles // 2
    degrees, slots = legendre.shape[:2]
    orders_count = order_slots.shape[0]
    probes = probes_in.shape[0]
    chunks = probes // CHUNK
    lanes = CHUNK * cycles
    part_lanes = PART * cycles
    parts = CHUNK // PART
    south = my_index >= groups // 2
    params = functools.partial(pltpu.CompilerParams, vmem_limit_bytes=VMEM_LIMIT)
    f32, bf16 = jnp.float32, jnp.bfloat16

    me = my_index[None].astype(jnp.int32)
    root = root_spectrum[None, :]
    table = legendre.reshape(degrees // 2, 2, slots, all_cycles)
    rows = CHUNK * 2
    whole = lambda shape: pl.BlockSpec(shape, lambda *_: (0,) * len(shape))
    table_spec = pl.BlockSpec((degrees // 2, 2, GROUP, half_cycles), lambda g, *_: (0, 0, g, 0))
    payload_spec = pl.BlockSpec((groups, 2, GROUP, lanes), lambda g, *_: (0, 0, g, 0))
    payload = jax.ShapeDtypeStruct((groups, 2, slots, lanes), bf16)
    table_bytes = degrees * slots * half_cycles * 2
    legendre_cost = pl.CostEstimate(
        flops=1000 * table_bytes, bytes_accessed=table_bytes, transcendentals=0
    )
    tiled = lambda width, height: pltpu.VMEM((width // LANES, height, LANES), f32)
    degree_tiles = tiled(degrees, rows * PITCH)
    cycle_tiles = tiled(half_cycles, rows * PITCH)
    wide = tiled(half_cycles, degrees * PITCH)

    def chunk_spec(q):
        return pl.BlockSpec((CHUNK, 2, GROUP, degrees), lambda g, *_: (q, 0, g, 0))

    piece = jax.ShapeDtypeStruct((2, slots, lanes), bf16)
    piece_spec = pl.BlockSpec((2, GROUP, lanes), lambda g, *_: (0, g, 0))
    stack = pltpu.VMEM((groups, 2, GROUP, lanes), bf16)

    def synth(q, split_up):
        return pl.pallas_call(
            functools.partial(synth_kernel, slots=slots, split_up=split_up),
            name="synth",
            grid_spec=pltpu.PrefetchScalarGridSpec(
                num_scalar_prefetch=2,
                grid=(slots // GROUP,),
                in_specs=[chunk_spec(q), whole(root.shape), table_spec],
                out_specs=[piece_spec] * groups if split_up else payload_spec,
                scratch_shapes=[
                    degree_tiles,
                    wide,
                    pltpu.VMEM((GROUP, 2 * rows, half_cycles), f32),
                    cycle_tiles,
                    cycle_tiles,
                ]
                + ([stack] if split_up else []),
            ),
            out_shape=[piece] * groups if split_up else payload,
            compiler_params=params(),
            cost_estimate=legendre_cost,
        )(order_slots, me, probes_in, root, table)

    def analyse(q, returned, held, split_up):
        first = held is None
        arrays = list(returned) if split_up else [returned]
        return pl.pallas_call(
            functools.partial(
                analysis_kernel, slots=slots, sources=groups, split_up=split_up
            ),
            name="analyse",
            grid_spec=pltpu.PrefetchScalarGridSpec(
                num_scalar_prefetch=2,
                grid=(slots // GROUP,),
                in_specs=[whole(root.shape), table_spec]
                + [piece_spec if split_up else payload_spec] * len(arrays)
                + ([] if first else [pl.BlockSpec(memory_space=pl.ANY)]),
                out_specs=chunk_spec(q),
                scratch_shapes=[
                    cycle_tiles,
                    cycle_tiles,
                    wide,
                    pltpu.VMEM((GROUP, 4 * rows, half_cycles), bf16),
                    degree_tiles,
                ]
                + ([stack] if split_up else []),
            ),
            out_shape=jax.ShapeDtypeStruct((probes, 2, slots, degrees), f32),
            input_output_aliases={} if first else {4 + len(arrays): 0},
            compiler_params=params(),
            cost_estimate=legendre_cost,
        )(order_slots, me, root, table, *arrays, *([] if first else [held]))

    ahead_spec = pl.BlockSpec((1, 2 * TILE, orders_count), lambda i, h, o: (i, 0, 0))
    back_spec = pl.BlockSpec((2 * orders_count, TILE), lambda i, h, o: (0, i))
    grid_spec = pl.BlockSpec((TILE, part_lanes), lambda i, h, o: (i, 0))

    def fourier(received, tables, w_low, w_high, turn, chunk_beta, old, split_up):
        first = old is None
        ahead, back = tables
        square = jax.ShapeDtypeStruct((half_lon, part_lanes), f32)
        arrays = list(received) if split_up else [received]
        shapes = [piece] * groups if split_up else [payload]
        specs = [whole(shape.shape) for shape in shapes]
        return pl.pallas_call(
            functools.partial(
                fourier_kernel, first=first, sources=groups, split_up=split_up
            ),
            name="fourier",
            grid_spec=pltpu.PrefetchScalarGridSpec(
                num_scalar_prefetch=1,
                grid=(half_lon // TILE, parts),
                in_specs=[ahead_spec] * 2
                + [back_spec] * 2
                + [grid_spec] * 2
                + [whole((orders_count, 1)), whole((1, lanes))]
                + ([] if first else [grid_spec] * 2)
                + specs,
                out_specs=specs + [grid_spec, grid_spec],
                scratch_shapes=[pltpu.VMEM((parts, orders_count, part_lanes), bf16)] * 2
                + [pltpu.VMEM((parts, orders_count, part_lanes), f32)] * 2
                + [pltpu.VMEM((parts, 1, part_lanes), f32)]
                + ([pltpu.VMEM(payload.shape, bf16)] if split_up else []),
            ),
            out_shape=shapes + [square, square],
            input_output_aliases={} if first else {9: len(shapes), 10: len(shapes) + 1},
            compiler_params=params(),
            cost_estimate=pl.CostEstimate(
                flops=40 * half_lon * lanes * orders_count,
                bytes_accessed=16 * half_lon * orders_count + 16 * half_lon * part_lanes,
                transcendentals=0,
            ),
        )(
            me,
            *ahead,
            *back,
            w_low,
            w_high,
            turn,
            chunk_beta,
            *([] if first else old),
            *arrays,
        )

    def exchange(x, split_up):
        if split_up:
            middle_bit = lax.axis_size("blk") // 2
            pieces = list(x)
            for r in sorted(range(1, groups), key=lambda r: (not r & middle_bit, r)):
                pairs = [(i, i ^ r) for i in range(groups)]
                pieces[r] = lax.ppermute(x[r], axes, pairs)
            return pieces
        return lax.all_to_all(x, axes, split_axis=0, concat_axis=0, tiled=True)

    local = jnp.arange(cycles, dtype=jnp.int32)
    flipped = jnp.where(south, cycles - 1 - local, local)
    cycle_index = (my_index * cycles + flipped).astype(f32)
    area = 2.0 * math.pi / lon_count * (math.pi / all_cycles) * jnp.sin(
        math.pi * (cycle_index + 0.5) / all_cycles
    )
    turned = jnp.where(south, jnp.flip(weight, 0), weight)
    turned = (area[:, None] * turned).T
    w_low = jnp.tile(turned[:half_lon], (1, PART))
    w_high = jnp.concatenate(
        [turned[half_lon : half_lon + 1], jnp.flip(turned[half_lon + 1 :], 0)], axis=0
    )
    w_high = jnp.tile(w_high, (1, PART))
    turn = (1 - 2 * (order_slots % 2)).astype(f32)[:, None]
    tables = half_tables(order_slots, lon_count)

    split_up = [q % 2 == 1 for q in range(chunks)]
    received = []
    for q in range(chunks):
        spectra = synth(q, split_up[q])
        if split_up[q]:
            spectra, tables, w_low, w_high = lax.optimization_barrier(
                (spectra, tables, w_low, w_high)
            )
        received.append(exchange(spectra, split_up[q]))
    old, held = None, None
    returned = []
    for q in range(chunks):
        chunk_beta = jnp.repeat(beta[q * CHUNK : (q + 1) * CHUNK], cycles)[None, :]
        *analysed, low, high = fourier(
            received[q], tables, w_low, w_high, turn, chunk_beta, old, split_up[q]
        )
        old = (low, high)
        ready = analysed if split_up[q] else analysed[0]
        returned.append(exchange(ready, split_up[q]))
    for q in range(chunks):
        held = analyse(q, returned[q], held, split_up[q])

    lane_cycle = jnp.arange(part_lanes, dtype=jnp.int32) % cycles
    pick = (lane_cycle[None, :] == flipped[:, None]).astype(f32)
    sums = [
        lax.dot_general(
            pick, s, (((1,), (1,)), ((), ())), precision=lax.Precision.HIGHEST,
            preferred_element_type=f32,
        )
        for s in old
    ]
    natural = 2.0 * math.pi / lon_count * (math.pi / all_cycles) * jnp.sin(
        math.pi * ((my_index * cycles + local).astype(f32) + 0.5) / all_cycles
    )
    if lax.axis_size("probe") == 2:
        ahead_half = lax.axis_index("probe") == 0
        keep = jnp.where(ahead_half, sums[0], sums[1])
        give = jnp.where(ahead_half, sums[1], sums[0])
        half = (keep + lax.ppermute(give, "probe", [(0, 1), (1, 0)])) * natural[:, None]
        mirrored = jnp.concatenate([half[:, :1], jnp.flip(half[:, 1:], 1)], axis=1)
        gradient = jnp.where(ahead_half, half, mirrored)
    else:
        terms = jnp.concatenate([sums[0], sums[1][:, :1], jnp.flip(sums[1][:, 1:], 1)], axis=1)
        gradient = lax.psum_scatter(
            terms * natural[:, None], "probe", scatter_dimension=1, tiled=True
        )
    return (held, gradient)


def body(probes_in, root_spectrum, order_slots, legendre, weight, beta):
    degrees, slots, all_cycles = legendre.shape
    fits = (
        slots % GROUP == 0
        and degrees % DEPTH == 0
        and degrees == order_slots.shape[0]
        and all_cycles % (2 * LANES) == 0
        and (PART * weight.shape[0]) % LANES == 0
        and probes_in.shape[0] % CHUNK == 0
        and weight.shape[1] % (2 * TILE) == 0
        and lax.axis_size(("lat", "blk")) in (2, 4, 8, 16, 32)
    )
    chosen = fast_body if fits else plain_body
    return chosen(probes_in, root_spectrum, order_slots, legendre, weight, beta)


def solution(mesh):
    return jax.shard_map(
        body,
        mesh=mesh,
        in_specs=(
            P("probe", None, ("lat", "blk"), None),
            P(),
            P(),
            P(None, ("lat", "blk"), None),
            P(("lat", "blk"), None),
            P("probe"),
        ),
        out_specs=(P("probe", None, ("lat", "blk"), None), P(("lat", "blk"), "probe")),
        check_vma=False,
    )
```

```python
import functools
import math

import jax
import jax.numpy as jnp
from jax import lax
from jax.experimental import pallas as pl
from jax.experimental.pallas import tpu as pltpu
from jax.sharding import PartitionSpec as P


GROUP = 8
DEPTH = 128
CHUNK = 16
PART = 8
TILE = 256
VMEM_LIMIT = 60 * 2**20


def fourier_tables(orders, lon_count):
    longitude = jnp.arange(lon_count, dtype=jnp.int32)
    phase_idx = orders[:, None] * longitude[None, :] % lon_count
    angle = phase_idx.astype(jnp.float32) * (2.0 * math.pi / lon_count)
    twiddle = jnp.stack([jnp.cos(angle), jnp.sin(angle)])
    upper = twiddle.astype(jnp.bfloat16)
    lower = (twiddle - upper.astype(jnp.float32)).astype(jnp.bfloat16)
    return (upper, lower)


def cycle_work(spectra, inverse_tables, forward_tables, area, weight):
    grid_field = jnp.einsum(
        "pcmj,cmx->pjx", spectra, inverse_tables[0], preferred_element_type=jnp.float32
    )
    grid_field = grid_field + jnp.einsum(
        "pcmj,cmx->pjx", spectra, inverse_tables[1], preferred_element_type=jnp.float32
    )
    squares = grid_field * grid_field
    weighted = (area[None, :, None] * weight[None] * grid_field).astype(jnp.bfloat16)
    analysed = jnp.einsum(
        "pjx,cmx->pcmj", weighted, forward_tables[0], preferred_element_type=jnp.float32
    )
    analysed = analysed + jnp.einsum(
        "pjx,cmx->pcmj", weighted, forward_tables[1], preferred_element_type=jnp.float32
    )
    return (squares, analysed.astype(jnp.bfloat16))


def plain_body(probes_in, root_spectrum, order_slots, legendre, weight, beta):
    groups = lax.axis_size(("lat", "blk"))
    my_index = lax.axis_index(("lat", "blk"))
    cycle_count = weight.shape[0]
    lon_count = weight.shape[1]
    all_cycles = cycle_count * groups
    scaled = (probes_in.astype(jnp.float32) * root_spectrum).astype(jnp.bfloat16)
    spectra = jnp.einsum(
        "pcml,lmj->pcmj", scaled, legendre, preferred_element_type=jnp.float32
    ).astype(jnp.bfloat16)
    cycle_index = (my_index * cycle_count + jnp.arange(cycle_count, dtype=jnp.int32)).astype(
        jnp.float32
    )
    local_sines = jnp.sin(math.pi * (cycle_index + 0.5) / all_cycles)
    area = 2.0 * math.pi / lon_count * (math.pi / all_cycles) * local_sines
    forward_tables = fourier_tables(order_slots, lon_count)
    squares, analysed = cycle_work(
        lax.all_to_all(spectra, ("lat", "blk"), split_axis=3, concat_axis=2, tiled=True),
        forward_tables,
        forward_tables,
        area,
        weight,
    )
    returned = lax.all_to_all(analysed, ("lat", "blk"), split_axis=2, concat_axis=3, tiled=True)
    matvec = (
        jnp.einsum("pcmj,lmj->pcml", returned, legendre, preferred_element_type=jnp.float32)
        * root_spectrum
    )
    grad_terms = jnp.einsum("pjx,p->jx", squares, beta) * area[:, None]
    gradient = lax.psum_scatter(grad_terms, "probe", scatter_dimension=1, tiled=True)
    return (matvec, gradient)


def dot(a, b, dims=((1,), (0,))):
    return lax.dot_general(a, b, (dims, ((), ())), preferred_element_type=jnp.float32)


def split(x):
    upper = x.astype(jnp.bfloat16)
    return upper, (x - upper.astype(jnp.float32)).astype(jnp.bfloat16)


LANES = 128
PITCH = GROUP + 1


def every(slot, count):
    return pl.ds(slot, count, stride=PITCH)


def tiles(ref):
    return range(ref.shape[0])


def put(ref, rows, value):
    for t in tiles(ref):
        ref[t, rows, :] = value[:, t * LANES : (t + 1) * LANES]


def take(ref, rows):
    return jnp.concatenate([ref[t, rows, :] for t in tiles(ref)], axis=-1)


def spread_rows(tbl_ref, wide):
    @pl.loop(0, tbl_ref.shape[0] * 2 // DEPTH)
    def _(step):
        some = pl.ds(step * (DEPTH // 2), DEPTH // 2)
        for t in tiles(wide):
            piece = tbl_ref[some, :, :, t * LANES : (t + 1) * LANES].astype(jnp.float32)
            piece = piece.reshape(DEPTH, GROUP, LANES)
            for i in range(DEPTH):
                wide[t, pl.ds(step * (DEPTH * PITCH) + i * PITCH, GROUP), :] = piece[i]


def table_block(wide, step, slot):
    rows = pl.ds(step * (DEPTH * PITCH) + slot, DEPTH, stride=PITCH)
    return take(wide, rows).astype(jnp.bfloat16)


def slot_signs(orders_ref, base, shape):
    row = lax.broadcasted_iota(jnp.int32, shape, 0)
    odd = jnp.zeros(shape, jnp.int32)
    for slot in range(GROUP):
        odd = jnp.where(row == slot, orders_ref[base + slot] % 2, odd)
    return (1 - 2 * odd).astype(jnp.float32)


def visit(orders_ref, base, turn, pair, steps):
    first = orders_ref[base + 2 * pair] // DEPTH
    mine = turn < steps - first
    slot = 2 * pair + jnp.where(mine, 0, 1)
    return slot, jnp.where(mine, first + turn, turn - 1)


def even_degree(shape):
    return lax.broadcasted_iota(jnp.int32, shape, 1) % 2 == 0


def synth_kernel(orders_ref, me_ref, x_ref, root_ref, tbl_ref, *refs, slots, split_up):
    xs, wide, acc, ns, ss = refs[-6:-1] if split_up else refs[-5:]
    outs = refs[:-6] if split_up else refs[:1]
    out_ref = refs[-1] if split_up else outs[0]
    mine = me_ref[0]
    base = mine * slots + pl.program_id(0) * GROUP
    chunk = x_ref.shape[0]
    cycles = out_ref.shape[3] // chunk
    half = out_ref.shape[0] // 2
    rows = chunk * 2
    scaled = (x_ref[...].astype(jnp.float32) * root_ref[...]).astype(jnp.bfloat16)
    scaled = scaled.astype(jnp.float32).reshape(rows, GROUP, scaled.shape[-1])
    for i in range(rows):
        put(xs, pl.ds(i * PITCH, GROUP), scaled[i])
    acc[...] = jnp.zeros_like(acc)

    spread_rows(tbl_ref, wide)
    steps = tbl_ref.shape[0] * 2 // DEPTH

    @pl.loop(0, steps + 1)
    def _(turn):
        for pair in range(GROUP // 2):
            slot, step = visit(orders_ref, base, turn, pair, steps)
            x = xs[step, every(slot, rows), :]
            even = even_degree(x.shape)
            x = jnp.concatenate([jnp.where(even, x, 0.0), jnp.where(even, 0.0, x)], axis=0)
            table = table_block(wide, step, slot)
            acc[slot] += dot(x.astype(jnp.bfloat16), table)

    for slot in range(GROUP):
        even, odd = acc[slot, :rows], acc[slot, rows:]
        put(ns, every(slot, rows), even + odd)
        put(ss, every(slot, rows), even - odd)
    sign = slot_signs(orders_ref, base, (GROUP, acc.shape[-1]))
    for c in range(2):
        north, south = [], []
        for p in range(chunk):
            place = pl.ds((2 * p + c) * PITCH, GROUP)
            north.append(take(ns, place))
            south.append(take(ss, place) * sign)
        for d in range(half):
            for source, place in ((north, d), (south, 2 * half - 1 - d)):
                pieces = [piece[:, d * cycles : (d + 1) * cycles] for piece in source]
                at = place ^ mine if split_up else place
                out_ref[at, c] = jnp.concatenate(pieces, axis=-1).astype(jnp.bfloat16)
    if split_up:
        for r, out in enumerate(outs):
            out[...] = out_ref[r]


def analysis_kernel(
    orders_ref, me_ref, root_ref, tbl_ref, *refs, slots, begin, sources, split_up
):
    mine = me_ref[0]
    if split_up:
        q_ref = refs[-1]
        refs, parts = refs[:-1], refs[:sources]
        for r, part in enumerate(parts):
            q_ref[mine ^ r] = part[...]
    else:
        q_ref = refs[0]
    out_ref, plus, minus, wide, held, outs = refs[-6:]
    base = mine * slots + begin + pl.program_id(0) * GROUP
    chunk = out_ref.shape[0]
    cycles = q_ref.shape[3] // chunk
    half = q_ref.shape[0] // 2
    rows = chunk * 2

    sign = slot_signs(orders_ref, base, (GROUP, half * cycles))
    for c in range(2):
        blocks = [q_ref[d, c].astype(jnp.float32) for d in range(2 * half)]
        for p in range(chunk):
            cut = slice(p * cycles, (p + 1) * cycles)
            north = jnp.concatenate([blocks[d][:, cut] for d in range(half)], axis=-1)
            other = [blocks[2 * half - 1 - d][:, cut] for d in range(half)]
            south = jnp.concatenate(other, axis=-1) * sign
            place = pl.ds((2 * p + c) * PITCH, GROUP)
            put(plus, place, north + south)
            put(minus, place, north - south)
    for slot in range(GROUP):
        both = [take(ref, every(slot, rows)) for ref in (plus, minus)]
        upper, lower = split(jnp.concatenate(both, axis=0))
        held[slot, : 2 * rows] = upper
        held[slot, 2 * rows :] = lower
    outs[...] = jnp.zeros_like(outs)

    spread_rows(tbl_ref, wide)
    steps = tbl_ref.shape[0] * 2 // DEPTH

    @pl.loop(0, steps + 1)
    def _(turn):
        for pair in range(GROUP // 2):
            slot, step = visit(orders_ref, base, turn, pair, steps)
            now = pl.ds(pl.multiple_of(step * DEPTH, DEPTH), DEPTH)
            table = table_block(wide, step, slot)
            both = dot(held[slot], table, ((1,), (1,)))
            both = both[: 2 * rows] + both[2 * rows :]
            even = even_degree((rows, DEPTH))
            chosen = jnp.where(even, both[:rows], both[rows:])
            outs[step, every(slot, rows), :] = chosen * root_ref[:, now]

    for p in range(chunk):
        for c in range(2):
            out_ref[p, c] = take(outs, pl.ds((2 * p + c) * PITCH, GROUP))


def fourier_kernel(me_ref, *refs, first, sources, split_up, cuts):
    ahead_cos, ahead_sin, back_cos, back_sin, w_low, w_high, turn_ref, beta_ref = refs[:8]
    old_low, old_high = (None, None) if first else refs[8:10]
    refs = refs[8:] if first else refs[10:]
    mine_at = me_ref[0]
    step, part = pl.program_id(0), pl.program_id(1)
    if split_up:
        arrived, sent = refs[:sources], refs[sources:-8]
        g_low, g_high, rc, rs, acc_c, acc_s, middle, r_ref = refs[-8:]

        @pl.when((step == 0) & (part == 0))
        def _():
            for r, piece in enumerate(arrived):
                r_ref[mine_at ^ r] = piece[...]

    else:
        r_ref, out_ref, g_low, g_high, rc, rs, acc_c, acc_s, middle = refs
    slots = r_ref.shape[2]
    tile, lanes = g_low.shape
    count = acc_c.shape[1]
    mine = pl.ds(pl.multiple_of(part * lanes, LANES), lanes)

    @pl.when(step == 0)
    def _():
        for pair in range(sources // 2):
            for c, place in ((0, rc), (1, rs)):
                both = [r_ref[2 * pair + i, c, :, mine].astype(jnp.float32) for i in range(2)]
                place[part, pl.ds(2 * slots * pair, 2 * slots)] = jnp.concatenate(
                    both, axis=0
                ).astype(jnp.bfloat16)
        turned = turn_ref[...] * rc[part].astype(jnp.float32)
        mid = jnp.sum(turned, axis=0, keepdims=True)
        middle[part] = mid
        w_mid = (w_high[pl.ds(0, 1), :] * mid).astype(jnp.bfloat16).astype(jnp.float32)
        acc_c[part] = turn_ref[...] * w_mid
        acc_s[part] = jnp.zeros_like(acc_s[part])

    c_part = dot(ahead_cos[0], rc[part])
    c_part = c_part[:tile] + c_part[tile:]
    s_part = dot(ahead_sin[0], rs[part])
    s_part = s_part[:tile] + s_part[tile:]
    low = c_part + s_part
    row = lax.broadcasted_iota(jnp.int32, low.shape, 0) + step * tile
    high = jnp.where(row == 0, middle[part], c_part - s_part)
    beta = beta_ref[:, mine]
    low_sq = beta * (low * low)
    high_sq = beta * (high * high)

    @pl.when(part == 0)
    def _():
        g_low[...] = low_sq if first else old_low[...] + low_sq
        g_high[...] = high_sq if first else old_high[...] + high_sq

    @pl.when(part > 0)
    def _():
        g_low[...] += low_sq
        g_high[...] += high_sq

    low = (w_low[...] * low).astype(jnp.bfloat16).astype(jnp.float32)
    high = jnp.where(row == 0, 0.0, w_high[...] * high).astype(jnp.bfloat16).astype(jnp.float32)
    for folded, back, acc in ((low + high, back_cos, acc_c), (low - high, back_sin, acc_s)):
        upper, lower = split(folded)
        both = dot(back[...], upper)
        acc[part] += both[:count] + both[count:] + dot(back[pl.ds(0, count), :], lower)

    @pl.when(step == pl.num_programs(0) - 1)
    def _():
        for d in range(sources):
            for c, acc in ((0, acc_c), (1, acc_s)):
                if split_up:
                    for k, (begin, size) in enumerate(cuts):
                        start = pl.multiple_of((mine_at ^ d) * slots + begin, GROUP)
                        found = acc[part, pl.ds(start, size)]
                        sent[k * sources + d][c, :, mine] = found.astype(jnp.bfloat16)
                else:
                    found = acc[part, pl.ds(slots * d, slots)]
                    out_ref[d, c, :, mine] = found.astype(jnp.bfloat16)


def half_tables(orders, lon_count):
    half = lon_count // 2

    def trig(points):
        idx = orders[:, None] * points[None, :] % lon_count
        angle = idx.astype(jnp.float32) * (2.0 * math.pi / lon_count)
        return lax.optimization_barrier((jnp.cos(angle), jnp.sin(angle)))

    def joined(parts, shape, axes):
        (ca, sa), (cb, sb) = parts
        ca, sa = (t[axes[0]] for t in (ca, sa))
        cb, sb = (t[axes[1]] for t in (cb, sb))
        cosine = (ca * cb - sa * sb).reshape(shape)
        sine = (sa * cb + ca * sb).reshape(shape)
        return split(cosine) + split(sine)

    count = orders.shape[0]
    fine = 128
    coarse_points = jnp.arange(half // fine, dtype=jnp.int32) * fine
    fine_points = jnp.arange(fine, dtype=jnp.int32)
    coarse, small = trig(coarse_points), trig(fine_points)
    every = slice(None)
    back = joined((coarse, small), (count, half), ((every, every, None), (every, None, every)))
    coarse_t = tuple(t.T for t in coarse)
    small_t = tuple(t.T for t in small)
    ahead = joined((coarse_t, small_t), (half, count), ((every, None, every), (None, every, every)))
    tiled = [t.reshape(half // TILE, TILE, count) for t in ahead]
    ahead = [jnp.concatenate(tiled[i : i + 2], axis=1) for i in (0, 2)]
    back = [jnp.concatenate(back[i : i + 2], axis=0) for i in (0, 2)]
    return ahead, back


def fast_body(probes_in, root_spectrum, order_slots, legendre, weight, beta):
    axes = ("lat", "blk")
    groups = lax.axis_size(axes)
    my_index = lax.axis_index(axes)
    cycles, lon_count = weight.shape
    half_lon = lon_count // 2
    all_cycles = cycles * groups
    half_cycles = all_cycles // 2
    degrees, slots = legendre.shape[:2]
    orders_count = order_slots.shape[0]
    probes = probes_in.shape[0]
    chunks = probes // CHUNK
    lanes = CHUNK * cycles
    part_lanes = PART * cycles
    parts = CHUNK // PART
    south = my_index >= groups // 2
    params = functools.partial(pltpu.CompilerParams, vmem_limit_bytes=VMEM_LIMIT)
    f32, bf16 = jnp.float32, jnp.bfloat16

    me = my_index[None].astype(jnp.int32)
    root = root_spectrum[None, :]
    table = legendre.reshape(degrees // 2, 2, slots, all_cycles)
    rows = CHUNK * 2
    whole = lambda shape: pl.BlockSpec(shape, lambda *_: (0,) * len(shape))
    table_spec = pl.BlockSpec((degrees // 2, 2, GROUP, half_cycles), lambda g, *_: (0, 0, g, 0))
    payload_spec = pl.BlockSpec((groups, 2, GROUP, lanes), lambda g, *_: (0, 0, g, 0))
    payload = jax.ShapeDtypeStruct((groups, 2, slots, lanes), bf16)
    table_bytes = degrees * slots * half_cycles * 2
    legendre_cost = pl.CostEstimate(
        flops=1000 * table_bytes, bytes_accessed=table_bytes, transcendentals=0
    )
    tiled = lambda width, height: pltpu.VMEM((width // LANES, height, LANES), f32)
    degree_tiles = tiled(degrees, rows * PITCH)
    cycle_tiles = tiled(half_cycles, rows * PITCH)
    wide = tiled(half_cycles, degrees * PITCH)

    def chunk_spec(q):
        return pl.BlockSpec((CHUNK, 2, GROUP, degrees), lambda g, *_: (q, 0, g, 0))

    piece = jax.ShapeDtypeStruct((2, slots, lanes), bf16)
    piece_spec = pl.BlockSpec((2, GROUP, lanes), lambda g, *_: (0, g, 0))
    stack = pltpu.VMEM((groups, 2, GROUP, lanes), bf16)

    def synth(q, split_up):
        return pl.pallas_call(
            functools.partial(synth_kernel, slots=slots, split_up=split_up),
            name="synth",
            grid_spec=pltpu.PrefetchScalarGridSpec(
                num_scalar_prefetch=2,
                grid=(slots // GROUP,),
                in_specs=[chunk_spec(q), whole(root.shape), table_spec],
                out_specs=[piece_spec] * groups if split_up else payload_spec,
                scratch_shapes=[
                    degree_tiles,
                    wide,
                    pltpu.VMEM((GROUP, 2 * rows, half_cycles), f32),
                    cycle_tiles,
                    cycle_tiles,
                ]
                + ([stack] if split_up else []),
            ),
            out_shape=[piece] * groups if split_up else payload,
            compiler_params=params(),
            cost_estimate=legendre_cost,
        )(order_slots, me, probes_in, root, table)

    def analyse(q, returned, held, split_up, begin, size):
        first = held is None
        skipped = begin // GROUP
        some_table = pl.BlockSpec(
            table_spec.block_shape, lambda g, *_: (0, 0, g + skipped, 0)
        )
        some_out = pl.BlockSpec(
            (CHUNK, 2, GROUP, degrees), lambda g, *_: (q, 0, g + skipped, 0)
        )
        arrays = list(returned) if split_up else [returned]
        return pl.pallas_call(
            functools.partial(
                analysis_kernel, slots=slots, begin=begin, sources=groups, split_up=split_up
            ),
            name="analyse",
            grid_spec=pltpu.PrefetchScalarGridSpec(
                num_scalar_prefetch=2,
                grid=(size // GROUP,),
                in_specs=[whole(root.shape), some_table]
                + [piece_spec if split_up else payload_spec] * len(arrays)
                + ([] if first else [pl.BlockSpec(memory_space=pl.ANY)]),
                out_specs=some_out,
                scratch_shapes=[
                    cycle_tiles,
                    cycle_tiles,
                    wide,
                    pltpu.VMEM((GROUP, 4 * rows, half_cycles), bf16),
                    degree_tiles,
                ]
                + ([stack] if split_up else []),
            ),
            out_shape=jax.ShapeDtypeStruct((probes, 2, slots, degrees), f32),
            input_output_aliases={} if first else {4 + len(arrays): 0},
            compiler_params=params(),
            cost_estimate=legendre_cost,
        )(order_slots, me, root, table, *arrays, *([] if first else [held]))

    ahead_spec = pl.BlockSpec((1, 2 * TILE, orders_count), lambda i, h, o: (i, 0, 0))
    back_spec = pl.BlockSpec((2 * orders_count, TILE), lambda i, h, o: (0, i))
    grid_spec = pl.BlockSpec((TILE, part_lanes), lambda i, h, o: (i, 0))

    def fourier(received, tables, w_low, w_high, turn, chunk_beta, old, split_up):
        first = old is None
        ahead, back = tables
        square = jax.ShapeDtypeStruct((half_lon, part_lanes), f32)
        arrays = list(received) if split_up else [received]
        shapes = [piece] * groups if split_up else [payload]
        specs = [whole(shape.shape) for shape in shapes]
        sent = [payload]
        if split_up:
            sent = [
                jax.ShapeDtypeStruct((2, size, lanes), bf16) for _, size in cuts for _ in shapes
            ]
        return pl.pallas_call(
            functools.partial(
                fourier_kernel, first=first, sources=groups, split_up=split_up, cuts=cuts
            ),
            name="fourier",
            grid_spec=pltpu.PrefetchScalarGridSpec(
                num_scalar_prefetch=1,
                grid=(half_lon // TILE, parts),
                in_specs=[ahead_spec] * 2
                + [back_spec] * 2
                + [grid_spec] * 2
                + [whole((orders_count, 1)), whole((1, lanes))]
                + ([] if first else [grid_spec] * 2)
                + specs,
                out_specs=[whole(shape.shape) for shape in sent] + [grid_spec, grid_spec],
                scratch_shapes=[pltpu.VMEM((parts, orders_count, part_lanes), bf16)] * 2
                + [pltpu.VMEM((parts, orders_count, part_lanes), f32)] * 2
                + [pltpu.VMEM((parts, 1, part_lanes), f32)]
                + ([pltpu.VMEM(payload.shape, bf16)] if split_up else []),
            ),
            out_shape=sent + [square, square],
            input_output_aliases={} if first else {9: len(sent), 10: len(sent) + 1},
            compiler_params=params(),
            cost_estimate=pl.CostEstimate(
                flops=40 * half_lon * lanes * orders_count,
                bytes_accessed=16 * half_lon * orders_count + 16 * half_lon * part_lanes,
                transcendentals=0,
            ),
        )(
            me,
            *ahead,
            *back,
            w_low,
            w_high,
            turn,
            chunk_beta,
            *([] if first else old),
            *arrays,
        )

    def exchange(x, split_up):
        if split_up:
            middle_bit = lax.axis_size("blk") // 2
            pieces = list(x)
            for r in sorted(range(1, groups), key=lambda r: (not r & middle_bit, r)):
                pairs = [(i, i ^ r) for i in range(groups)]
                pieces[r] = lax.ppermute(x[r], axes, pairs)
            return pieces
        return lax.all_to_all(x, axes, split_axis=0, concat_axis=0, tiled=True)

    local = jnp.arange(cycles, dtype=jnp.int32)
    flipped = jnp.where(south, cycles - 1 - local, local)
    cycle_index = (my_index * cycles + flipped).astype(f32)
    area = 2.0 * math.pi / lon_count * (math.pi / all_cycles) * jnp.sin(
        math.pi * (cycle_index + 0.5) / all_cycles
    )
    turned = jnp.where(south, jnp.flip(weight, 0), weight)
    turned = (area[:, None] * turned).T
    w_low = jnp.tile(turned[:half_lon], (1, PART))
    w_high = jnp.concatenate(
        [turned[half_lon : half_lon + 1], jnp.flip(turned[half_lon + 1 :], 0)], axis=0
    )
    w_high = jnp.tile(w_high, (1, PART))
    turn = (1 - 2 * (order_slots % 2)).astype(f32)[:, None]
    tables = half_tables(order_slots, lon_count)

    split_up = [q % 2 == 1 for q in range(chunks)]
    kept = max(GROUP, slots * 3 // 5 // GROUP * GROUP)
    cuts = [(0, kept), (kept, slots - kept)] if kept < slots else [(0, slots)]
    received = []
    for q in range(chunks):
        spectra = synth(q, split_up[q])
        if split_up[q]:
            spectra, tables, w_low, w_high = lax.optimization_barrier(
                (spectra, tables, w_low, w_high)
            )
        received.append(exchange(spectra, split_up[q]))
    old, held = None, None
    returned = []
    for q in range(chunks):
        chunk_beta = jnp.repeat(beta[q * CHUNK : (q + 1) * CHUNK], cycles)[None, :]
        *analysed, low, high = fourier(
            received[q], tables, w_low, w_high, turn, chunk_beta, old, split_up[q]
        )
        old = (low, high)
        if split_up[q]:
            for k, (begin, size) in enumerate(cuts):
                ready = exchange(analysed[k * groups : (k + 1) * groups], True)
                returned.append((q, ready, begin, size))
        else:
            returned.append((q, exchange(analysed[0], False), 0, slots))
    for q, ready, begin, size in returned:
        held = analyse(q, ready, held, split_up[q], begin, size)

    lane_cycle = jnp.arange(part_lanes, dtype=jnp.int32) % cycles
    pick = (lane_cycle[None, :] == flipped[:, None]).astype(f32)
    sums = [
        lax.dot_general(
            pick, s, (((1,), (1,)), ((), ())), precision=lax.Precision.HIGHEST,
            preferred_element_type=f32,
        )
        for s in old
    ]
    natural = 2.0 * math.pi / lon_count * (math.pi / all_cycles) * jnp.sin(
        math.pi * ((my_index * cycles + local).astype(f32) + 0.5) / all_cycles
    )
    if lax.axis_size("probe") == 2:
        ahead_half = lax.axis_index("probe") == 0
        keep = jnp.where(ahead_half, sums[0], sums[1])
        give = jnp.where(ahead_half, sums[1], sums[0])
        taken = lax.ppermute(give, "probe", [(0, 1), (1, 0)])
        half = (keep + taken) * natural[:, None]
        mirrored = jnp.concatenate([half[:, :1], jnp.flip(half[:, 1:], 1)], axis=1)
        gradient = jnp.where(ahead_half, half, mirrored)
    else:
        terms = jnp.concatenate([sums[0], sums[1][:, :1], jnp.flip(sums[1][:, 1:], 1)], axis=1)
        gradient = lax.psum_scatter(
            terms * natural[:, None], "probe", scatter_dimension=1, tiled=True
        )
    return (held, gradient)


def body(probes_in, root_spectrum, order_slots, legendre, weight, beta):
    degrees, slots, all_cycles = legendre.shape
    fits = (
        slots % GROUP == 0
        and degrees % DEPTH == 0
        and degrees == order_slots.shape[0]
        and all_cycles % (2 * LANES) == 0
        and (PART * weight.shape[0]) % LANES == 0
        and probes_in.shape[0] % CHUNK == 0
        and weight.shape[1] % (2 * TILE) == 0
        and lax.axis_size(("lat", "blk")) in (2, 4, 8, 16, 32)
    )
    chosen = fast_body if fits else plain_body
    return chosen(probes_in, root_spectrum, order_slots, legendre, weight, beta)


def solution(mesh):
    return jax.shard_map(
        body,
        mesh=mesh,
        in_specs=(
            P("probe", None, ("lat", "blk"), None),
            P(),
            P(),
            P(None, ("lat", "blk"), None),
            P(("lat", "blk"), None),
            P("probe"),
        ),
        out_specs=(P("probe", None, ("lat", "blk"), None), P(("lat", "blk"), "probe")),
        check_vma=False,
    )
```
